128 devices in a mesh: energy: 32 (over z, y, core), space: 4 (over x).
Axes of the slice: x: 4, y: 4, z: 4, core: 2. Of those that a mesh axis runs over, the one named last changes fastest.
Arguments:
- ham_diag: float32 [4, 256, 256], P('space')
- ham_coup: float32 [4, 256, 256], P('space'), may hold values from -0.1875 to 0.1875
- energies: float32 [32], P('energy'), may hold values from 1 to 2
- pattern: int32 [4, 43264], P('space'), may hold values from 0 to 65535, as said below
- coulomb: float32 [4, 43264], P('space', 'energy'), may hold values from 0.5 to 2
Outputs:
- green: float32 [32, 4, 256, 256], P('energy', 'space')
- screened: float32 [32, 4, 43264], P(None, 'space', 'energy')
The draws below stay inside these ranges and needn't reach their ends.
Inputs may be any that keep to these rules, and one draw needn't show every extreme that they name: `pattern`: each row holds 43264 distinct flat positions of one block, among them all 256 diagonal positions.
All inputs are finite; a program needn't handle non-finite values.
Results may differ from the reference program's by a relative error of at most 0.0001.
Values sent between devices are 32-bit elements; how exact they have to be, the bound alone decides.
A program may use at most 128 MiB of HBM per device.

```python
import math
import jax
import jax.numpy as jnp
from jax import lax

B = 256
NNZ = 43264
E = 32
NB = 4


def draw_ham_diag(key, part):
    key_noise, key_diag = jax.random.split(jax.random.fold_in(key, 11))
    noise = jax.random.normal(key_noise, (NB, B, B), jnp.float32) / jnp.sqrt(2.0 * B)
    symmetric = noise + jnp.swapaxes(noise, 1, 2)
    diagonal = jax.random.uniform(key_diag, (NB, B), jnp.float32, 2.0, 3.0)
    return symmetric + diagonal[:, :, None] * jnp.eye(B, dtype=jnp.float32)


def draw_pattern(key, part):
    keys = jax.random.split(jax.random.fold_in(key, 23), NB)
    flat_index = jnp.arange(B * B, dtype=jnp.int32)
    on_diagonal = flat_index // B == flat_index % B

    def one_block(block_key):
        scores = jax.random.permutation(block_key, B * B).astype(jnp.int32)
        scores = scores + jnp.where(on_diagonal, B * B, 0).astype(jnp.int32)
        unused_values, chosen = jax.lax.top_k(scores, NNZ)
        return chosen.astype(jnp.int32)
    return jax.vmap(one_block)(keys)


def level_of(own_key, dims, shards, low, largest):
    level, own = 1.0, jax.random.fold_in(own_key, 6)
    for dim, blocks in shards:
        heights = jnp.exp(jax.random.uniform(jax.random.fold_in(own, dim), (blocks,), jnp.float32, low / len(shards), largest / len(shards)))
        level = level * jnp.repeat(heights, dims[dim] // blocks).reshape([-1 if axis == dim else 1 for axis in range(len(dims))])
    return level


def bell_draw(own_key, extent, scale, bound, shards=(), held_as=jnp.bfloat16):
    entries = jax.random.normal(own_key, extent, jnp.float32) * scale
    if len(shards) > 0:
        entries = level_of(own_key, extent, shards, -0.22, 0.18) * entries
    return jnp.clip(entries, min=-bound, max=bound).astype(held_as)


def setup_inputs(seed: int = 0) -> dict:
    arg_keys = jax.random.split(jax.random.key(seed), 6)
    return {
        "ham_diag": draw_ham_diag(jax.random.fold_in(arg_keys[5], 71), 0),
        "ham_coup": bell_draw(arg_keys[1], (NB, B, B), (4 * B) ** -0.5, 0.1875, ((0, 4),), jnp.float32),
        "energies": jnp.clip(1.0 + 1.0 * jax.random.uniform(arg_keys[2], (E,), jnp.float32) ** level_of(arg_keys[2], (E,), ((0, 32),), -0.2, 0.2), 1.0, 2.0),
        "pattern": draw_pattern(jax.random.fold_in(arg_keys[5], 71), 0),
        "coulomb": jnp.clip(jnp.exp(math.log(2.0) - 1.3862944 * jax.random.uniform(arg_keys[4], (NB, NNZ), jnp.float32) ** level_of(arg_keys[4], (NB, NNZ), ((0, 4), (1, 32)), -0.2, 0.2)), 0.5, 2.0),
    }


polar_coef = 128.0
sigma_coef = 0.5

def tri_solve(factor, target, flipped):
    return lax.linalg.triangular_solve(factor, target, left_side=True, lower=True, transpose_a=flipped)

def invert_spd(matrix):
    ident = jnp.broadcast_to(jnp.eye(matrix.shape[-1], dtype=matrix.dtype), matrix.shape)
    factor = jnp.linalg.cholesky(matrix)
    return tri_solve(factor, tri_solve(factor, ident, False), True)

def left_segment(incoming, systems, couplings):

    def advance(incoming_term, block_pair):
        system, coupling = block_pair
        factor = jnp.linalg.cholesky(system - incoming_term)
        solved = tri_solve(factor, coupling, False)
        return (jnp.dot(solved.T, solved, precision=lax.Precision.HIGHEST), incoming_term)
    outgoing, left_terms = lax.scan(advance, incoming, (systems, couplings))
    return (left_terms, outgoing)

def right_segment(incoming_factor, systems, couplings):

    def retreat(factor, block_pair):
        system, coupling = block_pair
        solved = tri_solve(factor, coupling.T, False)
        rights = jnp.dot(solved.T, solved, precision=lax.Precision.HIGHEST)
        return (jnp.linalg.cholesky(system - rights), rights)
    outgoing, right_terms = lax.scan(retreat, incoming_factor, (systems, couplings), reverse=True)
    return (right_terms, outgoing)

def reference(ham_diag, ham_coup, energies, pattern, coulomb):
    width = ham_diag.shape[1]
    count = energies.shape[0]
    ident = jnp.eye(width, dtype=ham_diag.dtype)
    start_left = jnp.zeros((width, width), ham_diag.dtype)
    start_right = 2.0 * ident

    def one_energy(shift):
        systems = ham_diag + shift * ident
        left_terms, unused_left = left_segment(start_left, systems, ham_coup)
        right_terms, unused_right = right_segment(start_right, systems, ham_coup)
        reduced = systems - left_terms - right_terms
        base = invert_spd(reduced)
        flat = base.reshape(base.shape[0], width * width)
        sample = jnp.take_along_axis(flat, pattern, axis=1)
        return (sample, reduced)

    def sample_only(shift):
        return one_energy(shift)[0]
    samples = lax.map(sample_only, energies)
    length = 2 * count

    def screen_block(block_pair):
        series, bare = block_pair
        spectrum = jnp.fft.rfft(series, n=length, axis=0)
        power = spectrum.real * spectrum.real + spectrum.imag * spectrum.imag
        polar = jnp.fft.irfft(power, n=length, axis=0)[:count] * (polar_coef * width / count)
        scaled = bare[None, :] * polar
        screen_block_w = bare[None, :] / jnp.sqrt(1.0 + scaled * scaled)
        wspec = jnp.fft.rfft(screen_block_w, n=length, axis=0)
        selfen = jnp.fft.irfft(spectrum * wspec, n=length, axis=0)[:count] * (sigma_coef / count)
        return (screen_block_w, selfen)
    screened_t, selfen_t = lax.map(screen_block, (jnp.swapaxes(samples, 0, 1), coulomb))
    screened = jnp.swapaxes(screened_t, 0, 1)
    selfen = jnp.swapaxes(selfen_t, 0, 1)

    def update(block_pair):
        shift, values = block_pair
        reduced = one_energy(shift)[1]

        def place_row(row_values, positions):
            return jnp.zeros((width * width,), row_values.dtype).at[positions].set(row_values)
        spread = jax.vmap(place_row)(values, pattern).reshape(-1, width, width)
        sym = 0.5 * (spread + jnp.swapaxes(spread, 1, 2))
        return invert_spd(reduced - sym)
    green = lax.map(update, (energies, selfen))
    return (green, screened)
```

```python
import functools

import jax
import jax.numpy as jnp
from jax import lax
from jax.experimental import pallas as pl
from jax.experimental.pallas import tpu as pltpu
from jax.sharding import PartitionSpec as P

F32, BF16 = jnp.float32, jnp.bfloat16
MESH = pl.DeviceIdType.MESH
VMEM = pltpu.VMEM
DMA = pltpu.SemaphoreType.DMA

polar_coef = 128.0
sigma_coef = 0.5

START_DOUBLINGS = 5
MAX_STEPS = 48
TOLERANCE = 1e-6


def split(value):
    high = value.astype(BF16)
    return high, (value - high.astype(F32)).astype(BF16)


def dot(a, b):
    return jnp.dot(a, b, preferred_element_type=F32)


def dot_nt(a, b):
    return lax.dot_general(a, b, (((1,), (1,)), ((), ())), preferred_element_type=F32)


def mul(a, b):
    return dot(a[0], b[0]) + (dot(a[0], b[1]) + dot(a[1], b[0]))


def product(a, b):
    return mul(split(a), split(b))


def identity(width):
    rows = lax.broadcasted_iota(jnp.int32, (width, width), 0)
    cols = lax.broadcasted_iota(jnp.int32, (width, width), 1)
    return jnp.where(rows == cols, 1.0, 0.0).astype(F32)


def cold_start(matrix):
    ident = identity(matrix.shape[0])
    bound = jnp.max(jnp.sum(jnp.abs(matrix), axis=0, keepdims=True), axis=1, keepdims=True)
    alpha = 1.9 / bound
    power = ident - matrix * alpha
    guess = (ident + power) * alpha
    for _ in range(START_DOUBLINGS):
        high = power.astype(BF16)
        power = dot(high, high)
        guess = guess + dot(guess.astype(BF16), power.astype(BF16))
    return guess


def eliminate(matrix, out_ref):
    width = matrix.shape[0]
    out_ref[...] = matrix
    lanes = lax.broadcasted_iota(jnp.int32, (1, width), 1)

    def step(pivot, carry):
        whole = out_ref[...]
        row = out_ref[pl.ds(pivot, 1), :]
        here = lanes == pivot
        value = jnp.sum(jnp.where(here, row, 0.0), axis=1, keepdims=True)
        column = jnp.sum(jnp.where(here, whole, 0.0), axis=1, keepdims=True)
        scaled = jnp.where(here, 1.0, row) / value
        out_ref[...] = jnp.where(here, 0.0, whole) - column * scaled
        out_ref[pl.ds(pivot, 1), :] = scaled
        return carry

    lax.fori_loop(0, width, step, 0)


def settle(matrices, refs):
    ident = identity(matrices[0].shape[0])
    parts = [split(matrix) for matrix in matrices]

    def unsettled(carry):
        steps, worst = carry
        return jnp.logical_and(worst > TOLERANCE, steps < MAX_STEPS)

    def step(carry):
        worst = jnp.float32(0.0)
        for own, ref in zip(parts, refs):
            guess = ref[...]
            guess_parts = split(guess)
            residual = ident - mul(own, guess_parts)
            ref[...] = guess + dot(guess_parts[0], residual.astype(BF16))
            worst = jnp.maximum(worst, jnp.sum(residual * residual))
        return carry[0] + 1, worst

    steps, worst = lax.while_loop(unsettled, step, (jnp.int32(0), jnp.float32(1.0)))

    @pl.when(jnp.logical_not(worst <= TOLERANCE))
    def _():
        for matrix, ref in zip(matrices, refs):
            eliminate(matrix, ref)


def invert(matrices, refs):
    for matrix, ref in zip(matrices, refs):
        ref[...] = cold_start(matrix)
    settle(matrices, refs)


def send_blocks(count, me, source, target, send_sems, recv_sems):
    def one(step, carry):
        peer = lax.rem(me + step, count)
        pltpu.make_async_remote_copy(
            src_ref=source(peer), dst_ref=target(me),
            send_sem=send_sems.at[step], recv_sem=recv_sems.at[me],
            device_id={"energy": peer}, device_id_type=MESH,
        ).start()
        return carry

    lax.fori_loop(1, count, one, 0)


def await_blocks(count, me, source, target, send_sems, recv_sems):
    def one(step, carry):
        peer = lax.rem(me + step, count)
        copy = pltpu.make_async_remote_copy(
            src_ref=source(peer), dst_ref=target(peer),
            send_sem=send_sems.at[step], recv_sem=recv_sems.at[peer],
            device_id={"energy": peer}, device_id_type=MESH,
        )
        copy.wait_send()
        copy.wait_recv()
        return carry

    lax.fori_loop(1, count, one, 0)


def greet_energy(count, me, barrier):
    def one(step, carry):
        pl.semaphore_signal(barrier, inc=1, device_id={"energy": lax.rem(me + step, count)}, device_id_type=MESH)
        return carry

    lax.fori_loop(1, count, one, 0)


def collect_kernel(
    count, spaces, diag_ref, coup_ref, pattern_ref, bare_ref,
    diags_ref, coups_ref, rows_ref, slots_ref, bare_pos_ref, bare_own_ref,
    own_pattern, partial, arrived, own_sem, far_send, far_recv, near_send, near_recv, send_sems, recv_sems,
):
    me = lax.axis_index("energy")
    place = lax.axis_index("space")
    width = diag_ref.shape[1]
    half = width // 2
    core = lax.rem(me, 2)
    other = me + 1 - 2 * core
    chunk = bare_ref.shape[1]
    span = 1352

    barrier = pltpu.get_barrier_semaphore()
    greet_energy(count, me, barrier)
    for step in range(1, spaces):
        pl.semaphore_signal(
            barrier, inc=1, device_id={"space": lax.rem(place + step, spaces)}, device_id_type=MESH)
    pl.semaphore_wait(barrier, count + spaces - 2)

    own_half = pl.ds(pl.multiple_of(core * half, half), half)
    other_half = pl.ds(pl.multiple_of((1 - core) * half, half), half)

    def far_copy(step, kind):
        source, store = ((diag_ref, diags_ref), (coup_ref, coups_ref))[kind]
        return pltpu.make_async_remote_copy(
            src_ref=source.at[0, own_half], dst_ref=store.at[place, own_half],
            send_sem=far_send.at[step, kind], recv_sem=far_recv.at[step, kind],
            device_id={"space": lax.rem(place + step, spaces)}, device_id_type=MESH)

    def near_copy(step, kind):
        store = (diags_ref, coups_ref)[kind]
        source = lax.rem(place + spaces - step, spaces)
        return pltpu.make_async_remote_copy(
            src_ref=store.at[source, own_half], dst_ref=store.at[source, own_half],
            send_sem=near_send.at[step, kind], recv_sem=near_recv.at[step, kind],
            device_id={"energy": other}, device_id_type=MESH)

    order = (1, 3, 2)
    for step in order:
        for kind in range(2):
            far_copy(step, kind).start()
    own_copies = [
        pltpu.make_async_copy(diag_ref.at[0], diags_ref.at[place], own_sem.at[0]),
        pltpu.make_async_copy(coup_ref.at[0], coups_ref.at[place], own_sem.at[1]),
    ]
    for copy in own_copies:
        copy.start()

    for part in range(count):
        piece = pattern_ref[:, part * span:part * span + chunk]
        own_pattern[part] = piece
        row = lax.shift_right_logical(piece, 8)
        col = jnp.bitwise_and(piece, 255)
        high = jnp.maximum(row, col)
        low = jnp.minimum(row, col)
        lower = low >= 128
        pivot = high == low
        rows_ref[part] = jnp.where(jnp.logical_and(lower, jnp.logical_not(pivot)), low - 128, high)
        slots_ref[part] = jnp.where(lower, jnp.where(pivot, 128, high - 128), low)
    mine = own_pattern[me]
    bare = bare_ref[...]
    index = lax.broadcasted_iota(jnp.int32, (width, chunk), 0)
    on_row = index == lax.shift_right_logical(mine, 8)
    on_col = jnp.where(index == jnp.bitwise_and(mine, 255), 1.0, 0.0).astype(BF16)
    rest = bare
    total = None
    for _ in range(3):
        part = rest.astype(BF16).astype(F32)
        rest = rest - part
        term = dot_nt(jnp.where(on_row, part, 0.0).astype(BF16), on_col)
        total = term if total is None else total + term
    partial[...] = total
    for line in range(chunk // 128):
        bare_own_ref[line:line + 1, :] = bare[:, line * 128:(line + 1) * 128]
    for line in range(chunk // 128, bare_own_ref.shape[0]):
        bare_own_ref[line:line + 1, :] = jnp.zeros((1, 128), F32)

    source = lambda peer: partial.at[pl.ds(pl.multiple_of(peer * 8, 8), 8), :]
    target = lambda peer: arrived.at[peer]
    send_blocks(count, me, source, target, send_sems, recv_sems)
    arrived[me] = partial[pl.ds(pl.multiple_of(me * 8, 8), 8), :]

    for step in order:
        for kind in range(2):
            copy = far_copy(step, kind)
            copy.wait_recv()
            near_copy(step, kind).start()
    await_blocks(count, me, source, target, send_sems, recv_sems)
    pieces = [arrived[peer] for peer in range(count)]
    while len(pieces) > 1:
        pieces = [pieces[i] + pieces[i + 1] for i in range(0, len(pieces), 2)]
    bare_pos_ref[...] = pieces[0]
    for copy in own_copies:
        copy.wait()
    for step in order:
        for kind in range(2):
            far_copy(step, kind).wait_send()
            near_copy(step, kind).wait_send()
            store = (diags_ref, coups_ref)[kind]
            block = lax.rem(place + spaces - step, spaces)
            pltpu.make_async_remote_copy(
                src_ref=store.at[block, other_half], dst_ref=store.at[block, other_half],
                send_sem=near_send.at[step, kind], recv_sem=near_recv.at[step, kind],
                device_id={"energy": other}, device_id_type=MESH).wait_recv()


def chain_kernel(
    place_ref, shift_ref, diags_ref, coups_ref, reduced_ref, base_ref,
    u_ref, ut_ref, v_ref, vt_ref, w_ref, wt_ref, c_ref, ct_ref, last_ref, x_ref, y_ref,
):
    place = place_ref[0]
    width = base_ref.shape[0]
    shift = identity(width) * shift_ref[0]
    lead = coups_ref[3]
    lead_parts = split(lead)
    quarter = (
        dot_nt(lead_parts[0], lead_parts[0])
        + (dot_nt(lead_parts[0], lead_parts[1]) + dot_nt(lead_parts[1], lead_parts[0]))
    ) * 0.25
    last_ref[...] = diags_ref[3] - quarter

    def fill(pair, index, flipped):
        one, two = pair
        value = coups_ref[index]
        (two if flipped else one)[...] = value
        (one if flipped else two)[...] = value.T

    u, v, w, c = (u_ref, ut_ref), (v_ref, vt_ref), (w_ref, wt_ref), (c_ref, ct_ref)

    @pl.when(place == 0)
    def _():
        fill(u, 1, False)
        fill(v, 2, True)
        fill(w, 0, True)

    @pl.when(place == 1)
    def _():
        fill(c, 1, False)
        fill(v, 2, True)
        fill(w, 0, False)

    @pl.when(place == 2)
    def _():
        fill(c, 1, True)
        fill(v, 0, False)
        fill(w, 2, True)

    @pl.when(place == 3)
    def _():
        fill(u, 1, True)
        fill(v, 0, False)
        fill(w, 2, False)

    first = jnp.where(place == 0, 1, jnp.where(place == 1, 0, jnp.where(place == 2, 3, 2)))
    second = jnp.where(place <= 1, 3, 0)
    middle = jnp.where(place <= 1, 2, 1)

    def system(block):
        return jnp.where(block == 3, last_ref[...], diags_ref[block]) + shift

    inner = jnp.logical_or(place == 1, place == 2)
    invert([system(first), system(second)], [x_ref, y_ref])
    x = split(x_ref[...])
    y = split(y_ref[...])
    w_s, wt_s = split(w_ref[...]), split(wt_ref[...])
    xw = split(mul(x, w_s))
    yv = split(mul(y, split(v_ref[...])))
    rest = system(place) - mul(wt_s, xw)
    reduced_ref[...] = rest
    last_ref[...] = system(middle) - mul(split(vt_ref[...]), yv)

    @pl.when(jnp.logical_not(inner))
    def _():
        xu = split(mul(x, split(u_ref[...])))
        ut_s = split(ut_ref[...])
        last_ref[...] = last_ref[...] - mul(ut_s, xu)
        c_ref[...] = mul(wt_s, xu)
        ct_ref[...] = mul(ut_s, xw)

    invert([last_ref[...]], [x_ref])
    cz = split(product(c_ref[...], x_ref[...]))
    reduced = reduced_ref[...] - mul(cz, split(ct_ref[...]))
    reduced_ref[...] = reduced
    invert([reduced], [base_ref])


def screen(samples, bare, scale):
    count = len(samples)
    result = []
    for lag in range(count):
        total = samples[0] * samples[lag]
        for m in range(1, count - lag):
            total = total + samples[m] * samples[m + lag]
        scaled = bare * (total * scale)
        result.append(bare / jnp.sqrt(1.0 + scaled * scaled))
    return result


def regroup_kernel(
    count, base_ref, rows_ref, slots_ref, bare_pos_ref, spread_ref, taken_ref,
    lhs, arrived, selfen, taken, send_a, recv_a, send_b, recv_b, send_c, recv_c,
):
    me = lax.axis_index("energy")
    width = base_ref.shape[0]
    half = width // 2
    chunk = rows_ref.shape[2]
    lines = taken.shape[1]

    barrier = pltpu.get_barrier_semaphore()
    greet_energy(count, me, barrier)
    pl.semaphore_wait(barrier, count - 1)

    source_a = lambda peer: base_ref.at[pl.ds(pl.multiple_of(peer * 8, 8), 8), :]
    target_a = lambda peer: arrived.at[peer]
    send_blocks(count, me, source_a, target_a, send_a, recv_a)
    arrived[me] = base_ref[pl.ds(pl.multiple_of(me * 8, 8), 8), :]

    upper = base_ref[:half, :half]
    lower = base_ref[half:, half:]
    r = lax.broadcasted_iota(jnp.int32, (half, half), 0)
    c = lax.broadcasted_iota(jnp.int32, (half, half), 1)
    table = jnp.concatenate([jnp.where(r <= c, upper, lower), base_ref[:half, half:]], axis=1)
    diagonal = jnp.sum(jnp.where(r == c, lower, 0.0), axis=0, keepdims=True)
    extra = jnp.concatenate([jnp.zeros((1, half), F32), diagonal], axis=1)
    first = lax.broadcasted_iota(jnp.int32, (16, width), 0) == 0
    table = jnp.concatenate([table, jnp.where(first, extra, 0.0)], axis=0)
    high, low = split(table)
    tall = table.shape[0]
    lhs[:tall, :] = high
    lhs[tall:, :] = low
    row_index = lax.broadcasted_iota(jnp.int32, (width, chunk), 0)
    slot_index = lax.broadcasted_iota(jnp.int32, (tall, chunk), 0)

    def take(part, carry):
        hot = jnp.where(row_index == rows_ref[part], 1.0, 0.0).astype(BF16)
        both = dot(lhs[...], hot)
        found = jnp.where(slot_index == slots_ref[part], both[:tall] + both[tall:], 0.0)
        line = jnp.sum(found, axis=0, keepdims=True)
        for piece in range(chunk // 128):
            taken[part, piece:piece + 1, :] = line[:, piece * 128:(piece + 1) * 128]
        taken[part, chunk // 128:, :] = jnp.zeros((lines - chunk // 128, 128), F32)
        return carry

    lax.fori_loop(0, count, take, 0)
    source_c = lambda peer: taken.at[peer]
    target_c = lambda peer: taken_ref.at[peer]
    send_blocks(count, me, source_c, target_c, send_c, recv_c)
    taken_ref[me] = taken[me]
    await_blocks(count, me, source_a, target_a, send_a, recv_a)

    scale = polar_coef * width / count
    for side in range(width // 128):
        cols = slice(side * 128, (side + 1) * 128)
        samples = [arrived[e, :, cols] for e in range(count)]
        screened = screen(samples, bare_pos_ref[:, cols], scale)
        for e in range(count):
            total = samples[e] * screened[0]
            for n in range(1, e + 1):
                total = total + samples[e - n] * screened[n]
            selfen[e, :, cols] = total * (sigma_coef / count)
    source_b = lambda peer: selfen.at[peer]
    target_b = lambda peer: spread_ref.at[pl.ds(pl.multiple_of(peer * 8, 8), 8), :]
    send_blocks(count, me, source_b, target_b, send_b, recv_b)
    spread_ref[pl.ds(pl.multiple_of(me * 8, 8), 8), :] = selfen[me]
    await_blocks(count, me, source_b, target_b, send_b, recv_b)
    await_blocks(count, me, source_c, target_c, send_c, recv_c)


def finish_kernel(reduced_ref, base_ref, spread_ref, taken_ref, bare_ref, green_ref, screened_ref, x_ref):
    count = taken_ref.shape[0]
    width = base_ref.shape[0]
    chunk = screened_ref.shape[2]
    spread = spread_ref[...]
    matrix = reduced_ref[...] - 0.5 * (spread + spread.T)
    base = base_ref[...]
    residual = identity(width) - product(matrix, base)
    x_ref[...] = base

    @pl.when(jnp.logical_not(jnp.sum(residual * residual) < 0.5))
    def _():
        x_ref[...] = cold_start(matrix)

    settle([matrix], [x_ref])
    green_ref[0, 0] = x_ref[...]
    scale = polar_coef * width / count
    for group in range(taken_ref.shape[1] // 8):
        lines = slice(group * 8, group * 8 + 8)
        samples = [taken_ref[e, lines, :] for e in range(count)]
        screened = screen(samples, bare_ref[lines, :], scale)
        for line in range(group * 8, min(group * 8 + 8, pl.cdiv(chunk, 128))):
            start = line * 128
            stop = min(start + 128, chunk)
            for n in range(count):
                at = line - group * 8
                screened_ref[n, :, start:stop] = screened[n][at:at + 1, :stop - start]


def on_device(count, spaces, ham_diag, ham_coup, energies, pattern, coulomb):
    width = ham_diag.shape[1]
    span = coulomb.shape[1]
    chunk = pl.cdiv(span, 128) * 128
    lines = pl.cdiv(chunk // 128, 8) * 8
    vmem = pl.BlockSpec(memory_space=pltpu.VMEM)
    smem = pl.BlockSpec(memory_space=pltpu.SMEM)
    square = jax.ShapeDtypeStruct((width, width), F32)
    place = lax.axis_index("space").astype(jnp.int32).reshape(1)
    padded_pattern = jnp.pad(pattern, ((0, 0), (0, chunk - span)))
    padded_bare = jnp.pad(coulomb, ((0, 0), (0, chunk - span)))

    diags, coups, rows, slots, bare_pos, bare_own = pl.pallas_call(
        functools.partial(collect_kernel, count, spaces),
        out_shape=(
            jax.ShapeDtypeStruct((spaces, width, width), F32),
            jax.ShapeDtypeStruct((spaces, width, width), F32),
            jax.ShapeDtypeStruct((count, 1, chunk), jnp.int32),
            jax.ShapeDtypeStruct((count, 1, chunk), jnp.int32),
            jax.ShapeDtypeStruct((8, width), F32),
            jax.ShapeDtypeStruct((lines, 128), F32),
        ),
        in_specs=[vmem] * 4,
        out_specs=(vmem,) * 6,
        scratch_shapes=[
            VMEM((count, 1, chunk), jnp.int32), VMEM((width, width), F32), VMEM((count, 8, width), F32),
            DMA((2,)), DMA((spaces, 2)), DMA((spaces, 2)), DMA((spaces, 2)), DMA((spaces, 2)),
            DMA((count,)), DMA((count,)),
        ],
        compiler_params=pltpu.CompilerParams(collective_id=0, has_side_effects=True),
        name="collect",
    )(ham_diag, ham_coup, padded_pattern, padded_bare)

    reduced, base = pl.pallas_call(
        chain_kernel,
        out_shape=(square, square),
        in_specs=[smem, smem, vmem, vmem],
        out_specs=(vmem, vmem),
        scratch_shapes=[VMEM((width, width), F32)] * 11,
        name="chain",
    )(place, energies, diags, coups)

    spread, taken = pl.pallas_call(
        functools.partial(regroup_kernel, count),
        out_shape=(square, jax.ShapeDtypeStruct((count, lines, 128), F32)),
        in_specs=[vmem] * 4,
        out_specs=(vmem, vmem),
        scratch_shapes=[
            VMEM((2 * (width // 2 + 16), width), BF16), VMEM((count, 8, width), F32),
            VMEM((count, 8, width), F32), VMEM((count, lines, 128), F32),
            DMA((count,)), DMA((count,)), DMA((count,)), DMA((count,)), DMA((count,)), DMA((count,)),
        ],
        compiler_params=pltpu.CompilerParams(collective_id=1, has_side_effects=True),
        name="regroup",
    )(base, rows, slots, bare_pos)

    return pl.pallas_call(
        finish_kernel,
        out_shape=(
            jax.ShapeDtypeStruct((1, 1, width, width), F32),
            jax.ShapeDtypeStruct((count, 1, span), F32),
        ),
        in_specs=[vmem] * 5,
        out_specs=(vmem, vmem),
        scratch_shapes=[VMEM((width, width), F32)],
        name="finish",
    )(reduced, base, spread, taken, bare_own)


def solution(mesh):
    count, spaces = mesh.shape["energy"], mesh.shape["space"]
    return jax.shard_map(
        functools.partial(on_device, count, spaces),
        mesh=mesh,
        in_specs=(
            P("space", None, None),
            P("space", None, None),
            P("energy"),
            P("space", None),
            P("space", "energy"),
        ),
        out_specs=(P("energy", "space", None, None), P(None, "space", "energy")),
        check_vma=False,
    )
```

```python
import functools

import jax
import jax.numpy as jnp
from jax import lax
from jax.experimental import pallas as pl
from jax.experimental.pallas import tpu as pltpu
from jax.sharding import PartitionSpec as P

F32, BF16 = jnp.float32, jnp.bfloat16
MESH = pl.DeviceIdType.MESH
VMEM = pltpu.VMEM
DMA = pltpu.SemaphoreType.DMA

polar_coef = 128.0
sigma_coef = 0.5

START_DOUBLINGS = 5
MAX_STEPS = 48
TOLERANCE = 1e-6


def split(value):
    high = value.astype(BF16)
    return high, (value - high.astype(F32)).astype(BF16)


def dot(a, b):
    return jnp.dot(a, b, preferred_element_type=F32)


def dot_nt(a, b):
    return lax.dot_general(a, b, (((1,), (1,)), ((), ())), preferred_element_type=F32)


def mul(a, b):
    return dot(a[0], b[0]) + (dot(a[0], b[1]) + dot(a[1], b[0]))


def product(a, b):
    return mul(split(a), split(b))


def identity(width):
    rows = lax.broadcasted_iota(jnp.int32, (width, width), 0)
    cols = lax.broadcasted_iota(jnp.int32, (width, width), 1)
    return jnp.where(rows == cols, 1.0, 0.0).astype(F32)


def cold_start(matrix):
    ident = identity(matrix.shape[0])
    bound = jnp.max(jnp.sum(jnp.abs(matrix), axis=0, keepdims=True), axis=1, keepdims=True)
    alpha = 1.9 / bound
    power = ident - matrix * alpha
    guess = (ident + power) * alpha
    for _ in range(START_DOUBLINGS):
        high = power.astype(BF16)
        power = dot(high, high)
        guess = guess + dot(guess.astype(BF16), power.astype(BF16))
    return guess


def eliminate(matrix, out_ref):
    width = matrix.shape[0]
    out_ref[...] = matrix
    lanes = lax.broadcasted_iota(jnp.int32, (1, width), 1)

    def step(pivot, carry):
        whole = out_ref[...]
        row = out_ref[pl.ds(pivot, 1), :]
        here = lanes == pivot
        value = jnp.sum(jnp.where(here, row, 0.0), axis=1, keepdims=True)
        column = jnp.sum(jnp.where(here, whole, 0.0), axis=1, keepdims=True)
        scaled = jnp.where(here, 1.0, row) / value
        out_ref[...] = jnp.where(here, 0.0, whole) - column * scaled
        out_ref[pl.ds(pivot, 1), :] = scaled
        return carry

    lax.fori_loop(0, width, step, 0)


def settle(matrices, refs):
    ident = identity(matrices[0].shape[0])
    parts = [split(matrix) for matrix in matrices]

    def unsettled(carry):
        steps, worst = carry
        return jnp.logical_and(worst > TOLERANCE, steps < MAX_STEPS)

    def step(carry):
        worst = jnp.float32(0.0)
        for own, ref in zip(parts, refs):
            guess = ref[...]
            guess_parts = split(guess)
            residual = ident - mul(own, guess_parts)
            ref[...] = guess + dot(guess_parts[0], residual.astype(BF16))
            worst = jnp.maximum(worst, jnp.sum(residual * residual))
        return carry[0] + 1, worst

    steps, worst = lax.while_loop(unsettled, step, (jnp.int32(0), jnp.float32(1.0)))

    @pl.when(jnp.logical_not(worst <= TOLERANCE))
    def _():
        for matrix, ref in zip(matrices, refs):
            eliminate(matrix, ref)


def invert(matrices, refs):
    for matrix, ref in zip(matrices, refs):
        ref[...] = cold_start(matrix)
    settle(matrices, refs)


def peer_of(me, offset):
    core = lax.rem(me + offset, 2)
    y = lax.rem(me // 2 + offset // 2, 4)
    z = lax.rem(me // 8 + offset // 8, 4)
    return z * 8 + y * 2 + core


def block_copy(me, offset, source, target, slot, send_sems, recv_sems):
    peer = peer_of(me, offset)
    return pltpu.make_async_remote_copy(
        src_ref=source(peer), dst_ref=target(slot),
        send_sem=send_sems.at[offset], recv_sem=recv_sems.at[slot],
        device_id={"energy": peer}, device_id_type=MESH,
    )


def send_blocks(count, me, source, target, send_sems, recv_sems):
    def one(step, carry):
        block_copy(me, count - step, source, target, me, send_sems, recv_sems).start()
        return carry

    lax.fori_loop(1, count, one, 0)


def await_blocks(count, me, source, target, send_sems, recv_sems):
    def one(step, carry):
        offset = count - step
        copy = block_copy(me, offset, source, target, peer_of(me, offset), send_sems, recv_sems)
        copy.wait_send()
        copy.wait_recv()
        return carry

    lax.fori_loop(1, count, one, 0)


def rows_of(ref, peer):
    return ref.at[pl.ds(pl.multiple_of(peer * 8, 8), 8), :]


def collect_kernel(
    count, spaces, diag_ref, coup_ref, pattern_ref, bare_ref,
    diags_ref, coups_ref, rows_ref, slots_ref, partial_ref, bare_own_ref,
    own_pattern, own_bare, own_sem, far_send, far_recv, near_send, near_recv,
):
    me = lax.axis_index("energy")
    place = lax.axis_index("space")
    width = diag_ref.shape[1]
    half = width // 2
    core = lax.rem(me, 2)
    other = me + 1 - 2 * core
    span = bare_ref.shape[1]
    chunk = own_bare.shape[1]
    sides = (lax.rem(place + 1, spaces), lax.rem(place + spaces - 1, spaces))
    across = lax.rem(place + 2, spaces)

    barrier = pltpu.get_barrier_semaphore()
    for side in sides:
        pl.semaphore_signal(barrier, inc=1, device_id={"space": side}, device_id_type=MESH)
    pl.semaphore_signal(barrier, inc=1, device_id={"energy": other}, device_id_type=MESH)
    pl.semaphore_wait(barrier, 3)

    own_half = pl.ds(pl.multiple_of(core * half, half), half)
    other_half = pl.ds(pl.multiple_of((1 - core) * half, half), half)
    given = (diag_ref, coup_ref)
    stores = (diags_ref, coups_ref)

    def far(way, stage):
        kind = (way, 1 - way, way)[stage]
        block = place if stage < 2 else sides[1 - way]
        source = given[kind].at[0, own_half] if stage < 2 else stores[kind].at[block, own_half]
        return pltpu.make_async_remote_copy(
            src_ref=source, dst_ref=stores[kind].at[block, own_half],
            send_sem=far_send.at[way, stage], recv_sem=far_recv.at[way, stage],
            device_id={"space": sides[way]}, device_id_type=MESH)

    def near(way, stage, part):
        kind = (way, 1 - way, way)[stage]
        block = sides[1 - way] if stage < 2 else across
        piece = stores[kind].at[block, part]
        return pltpu.make_async_remote_copy(
            src_ref=piece, dst_ref=piece,
            send_sem=near_send.at[way, stage], recv_sem=near_recv.at[way, stage],
            device_id={"energy": other}, device_id_type=MESH)

    for stage in range(2):
        for way in range(2):
            far(way, stage).start()
    own_copies = [
        pltpu.make_async_copy(diag_ref.at[0], diags_ref.at[place], own_sem.at[0]),
        pltpu.make_async_copy(coup_ref.at[0], coups_ref.at[place], own_sem.at[1]),
    ]
    for copy in own_copies:
        copy.start()

    tail = chunk - 128
    for part in range(count):
        size = chunk if part < count - 1 else span
        if size < chunk:
            own_pattern[part, :, tail:] = jnp.zeros((1, 128), jnp.int32)
            rows_ref[part, :, tail:] = jnp.zeros((1, 128), jnp.int32)
            slots_ref[part, :, tail:] = jnp.zeros((1, 128), jnp.int32)
        piece = pattern_ref[:, part * span:part * span + size]
        own_pattern[part, :, :size] = piece
        row = lax.shift_right_logical(piece, 8)
        col = jnp.bitwise_and(piece, 255)
        high = jnp.maximum(row, col)
        low = jnp.minimum(row, col)
        lower = low >= 128
        pivot = high == low
        rows_ref[part, :, :size] = jnp.where(jnp.logical_and(lower, jnp.logical_not(pivot)), low - 128, high)
        slots_ref[part, :, :size] = jnp.where(lower, jnp.where(pivot, 128, high - 128), low)
    own_bare[:, tail:] = jnp.zeros((1, 128), F32)
    own_bare[:, :span] = bare_ref[...]

    for way in range(2):
        far(way, 0).wait_recv()
        far(way, 2).start()
        near(way, 0, own_half).start()

    mine = own_pattern[me]
    bare = own_bare[...]
    index = lax.broadcasted_iota(jnp.int32, (width, chunk), 0)
    on_row = index == lax.shift_right_logical(mine, 8)
    on_col = jnp.where(index == jnp.bitwise_and(mine, 255), 1.0, 0.0).astype(BF16)
    rest = bare
    total = None
    for _ in range(3):
        part = rest.astype(BF16).astype(F32)
        rest = rest - part
        term = dot_nt(jnp.where(on_row, part, 0.0).astype(BF16), on_col)
        total = term if total is None else total + term
    partial_ref[...] = total
    for line in range(chunk // 128):
        bare_own_ref[line:line + 1, :] = bare[:, line * 128:(line + 1) * 128]
    for line in range(chunk // 128, bare_own_ref.shape[0]):
        bare_own_ref[line:line + 1, :] = jnp.zeros((1, 128), F32)

    for stage in (1, 2):
        for way in range(2):
            far(way, stage).wait_recv()
            near(way, stage, own_half).start()
    for copy in own_copies:
        copy.wait()
    for stage in range(3):
        for way in range(2):
            far(way, stage).wait_send()
            near(way, stage, own_half).wait_send()
            near(way, stage, other_half).wait_recv()


def chain_kernel(
    shift_ref, diags_ref, coups_ref, reduced_ref, base_ref,
    u_ref, ut_ref, v_ref, vt_ref, w_ref, wt_ref, c_ref, ct_ref, last_ref, x_ref, y_ref,
):
    place = lax.axis_index("space")
    width = base_ref.shape[0]
    shift = identity(width) * shift_ref[0]
    lead = coups_ref[3]
    lead_parts = split(lead)
    quarter = (
        dot_nt(lead_parts[0], lead_parts[0])
        + (dot_nt(lead_parts[0], lead_parts[1]) + dot_nt(lead_parts[1], lead_parts[0]))
    ) * 0.25
    last_ref[...] = diags_ref[3] - quarter

    def fill(pair, index, flipped):
        one, two = pair
        value = coups_ref[index]
        (two if flipped else one)[...] = value
        (one if flipped else two)[...] = value.T

    u, v, w, c = (u_ref, ut_ref), (v_ref, vt_ref), (w_ref, wt_ref), (c_ref, ct_ref)

    @pl.when(place == 0)
    def _():
        fill(u, 1, False)
        fill(v, 2, True)
        fill(w, 0, True)

    @pl.when(place == 1)
    def _():
        fill(c, 1, False)
        fill(v, 2, True)
        fill(w, 0, False)

    @pl.when(place == 2)
    def _():
        fill(c, 1, True)
        fill(v, 0, False)
        fill(w, 2, True)

    @pl.when(place == 3)
    def _():
        fill(u, 1, True)
        fill(v, 0, False)
        fill(w, 2, False)

    first = jnp.where(place == 0, 1, jnp.where(place == 1, 0, jnp.where(place == 2, 3, 2)))
    second = jnp.where(place <= 1, 3, 0)
    middle = jnp.where(place <= 1, 2, 1)

    def system(block):
        return jnp.where(block == 3, last_ref[...], diags_ref[block]) + shift

    inner = jnp.logical_or(place == 1, place == 2)
    invert([system(first), system(second)], [x_ref, y_ref])
    x = split(x_ref[...])
    y = split(y_ref[...])
    w_s, wt_s = split(w_ref[...]), split(wt_ref[...])
    xw = split(mul(x, w_s))
    yv = split(mul(y, split(v_ref[...])))
    rest = system(place) - mul(wt_s, xw)
    reduced_ref[...] = rest
    last_ref[...] = system(middle) - mul(split(vt_ref[...]), yv)

    @pl.when(jnp.logical_not(inner))
    def _():
        xu = split(mul(x, split(u_ref[...])))
        ut_s = split(ut_ref[...])
        last_ref[...] = last_ref[...] - mul(ut_s, xu)
        c_ref[...] = mul(wt_s, xu)
        ct_ref[...] = mul(ut_s, xw)

    invert([last_ref[...]], [x_ref])
    cz = split(product(c_ref[...], x_ref[...]))
    reduced = reduced_ref[...] - mul(cz, split(ct_ref[...]))
    reduced_ref[...] = reduced
    invert([reduced], [base_ref])


def screen(samples, bare, scale):
    count = len(samples)
    result = []
    for lag in range(count):
        total = samples[0] * samples[lag]
        for m in range(1, count - lag):
            total = total + samples[m] * samples[m + lag]
        scaled = bare * (total * scale)
        result.append(bare / jnp.sqrt(1.0 + scaled * scaled))
    return result


TAKEN_FIRST = 4
TAKEN_SECOND = 13


def regroup_kernel(
    count, base_ref, partial_ref, rows_ref, slots_ref, spread_ref, taken_ref,
    lhs, arrived, bares, selfen, taken,
    send_a, recv_a, send_b, recv_b, send_c, recv_c, send_d, recv_d,
):
    me = lax.axis_index("energy")
    width = base_ref.shape[0]
    half = width // 2
    chunk = rows_ref.shape[2]
    lines = taken.shape[1]

    barrier = pltpu.get_barrier_semaphore()

    def greet(step, carry):
        pl.semaphore_signal(
            barrier, inc=1, device_id={"energy": peer_of(me, count - step)}, device_id_type=MESH)
        return carry

    lax.fori_loop(1, count, greet, 0)

    upper = base_ref[:half, :half]
    lower = base_ref[half:, half:]
    r = lax.broadcasted_iota(jnp.int32, (half, half), 0)
    c = lax.broadcasted_iota(jnp.int32, (half, half), 1)
    table = jnp.concatenate([jnp.where(r <= c, upper, lower), base_ref[:half, half:]], axis=1)
    diagonal = jnp.sum(jnp.where(r == c, lower, 0.0), axis=0, keepdims=True)
    extra = jnp.concatenate([jnp.zeros((1, half), F32), diagonal], axis=1)
    first = lax.broadcasted_iota(jnp.int32, (16, width), 0) == 0
    table = jnp.concatenate([table, jnp.where(first, extra, 0.0)], axis=0)
    high, low = split(table)
    tall = table.shape[0]
    used = half + 8
    lhs[:tall, :] = high
    lhs[tall:, :] = low
    row_index = lax.broadcasted_iota(jnp.int32, (width, chunk), 0)
    slot_index = lax.broadcasted_iota(jnp.int32, (used, chunk), 0)

    def take(part):
        hot = jnp.where(row_index == rows_ref[part], 1.0, 0.0).astype(BF16)
        both = dot(lhs[...], hot)
        found = jnp.where(slot_index == slots_ref[part], both[:used] + both[tall:tall + used], 0.0)
        line = jnp.sum(found, axis=0, keepdims=True)
        for piece in range(chunk // 128):
            taken[part, piece:piece + 1, :] = line[:, piece * 128:(piece + 1) * 128]
        taken[part, chunk // 128:, :] = jnp.zeros((lines - chunk // 128, 128), F32)

    source_a, target_a = lambda peer: rows_of(base_ref, peer), lambda slot: arrived.at[slot]
    source_d, target_d = lambda peer: rows_of(partial_ref, peer), lambda slot: bares.at[slot]
    source_b, target_b = lambda peer: selfen.at[peer], lambda slot: rows_of(spread_ref, slot)
    source_c, target_c = lambda peer: taken.at[peer], lambda slot: taken_ref.at[slot]

    def take_only(step, carry):
        take(peer_of(me, count - step))
        return carry

    def send_only(step, carry):
        block_copy(me, count - step, source_c, target_c, me, send_c, recv_c).start()
        return carry

    def take_and_send(step, carry):
        take_only(step, carry)
        return send_only(step, carry)

    lax.fori_loop(1, 1 + TAKEN_FIRST, take_only, 0)
    pl.semaphore_wait(barrier, count - 1)
    send_blocks(count, me, source_a, target_a, send_a, recv_a)
    send_blocks(count, me, source_d, target_d, send_d, recv_d)
    lax.fori_loop(1, 1 + TAKEN_FIRST, send_only, 0)
    arrived[me] = rows_of(base_ref, me)[...]
    bares[me] = rows_of(partial_ref, me)[...]
    lax.fori_loop(1 + TAKEN_FIRST, 1 + TAKEN_FIRST + TAKEN_SECOND, take_and_send, 0)
    await_blocks(count, me, source_a, target_a, send_a, recv_a)
    await_blocks(count, me, source_d, target_d, send_d, recv_d)

    scale = polar_coef * width / count
    for side in range(width // 128):
        cols = slice(side * 128, (side + 1) * 128)
        bare = bares[0, :, cols]
        for e in range(1, count):
            bare = bare + bares[e, :, cols]
        samples = [arrived[e, :, cols] for e in range(count)]
        screened = screen(samples, bare, scale)
        for e in range(count):
            total = samples[e] * screened[0]
            for n in range(1, e + 1):
                total = total + samples[e - n] * screened[n]
            selfen[e, :, cols] = total * (sigma_coef / count)
    send_blocks(count, me, source_b, target_b, send_b, recv_b)
    lax.fori_loop(1 + TAKEN_FIRST + TAKEN_SECOND, count, take_and_send, 0)
    take(me)
    taken_ref[me] = taken[me]
    spread_ref[pl.ds(pl.multiple_of(me * 8, 8), 8), :] = selfen[me]
    await_blocks(count, me, source_b, target_b, send_b, recv_b)
    await_blocks(count, me, source_c, target_c, send_c, recv_c)


def finish_kernel(reduced_ref, base_ref, spread_ref, taken_ref, bare_ref, green_ref, screened_ref, x_ref):
    count = taken_ref.shape[0]
    width = base_ref.shape[0]
    chunk = screened_ref.shape[2]
    spread = spread_ref[...]
    matrix = reduced_ref[...] - 0.5 * (spread + spread.T)
    base = base_ref[...]
    residual = identity(width) - product(matrix, base)
    x_ref[...] = base

    @pl.when(jnp.logical_not(jnp.sum(residual * residual) < 0.5))
    def _():
        x_ref[...] = cold_start(matrix)

    settle([matrix], [x_ref])
    green_ref[0, 0] = x_ref[...]
    scale = polar_coef * width / count
    for group in range(taken_ref.shape[1] // 8):
        lines = slice(group * 8, group * 8 + 8)
        samples = [taken_ref[e, lines, :] for e in range(count)]
        screened = screen(samples, bare_ref[lines, :], scale)
        for line in range(group * 8, min(group * 8 + 8, pl.cdiv(chunk, 128))):
            start = line * 128
            stop = min(start + 128, chunk)
            for n in range(count):
                at = line - group * 8
                screened_ref[n, :, start:stop] = screened[n][at:at + 1, :stop - start]


def on_device(count, spaces, ham_diag, ham_coup, energies, pattern, coulomb):
    width = ham_diag.shape[1]
    span = coulomb.shape[1]
    chunk = pl.cdiv(span, 128) * 128
    lines = pl.cdiv(chunk // 128, 8) * 8
    vmem = pl.BlockSpec(memory_space=pltpu.VMEM)
    smem = pl.BlockSpec(memory_space=pltpu.SMEM)
    square = jax.ShapeDtypeStruct((width, width), F32)
    diags, coups, rows, slots, partial, bare_own = pl.pallas_call(
        functools.partial(collect_kernel, count, spaces),
        out_shape=(
            jax.ShapeDtypeStruct((spaces, width, width), F32),
            jax.ShapeDtypeStruct((spaces, width, width), F32),
            jax.ShapeDtypeStruct((count, 1, chunk), jnp.int32),
            jax.ShapeDtypeStruct((count, 1, chunk), jnp.int32),
            square,
            jax.ShapeDtypeStruct((lines, 128), F32),
        ),
        in_specs=[vmem] * 4,
        out_specs=(vmem,) * 6,
        scratch_shapes=[
            VMEM((count, 1, chunk), jnp.int32), VMEM((1, chunk), F32),
            DMA((2,)), DMA((2, 3)), DMA((2, 3)), DMA((2, 3)), DMA((2, 3)),
        ],
        compiler_params=pltpu.CompilerParams(collective_id=0, has_side_effects=True),
        name="collect",
    )(ham_diag, ham_coup, pattern, coulomb)

    reduced, base = pl.pallas_call(
        chain_kernel,
        out_shape=(square, square),
        in_specs=[smem, vmem, vmem],
        out_specs=(vmem, vmem),
        scratch_shapes=[VMEM((width, width), F32)] * 11,
        name="chain",
    )(energies, diags, coups)

    spread, taken = pl.pallas_call(
        functools.partial(regroup_kernel, count),
        out_shape=(square, jax.ShapeDtypeStruct((count, lines, 128), F32)),
        in_specs=[vmem] * 4,
        out_specs=(vmem, vmem),
        scratch_shapes=[
            VMEM((2 * (width // 2 + 16), width), BF16), VMEM((count, 8, width), F32),
            VMEM((count, 8, width), F32), VMEM((count, 8, width), F32), VMEM((count, lines, 128), F32),
        ] + [DMA((count,))] * 8,
        compiler_params=pltpu.CompilerParams(collective_id=1, has_side_effects=True),
        name="regroup",
    )(base, partial, rows, slots)

    return pl.pallas_call(
        finish_kernel,
        out_shape=(
            jax.ShapeDtypeStruct((1, 1, width, width), F32),
            jax.ShapeDtypeStruct((count, 1, span), F32),
        ),
        in_specs=[vmem] * 5,
        out_specs=(vmem, vmem),
        scratch_shapes=[VMEM((width, width), F32)],
        name="finish",
    )(reduced, base, spread, taken, bare_own)


def solution(mesh):
    count, spaces = mesh.shape["energy"], mesh.shape["space"]
    return jax.shard_map(
        functools.partial(on_device, count, spaces),
        mesh=mesh,
        in_specs=(
            P("space", None, None),
            P("space", None, None),
            P("energy"),
            P("space", None),
            P("space", "energy"),
        ),
        out_specs=(P("energy", "space", None, None), P(None, "space", "energy")),
        check_vma=False,
    )
```

```python
import functools

import jax
import jax.numpy as jnp
from jax import lax
from jax.experimental import pallas as pl
from jax.experimental.pallas import tpu as pltpu
from jax.sharding import PartitionSpec as P

F32, BF16 = jnp.float32, jnp.bfloat16
MESH = pl.DeviceIdType.MESH
VMEM = pltpu.VMEM
DMA = pltpu.SemaphoreType.DMA

polar_coef = 128.0
sigma_coef = 0.5

TOLERANCE = 1e-6
VMEM_LIMIT = 20 << 20


def split(value):
    high = value.astype(BF16)
    return high, (value - high.astype(F32)).astype(BF16)


def dot(a, b):
    return jnp.dot(a, b, preferred_element_type=F32)


def dot_nt(a, b):
    return lax.dot_general(a, b, (((1,), (1,)), ((), ())), preferred_element_type=F32)


def mul(a, b):
    return dot(a[0], b[0]) + (dot(a[0], b[1]) + dot(a[1], b[0]))


def product(a, b):
    return mul(split(a), split(b))


def identity(width):
    rows = lax.broadcasted_iota(jnp.int32, (width, width), 0)
    cols = lax.broadcasted_iota(jnp.int32, (width, width), 1)
    return jnp.where(rows == cols, 1.0, 0.0).astype(F32)


def series(matrix, alpha, doublings):
    power = identity(matrix.shape[0]) - matrix * alpha
    guess = alpha * (identity(matrix.shape[0]) + power)
    for _ in range(doublings):
        high = power.astype(BF16)
        power = dot(high, high)
        guess = guess + dot(guess.astype(BF16), power.astype(BF16))
    return guess


def total_of(value):
    return jnp.sum(jnp.sum(value, axis=0, keepdims=True), axis=1, keepdims=True)


def mean_scale(matrix):
    trace = total_of(jnp.where(identity(matrix.shape[0]) > 0.0, matrix, 0.0))
    return trace / total_of(matrix * matrix)


def safe_scale(matrix):
    return 1.9 / jnp.max(jnp.sum(jnp.abs(matrix), axis=0, keepdims=True), axis=1, keepdims=True)


def eliminate(matrix, out_ref):
    width = matrix.shape[0]
    out_ref[...] = matrix
    lanes = lax.broadcasted_iota(jnp.int32, (1, width), 1)

    def step(pivot, carry):
        whole = out_ref[...]
        row = out_ref[pl.ds(pivot, 1), :]
        here = lanes == pivot
        value = jnp.sum(jnp.where(here, row, 0.0), axis=1, keepdims=True)
        column = jnp.sum(jnp.where(here, whole, 0.0), axis=1, keepdims=True)
        scaled = jnp.where(here, 1.0, row) / value
        out_ref[...] = jnp.where(here, 0.0, whole) - column * scaled
        out_ref[pl.ds(pivot, 1), :] = scaled
        return carry

    lax.fori_loop(0, width, step, 0)


def newton(matrices, refs, limit):
    ident = identity(matrices[0].shape[0])
    parts = [split(matrix) for matrix in matrices]

    def unsettled(carry):
        steps, worst = carry
        return jnp.logical_and(worst > TOLERANCE, steps < limit)

    def step(carry):
        worst = jnp.float32(0.0)
        for own, ref in zip(parts, refs):
            guess = ref[...]
            guess_parts = split(guess)
            residual = ident - mul(own, guess_parts)
            ref[...] = guess + dot(guess_parts[0], residual.astype(BF16))
            worst = jnp.maximum(worst, jnp.sum(residual * residual))
        return carry[0] + 1, worst

    return lax.while_loop(unsettled, step, (jnp.int32(0), jnp.float32(1.0)))[1]


def settle(matrices, refs):
    worst = newton(matrices, refs, 8)

    @pl.when(jnp.logical_not(worst <= TOLERANCE))
    def _():
        for matrix, ref in zip(matrices, refs):
            ref[...] = series(matrix, safe_scale(matrix), 5)
        again = newton(matrices, refs, 48)

        @pl.when(jnp.logical_not(again <= TOLERANCE))
        def _():
            for matrix, ref in zip(matrices, refs):
                eliminate(matrix, ref)


def invert(matrices, refs):
    for matrix, ref in zip(matrices, refs):
        ref[...] = series(matrix, mean_scale(matrix), 3)
    settle(matrices, refs)


def peer_of(me, offset):
    core = lax.rem(me + offset, 2)
    y = lax.rem(me // 2 + offset // 2, 4)
    z = lax.rem(me // 8 + offset // 8, 4)
    return z * 8 + y * 2 + core


def block_copy(me, offset, source, target, slot, send_sems, recv_sems):
    peer = peer_of(me, offset)
    return pltpu.make_async_remote_copy(
        src_ref=source(peer), dst_ref=target(slot),
        send_sem=send_sems.at[offset], recv_sem=recv_sems.at[slot],
        device_id={"energy": peer}, device_id_type=MESH,
    )


def send_blocks(count, me, source, target, send_sems, recv_sems):
    def one(step, carry):
        block_copy(me, count - step, source, target, me, send_sems, recv_sems).start()
        return carry

    lax.fori_loop(1, count, one, 0)


def await_blocks(count, me, source, target, send_sems, recv_sems):
    def one(step, carry):
        offset = count - step
        copy = block_copy(me, offset, source, target, peer_of(me, offset), send_sems, recv_sems)
        copy.wait_send()
        copy.wait_recv()
        return carry

    lax.fori_loop(1, count, one, 0)


def rows_of(ref, peer):
    return ref.at[pl.ds(pl.multiple_of(peer * 8, 8), 8), :]


def collect_kernel(
    count, spaces, diag_ref, coup_ref, pattern_ref, bare_ref,
    diags_ref, coups_ref, rows_ref, slots_ref, partial_ref, bare_own_ref,
    own_pattern, own_bare, own_sem, far_send, far_recv, near_send, near_recv,
):
    me = lax.axis_index("energy")
    place = lax.axis_index("space")
    width = diag_ref.shape[1]
    half = width // 2
    core = lax.rem(me, 2)
    other = me + 1 - 2 * core
    span = bare_ref.shape[1]
    chunk = own_bare.shape[1]
    sides = (lax.rem(place + 1, spaces), lax.rem(place + spaces - 1, spaces))
    across = lax.rem(place + 2, spaces)

    barrier = pltpu.get_barrier_semaphore()
    for side in sides:
        pl.semaphore_signal(barrier, inc=1, device_id={"space": side}, device_id_type=MESH)
    pl.semaphore_signal(barrier, inc=1, device_id={"energy": other}, device_id_type=MESH)
    pl.semaphore_wait(barrier, 3)

    own_half = pl.ds(pl.multiple_of(core * half, half), half)
    other_half = pl.ds(pl.multiple_of((1 - core) * half, half), half)
    given = (diag_ref, coup_ref)
    stores = (diags_ref, coups_ref)

    def far(way, stage):
        kind = (way, 1 - way, way)[stage]
        block = place if stage < 2 else sides[1 - way]
        source = given[kind].at[0, own_half] if stage < 2 else stores[kind].at[block, own_half]
        return pltpu.make_async_remote_copy(
            src_ref=source, dst_ref=stores[kind].at[block, own_half],
            send_sem=far_send.at[way, stage], recv_sem=far_recv.at[way, stage],
            device_id={"space": sides[way]}, device_id_type=MESH)

    def near(way, stage, part):
        kind = (way, 1 - way, way)[stage]
        block = sides[1 - way] if stage < 2 else across
        piece = stores[kind].at[block, part]
        return pltpu.make_async_remote_copy(
            src_ref=piece, dst_ref=piece,
            send_sem=near_send.at[way, stage], recv_sem=near_recv.at[way, stage],
            device_id={"energy": other}, device_id_type=MESH)

    for stage in range(2):
        for way in range(2):
            far(way, stage).start()
    own_copies = [
        pltpu.make_async_copy(diag_ref.at[0], diags_ref.at[place], own_sem.at[0]),
        pltpu.make_async_copy(coup_ref.at[0], coups_ref.at[place], own_sem.at[1]),
    ]
    for copy in own_copies:
        copy.start()

    tail = chunk - 128
    for part in range(count):
        size = chunk if part < count - 1 else span
        if size < chunk:
            own_pattern[part, :, tail:] = jnp.zeros((1, 128), jnp.int32)
            rows_ref[part, :, tail:] = jnp.zeros((1, 128), jnp.int32)
            slots_ref[part, :, tail:] = jnp.zeros((1, 128), jnp.int32)
        piece = pattern_ref[:, part * span:part * span + size]
        own_pattern[part, :, :size] = piece
        row = lax.shift_right_logical(piece, 8)
        col = jnp.bitwise_and(piece, 255)
        high = jnp.maximum(row, col)
        low = jnp.minimum(row, col)
        lower = low >= 128
        pivot = high == low
        rows_ref[part, :, :size] = jnp.where(jnp.logical_and(lower, jnp.logical_not(pivot)), low - 128, high)
        slots_ref[part, :, :size] = jnp.where(lower, jnp.where(pivot, 128, high - 128), low)
    own_bare[:, tail:] = jnp.zeros((1, 128), F32)
    own_bare[:, :span] = bare_ref[...]

    for way in range(2):
        far(way, 0).wait_recv()
        far(way, 2).start()
        near(way, 0, own_half).start()

    mine = own_pattern[me]
    bare = own_bare[...]
    index = lax.broadcasted_iota(jnp.int32, (width, chunk), 0)
    on_row = index == lax.shift_right_logical(mine, 8)
    on_col = jnp.where(index == jnp.bitwise_and(mine, 255), 1.0, 0.0).astype(BF16)
    rest = bare
    total = None
    for _ in range(3):
        part = rest.astype(BF16).astype(F32)
        rest = rest - part
        term = dot_nt(jnp.where(on_row, part, 0.0).astype(BF16), on_col)
        total = term if total is None else total + term
    partial_ref[...] = total
    for line in range(chunk // 128):
        bare_own_ref[line:line + 1, :] = bare[:, line * 128:(line + 1) * 128]
    for line in range(chunk // 128, bare_own_ref.shape[0]):
        bare_own_ref[line:line + 1, :] = jnp.zeros((1, 128), F32)

    for stage in (1, 2):
        for way in range(2):
            far(way, stage).wait_recv()
            near(way, stage, own_half).start()
    for copy in own_copies:
        copy.wait()
    for stage in range(3):
        for way in range(2):
            far(way, stage).wait_send()
            near(way, stage, own_half).wait_send()
            near(way, stage, other_half).wait_recv()


def chain_kernel(
    shift_ref, diags_ref, coups_ref, reduced_ref, base_ref,
    v_ref, vt_ref, w_ref, wt_ref, c_ref, ct_ref, last_ref, x_ref, y_ref,
):
    place = lax.axis_index("space")
    width = base_ref.shape[0]
    shift = identity(width) * shift_ref[0]
    lead_parts = split(coups_ref[3])
    quarter = (
        dot_nt(lead_parts[0], lead_parts[0])
        + (dot_nt(lead_parts[0], lead_parts[1]) + dot_nt(lead_parts[1], lead_parts[0]))
    ) * 0.25
    last_ref[...] = diags_ref[3] - quarter
    lower = place <= 1

    def system(block):
        return jnp.where(block == 3, last_ref[...], diags_ref[block]) + shift

    def choose(block, flipped, ref, turned_ref):
        value = coups_ref[block]
        turned = value.T
        ref[...] = jnp.where(flipped, turned, value)
        turned_ref[...] = jnp.where(flipped, value, turned)

    first = jnp.where(place == 0, 1, jnp.where(place == 1, 0, jnp.where(place == 2, 3, 2)))
    second = jnp.where(lower, 3, 0)
    middle = jnp.where(lower, 2, 1)
    choose(1, jnp.logical_not(lower), c_ref, ct_ref)
    choose(jnp.where(lower, 2, 0), lower, v_ref, vt_ref)
    choose(jnp.where(lower, 0, 2), lax.rem(place, 2) == 0, w_ref, wt_ref)

    invert([system(first), system(second)], [x_ref, y_ref])
    x = split(x_ref[...])
    y = split(y_ref[...])
    wt_s = split(wt_ref[...])
    xw = split(mul(x, split(w_ref[...])))
    yv = split(mul(y, split(v_ref[...])))
    reduced_ref[...] = system(place) - mul(wt_s, xw)
    last_ref[...] = system(middle) - mul(split(vt_ref[...]), yv)

    @pl.when(jnp.logical_or(place == 0, place == 3))
    def _():
        xu = split(mul(x, split(c_ref[...])))
        ut_s = split(ct_ref[...])
        last_ref[...] = last_ref[...] - mul(ut_s, xu)
        c_ref[...] = mul(wt_s, xu)
        ct_ref[...] = mul(ut_s, xw)

    invert([last_ref[...]], [x_ref])
    cz = split(product(c_ref[...], x_ref[...]))
    reduced = reduced_ref[...] - mul(cz, split(ct_ref[...]))
    reduced_ref[...] = reduced
    invert([reduced], [base_ref])


def screen(samples, bare, scale):
    count = len(samples)
    result = []
    for lag in range(count):
        total = samples[0] * samples[lag]
        for m in range(1, count - lag):
            total = total + samples[m] * samples[m + lag]
        scaled = bare * (total * scale)
        result.append(bare * lax.rsqrt(1.0 + scaled * scaled))
    return result


PAIRS_FIRST = 2
PAIRS_SECOND = 7


def regroup_kernel(
    count, base_ref, partial_ref, rows_ref, slots_ref, spread_ref, taken_ref,
    lhs, outgoing, arrived, selfen, taken, send_a, recv_a, send_b, recv_b, send_c, recv_c,
):
    me = lax.axis_index("energy")
    width = base_ref.shape[0]
    half = width // 2
    chunk = rows_ref.shape[2]
    lines = taken.shape[1]
    pairs = count // 2

    barrier = pltpu.get_barrier_semaphore()

    def greet(step, carry):
        pl.semaphore_signal(
            barrier, inc=1, device_id={"energy": peer_of(me, count - step)}, device_id_type=MESH)
        return carry

    lax.fori_loop(1, count, greet, 0)
    for peer in range(count):
        outgoing[peer, :8, :] = base_ref[peer * 8:peer * 8 + 8, :]
        outgoing[peer, 8:, :] = partial_ref[peer * 8:peer * 8 + 8, :]
    arrived[me] = outgoing[me]

    upper = base_ref[:half, :half]
    lower = base_ref[half:, half:]
    r = lax.broadcasted_iota(jnp.int32, (half, half), 0)
    c = lax.broadcasted_iota(jnp.int32, (half, half), 1)
    table = jnp.concatenate([jnp.where(r <= c, upper, lower), base_ref[:half, half:]], axis=1)
    diagonal = jnp.sum(jnp.where(r == c, lower, 0.0), axis=0, keepdims=True)
    extra = jnp.concatenate([jnp.zeros((1, half), F32), diagonal], axis=1)
    first = lax.broadcasted_iota(jnp.int32, (8, width), 0) == 0
    table = jnp.concatenate([table, jnp.where(first, extra, 0.0)], axis=0)
    tall = table.shape[0]
    high = table.astype(BF16).astype(F32)
    lhs[...] = jnp.concatenate([high, table - high], axis=0).astype(BF16)
    row_index = lax.broadcasted_iota(jnp.int32, (width, chunk), 0).astype(F32).astype(BF16)
    line_index = lax.broadcasted_iota(jnp.int32, (8, chunk), 0)
    one, none = jnp.bfloat16(1), jnp.bfloat16(0)

    def take(part):
        hot = jnp.where(row_index == rows_ref[part].astype(F32).astype(BF16), one, none)
        both = dot(lhs[...], hot)
        slots = slots_ref[part]
        group = jnp.broadcast_to(lax.shift_right_logical(slots, 3), (8, chunk))
        found, found_rest = both[:8], both[tall:tall + 8]
        for at in range(1, tall // 8):
            here = group == at
            found = jnp.where(here, both[at * 8:at * 8 + 8], found)
            found_rest = jnp.where(here, both[tall + at * 8:tall + at * 8 + 8], found_rest)
        here = line_index == jnp.bitwise_and(slots, 7)
        line = jnp.sum(jnp.where(here, found + found_rest, 0.0), axis=0, keepdims=True)
        for piece in range(chunk // 128):
            taken[part, piece:piece + 1, :] = line[:, piece * 128:(piece + 1) * 128]
        taken[part, chunk // 128:, :] = jnp.zeros((lines - chunk // 128, 128), F32)

    source_a, target_a = lambda peer: outgoing.at[peer], lambda slot: arrived.at[slot]
    source_b, target_b = lambda peer: selfen.at[peer], lambda slot: rows_of(spread_ref, slot)
    source_c, target_c = lambda peer: taken.at[peer], lambda slot: taken_ref.at[slot]

    def take_pair(pair, carry):
        take(peer_of(me, count - 1 - 2 * pair))
        take(peer_of(me, count - 2 - 2 * pair))
        return carry

    def send_pair(pair, carry):
        for offset in (count - 1 - 2 * pair, count - 2 - 2 * pair):
            block_copy(me, offset, source_c, target_c, me, send_c, recv_c).start()
        return carry

    def take_and_send(pair, carry):
        take_pair(pair, carry)
        return send_pair(pair, carry)

    lax.fori_loop(0, PAIRS_FIRST, take_pair, 0)
    pl.semaphore_wait(barrier, count - 1)
    send_blocks(count, me, source_a, target_a, send_a, recv_a)
    lax.fori_loop(0, PAIRS_FIRST, send_pair, 0)
    lax.fori_loop(PAIRS_FIRST, PAIRS_FIRST + PAIRS_SECOND, take_and_send, 0)
    await_blocks(count, me, source_a, target_a, send_a, recv_a)

    scale = polar_coef * width / count
    for side in range(width // 128):
        cols = slice(side * 128, (side + 1) * 128)
        bare = arrived[0, 8:, cols]
        for e in range(1, count):
            bare = bare + arrived[e, 8:, cols]
        samples = [arrived[e, :8, cols] for e in range(count)]
        screened = screen(samples, bare, scale)
        for e in range(count):
            total = samples[e] * screened[0]
            for n in range(1, e + 1):
                total = total + samples[e - n] * screened[n]
            selfen[e, :, cols] = total * (sigma_coef / count)
    send_blocks(count, me, source_b, target_b, send_b, recv_b)
    lax.fori_loop(PAIRS_FIRST + PAIRS_SECOND, pairs - 1, take_and_send, 0)
    take_pair(pairs - 1, 0)
    block_copy(me, 1, source_c, target_c, me, send_c, recv_c).start()
    taken_ref[me] = taken[me]
    spread_ref[pl.ds(pl.multiple_of(me * 8, 8), 8), :] = selfen[me]
    await_blocks(count, me, source_b, target_b, send_b, recv_b)
    await_blocks(count, me, source_c, target_c, send_c, recv_c)


def finish_kernel(reduced_ref, base_ref, spread_ref, taken_ref, bare_ref, green_ref, screened_ref, x_ref):
    count = taken_ref.shape[0]
    width = base_ref.shape[0]
    chunk = screened_ref.shape[2]
    spread = spread_ref[...]
    matrix = reduced_ref[...] - 0.5 * (spread + spread.T)
    x_ref[...] = base_ref[...]
    settle([matrix], [x_ref])
    green_ref[0, 0] = x_ref[...]
    scale = polar_coef * width / count
    for group in range(taken_ref.shape[1] // 8):
        lines = slice(group * 8, group * 8 + 8)
        samples = [taken_ref[e, lines, :] for e in range(count)]
        screened = screen(samples, bare_ref[lines, :], scale)
        for line in range(group * 8, min(group * 8 + 8, pl.cdiv(chunk, 128))):
            start = line * 128
            stop = min(start + 128, chunk)
            for n in range(count):
                at = line - group * 8
                screened_ref[n, :, start:stop] = screened[n][at:at + 1, :stop - start]


def on_device(count, spaces, ham_diag, ham_coup, energies, pattern, coulomb):
    width = ham_diag.shape[1]
    span = coulomb.shape[1]
    chunk = pl.cdiv(span, 128) * 128
    lines = pl.cdiv(chunk // 128, 8) * 8
    vmem = pl.BlockSpec(memory_space=pltpu.VMEM)
    smem = pl.BlockSpec(memory_space=pltpu.SMEM)
    square = jax.ShapeDtypeStruct((width, width), F32)
    diags, coups, rows, slots, partial, bare_own = pl.pallas_call(
        functools.partial(collect_kernel, count, spaces),
        out_shape=(
            jax.ShapeDtypeStruct((spaces, width, width), F32),
            jax.ShapeDtypeStruct((spaces, width, width), F32),
            jax.ShapeDtypeStruct((count, 1, chunk), jnp.int32),
            jax.ShapeDtypeStruct((count, 1, chunk), jnp.int32),
            square,
            jax.ShapeDtypeStruct((lines, 128), F32),
        ),
        in_specs=[vmem] * 4,
        out_specs=(vmem,) * 6,
        scratch_shapes=[
            VMEM((count, 1, chunk), jnp.int32), VMEM((1, chunk), F32),
            DMA((2,)), DMA((2, 3)), DMA((2, 3)), DMA((2, 3)), DMA((2, 3)),
        ],
        compiler_params=pltpu.CompilerParams(collective_id=0, has_side_effects=True, vmem_limit_bytes=VMEM_LIMIT),
        name="collect",
    )(ham_diag, ham_coup, pattern, coulomb)

    reduced, base = pl.pallas_call(
        chain_kernel,
        out_shape=(square, square),
        in_specs=[smem, vmem, vmem],
        out_specs=(vmem, vmem),
        scratch_shapes=[VMEM((width, width), F32)] * 9,
        compiler_params=pltpu.CompilerParams(vmem_limit_bytes=VMEM_LIMIT),
        name="chain",
    )(energies, diags, coups)

    spread, taken = pl.pallas_call(
        functools.partial(regroup_kernel, count),
        out_shape=(square, jax.ShapeDtypeStruct((count, lines, 128), F32)),
        in_specs=[vmem] * 4,
        out_specs=(vmem, vmem),
        scratch_shapes=[
            VMEM((width + 16, width), BF16), VMEM((count, 16, width), F32), VMEM((count, 16, width), F32),
            VMEM((count, 8, width), F32), VMEM((count, lines, 128), F32),
        ] + [DMA((count,))] * 6,
        compiler_params=pltpu.CompilerParams(collective_id=1, has_side_effects=True, vmem_limit_bytes=VMEM_LIMIT),
        name="regroup",
    )(base, partial, rows, slots)

    return pl.pallas_call(
        finish_kernel,
        out_shape=(
            jax.ShapeDtypeStruct((1, 1, width, width), F32),
            jax.ShapeDtypeStruct((count, 1, span), F32),
        ),
        in_specs=[vmem] * 5,
        out_specs=(vmem, vmem),
        scratch_shapes=[VMEM((width, width), F32)],
        compiler_params=pltpu.CompilerParams(vmem_limit_bytes=VMEM_LIMIT),
        name="finish",
    )(reduced, base, spread, taken, bare_own)


def solution(mesh):
    count, spaces = mesh.shape["energy"], mesh.shape["space"]
    return jax.shard_map(
        functools.partial(on_device, count, spaces),
        mesh=mesh,
        in_specs=(
            P("space", None, None),
            P("space", None, None),
            P("energy"),
            P("space", None),
            P("space", "energy"),
        ),
        out_specs=(P("energy", "space", None, None), P(None, "space", "energy")),
        check_vma=False,
    )
```

```python
import functools

import jax
import jax.numpy as jnp
from jax import lax
from jax.experimental import pallas as pl
from jax.experimental.pallas import tpu as pltpu
from jax.sharding import PartitionSpec as P

F32, BF16 = jnp.float32, jnp.bfloat16
MESH = pl.DeviceIdType.MESH
VMEM = pltpu.VMEM
DMA = pltpu.SemaphoreType.DMA

polar_coef = 128.0
sigma_coef = 0.5

TOLERANCE = 1e-6
VMEM_LIMIT = 20 << 20


def split(value):
    high = value.astype(BF16)
    return high, (value - high.astype(F32)).astype(BF16)


def dot(a, b):
    return jnp.dot(a, b, preferred_element_type=F32)


def dot_nt(a, b):
    return lax.dot_general(a, b, (((1,), (1,)), ((), ())), preferred_element_type=F32)


def mul(a, b):
    return dot(a[0], b[0]) + (dot(a[0], b[1]) + dot(a[1], b[0]))


def product(a, b):
    return mul(split(a), split(b))


def identity(width):
    rows = lax.broadcasted_iota(jnp.int32, (width, width), 0)
    cols = lax.broadcasted_iota(jnp.int32, (width, width), 1)
    return jnp.where(rows == cols, 1.0, 0.0).astype(F32)


def series(matrix, alpha, doublings):
    power = identity(matrix.shape[0]) - matrix * alpha
    guess = alpha * (identity(matrix.shape[0]) + power)
    for _ in range(doublings):
        high = power.astype(BF16)
        power = dot(high, high)
        guess = guess + dot(guess.astype(BF16), power.astype(BF16))
    return guess


def total_of(value):
    return jnp.sum(jnp.sum(value, axis=0, keepdims=True), axis=1, keepdims=True)


def mean_scale(matrix):
    trace = total_of(jnp.where(identity(matrix.shape[0]) > 0.0, matrix, 0.0))
    return trace / total_of(matrix * matrix)


def safe_scale(matrix):
    return 1.9 / jnp.max(jnp.sum(jnp.abs(matrix), axis=0, keepdims=True), axis=1, keepdims=True)


def eliminate(matrix, out_ref):
    width = matrix.shape[0]
    out_ref[...] = matrix
    lanes = lax.broadcasted_iota(jnp.int32, (1, width), 1)

    def step(pivot, carry):
        whole = out_ref[...]
        row = out_ref[pl.ds(pivot, 1), :]
        here = lanes == pivot
        value = jnp.sum(jnp.where(here, row, 0.0), axis=1, keepdims=True)
        column = jnp.sum(jnp.where(here, whole, 0.0), axis=1, keepdims=True)
        scaled = jnp.where(here, 1.0, row) / value
        out_ref[...] = jnp.where(here, 0.0, whole) - column * scaled
        out_ref[pl.ds(pivot, 1), :] = scaled
        return carry

    lax.fori_loop(0, width, step, 0)


def newton(matrices, refs, limit):
    ident = identity(matrices[0].shape[0])
    parts = [split(matrix) for matrix in matrices]

    def unsettled(carry):
        steps, worst = carry
        return jnp.logical_and(worst > TOLERANCE, steps < limit)

    def step(carry):
        worst = jnp.float32(0.0)
        for own, ref in zip(parts, refs):
            guess = ref[...]
            guess_parts = split(guess)
            residual = ident - mul(own, guess_parts)
            ref[...] = guess + dot(guess_parts[0], residual.astype(BF16))
            worst = jnp.maximum(worst, jnp.sum(residual * residual))
        return carry[0] + 1, worst

    return lax.while_loop(unsettled, step, (jnp.int32(0), jnp.float32(1.0)))[1]


def settle(matrices, refs):
    worst = newton(matrices, refs, 8)

    @pl.when(jnp.logical_not(worst <= TOLERANCE))
    def _():
        for matrix, ref in zip(matrices, refs):
            ref[...] = series(matrix, safe_scale(matrix), 5)
        again = newton(matrices, refs, 48)

        @pl.when(jnp.logical_not(again <= TOLERANCE))
        def _():
            for matrix, ref in zip(matrices, refs):
                eliminate(matrix, ref)


def invert(matrices, refs):
    for matrix, ref in zip(matrices, refs):
        ref[...] = series(matrix, mean_scale(matrix), 3)
    settle(matrices, refs)


def peer_of(me, offset):
    core = lax.rem(me + offset, 2)
    y = lax.rem(me // 2 + offset // 2, 4)
    z = lax.rem(me // 8 + offset // 8, 4)
    return z * 8 + y * 2 + core


def block_copy(me, offset, source, target, slot, send_sems, recv_sems):
    peer = peer_of(me, offset)
    return pltpu.make_async_remote_copy(
        src_ref=source(peer), dst_ref=target(slot),
        send_sem=send_sems.at[offset], recv_sem=recv_sems.at[slot],
        device_id={"energy": peer}, device_id_type=MESH,
    )


def send_blocks(count, me, source, target, send_sems, recv_sems):
    def one(step, carry):
        block_copy(me, count - step, source, target, me, send_sems, recv_sems).start()
        return carry

    lax.fori_loop(1, count, one, 0)


def await_blocks(count, me, source, target, send_sems, recv_sems):
    def one(step, carry):
        offset = count - step
        copy = block_copy(me, offset, source, target, peer_of(me, offset), send_sems, recv_sems)
        copy.wait_send()
        copy.wait_recv()
        return carry

    lax.fori_loop(1, count, one, 0)


def rows_of(ref, peer):
    return ref.at[pl.ds(pl.multiple_of(peer * 8, 8), 8), :]


def collect_kernel(
    count, spaces, diag_ref, coup_ref, pattern_ref, bare_ref,
    diags_ref, coups_ref, rows_ref, slots_ref, bare_pos_ref, bare_own_ref,
    pattern, bare_in, own_pattern, own_bare, scattered, from_core, by_y, from_y, by_z, from_z,
    own_sem, far_send, far_recv, near_send, near_recv, core_sems, y_send, y_recv, z_send, z_recv,
):
    me = lax.axis_index("energy")
    place = lax.axis_index("space")
    width = diag_ref.shape[1]
    half = width // 2
    core = lax.rem(me, 2)
    other = me + 1 - 2 * core
    own_y = lax.rem(me // 2, 4)
    own_z = me // 8
    span = bare_ref.shape[1]
    chunk = own_bare.shape[1]
    sides = (lax.rem(place + 1, spaces), lax.rem(place + spaces - 1, spaces))
    across = lax.rem(place + 2, spaces)

    own_copies = [
        pltpu.make_async_copy(pattern_ref, pattern, own_sem.at[0]),
        pltpu.make_async_copy(bare_ref, bare_in, own_sem.at[1]),
        pltpu.make_async_copy(diag_ref.at[0], diags_ref.at[place], own_sem.at[2]),
        pltpu.make_async_copy(coup_ref.at[0], coups_ref.at[place], own_sem.at[3]),
    ]
    for copy in own_copies:
        copy.start()

    barrier = pltpu.get_barrier_semaphore()
    for side in sides:
        pl.semaphore_signal(barrier, inc=1, device_id={"space": side}, device_id_type=MESH)
    for step in (2, 1, 3):
        for stride in (2, 8):
            pl.semaphore_signal(
                barrier, inc=1, device_id={"energy": peer_of(me, step * stride)}, device_id_type=MESH)
    pl.semaphore_signal(barrier, inc=1, device_id={"energy": other}, device_id_type=MESH)
    pl.semaphore_wait(barrier, 9)

    own_half = pl.ds(pl.multiple_of(core * half, half), half)
    other_half = pl.ds(pl.multiple_of((1 - core) * half, half), half)
    given = (diag_ref, coup_ref)
    stores = (diags_ref, coups_ref)

    def far(way, stage):
        kind = (way, 1 - way, way)[stage]
        block = place if stage < 2 else sides[1 - way]
        source = given[kind].at[0, own_half] if stage < 2 else stores[kind].at[block, own_half]
        return pltpu.make_async_remote_copy(
            src_ref=source, dst_ref=stores[kind].at[block, own_half],
            send_sem=far_send.at[way, stage], recv_sem=far_recv.at[way, stage],
            device_id={"space": sides[way]}, device_id_type=MESH)

    def near(way, stage, part):
        kind = (way, 1 - way, way)[stage]
        block = sides[1 - way] if stage < 2 else across
        piece = stores[kind].at[block, part]
        return pltpu.make_async_remote_copy(
            src_ref=piece, dst_ref=piece,
            send_sem=near_send.at[way, stage], recv_sem=near_recv.at[way, stage],
            device_id={"energy": other}, device_id_type=MESH)

    for stage in range(2):
        for way in range(2):
            far(way, stage).start()

    own_copies[0].wait()
    own_copies[1].wait()
    tail = chunk - 128
    for part in range(count):
        size = chunk if part < count - 1 else span
        if size < chunk:
            own_pattern[part, :, tail:] = jnp.zeros((1, 128), jnp.int32)
            rows_ref[part, :, tail:] = jnp.zeros((1, 128), jnp.int32)
            slots_ref[part, :, tail:] = jnp.zeros((1, 128), jnp.int32)
        piece = pattern[:, part * span:part * span + size]
        own_pattern[part, :, :size] = piece
        row = lax.shift_right_logical(piece, 8)
        col = jnp.bitwise_and(piece, 255)
        high = jnp.maximum(row, col)
        low = jnp.minimum(row, col)
        lower = low >= 128
        pivot = high == low
        rows_ref[part, :, :size] = jnp.where(jnp.logical_and(lower, jnp.logical_not(pivot)), low - 128, high)
        slots_ref[part, :, :size] = jnp.where(lower, jnp.where(pivot, 128, high - 128), low)
    own_bare[:, tail:] = jnp.zeros((1, 128), F32)
    own_bare[:, :span] = bare_in[...]

    mine = own_pattern[me]
    bare = own_bare[...]
    index = lax.broadcasted_iota(jnp.int32, (width, chunk), 0)
    on_row = index == lax.shift_right_logical(mine, 8)
    on_col = jnp.where(index == jnp.bitwise_and(mine, 255), 1.0, 0.0).astype(BF16)
    rest = bare
    total = None
    for _ in range(3):
        part = rest.astype(BF16).astype(F32)
        rest = rest - part
        term = dot_nt(jnp.where(on_row, part, 0.0).astype(BF16), on_col)
        total = term if total is None else total + term
    for peer in range(count):
        scattered[peer % 2, peer // 2 % 4, peer // 8] = total[peer * 8:peer * 8 + 8, :]
    for line in range(chunk // 128):
        bare_own_ref[line:line + 1, :] = bare[:, line * 128:(line + 1) * 128]
    for line in range(chunk // 128, bare_own_ref.shape[0]):
        bare_own_ref[line:line + 1, :] = jnp.zeros((1, 128), F32)

    for way in range(2):
        far(way, 0).wait_recv()
        far(way, 2).start()
        near(way, 0, own_half).start()

    to_core = pltpu.make_async_remote_copy(
        src_ref=scattered.at[1 - core], dst_ref=from_core,
        send_sem=core_sems.at[0], recv_sem=core_sems.at[1],
        device_id={"energy": other}, device_id_type=MESH)

    def to_y(step):
        return pltpu.make_async_remote_copy(
            src_ref=by_y.at[lax.rem(own_y + step, 4)], dst_ref=from_y.at[step],
            send_sem=y_send.at[step], recv_sem=y_recv.at[step],
            device_id={"energy": peer_of(me, 2 * step)}, device_id_type=MESH)

    def to_z(step):
        return pltpu.make_async_remote_copy(
            src_ref=by_z.at[lax.rem(own_z + step, 4)], dst_ref=from_z.at[step],
            send_sem=z_send.at[step], recv_sem=z_recv.at[step],
            device_id={"energy": peer_of(me, 8 * step)}, device_id_type=MESH)

    to_core.start()
    to_core.wait()
    for y in range(4):
        for z in range(4):
            by_y[y, z] = scattered[core, y, z] + from_core[y, z]
    for step in (2, 1, 3):
        to_y(step).start()
    for way in range(2):
        far(way, 1).wait_recv()
        near(way, 1, own_half).start()
    for step in (1, 3, 2):
        to_y(step).wait()
    for z in range(4):
        by_z[z] = (by_y[own_y, z] + from_y[1, z]) + (from_y[2, z] + from_y[3, z])
    for step in (2, 1, 3):
        to_z(step).start()
    for way in range(2):
        far(way, 2).wait_recv()
        near(way, 2, own_half).start()
    for step in (1, 3, 2):
        to_z(step).wait()
    bare_pos_ref[...] = (by_z[own_z] + from_z[1]) + (from_z[2] + from_z[3])
    for copy in own_copies[2:]:
        copy.wait()
    for stage in range(3):
        for way in range(2):
            far(way, stage).wait_send()
            near(way, stage, own_half).wait_send()
            near(way, stage, other_half).wait_recv()


def chain_kernel(
    shift_ref, diags_ref, coups_ref, reduced_ref, base_ref,
    v_ref, vt_ref, w_ref, wt_ref, c_ref, ct_ref, last_ref, x_ref, y_ref,
):
    place = lax.axis_index("space")
    width = base_ref.shape[0]
    shift = identity(width) * shift_ref[0]
    lead_parts = split(coups_ref[3])
    quarter = (
        dot_nt(lead_parts[0], lead_parts[0])
        + (dot_nt(lead_parts[0], lead_parts[1]) + dot_nt(lead_parts[1], lead_parts[0]))
    ) * 0.25
    last_ref[...] = diags_ref[3] - quarter
    lower = place <= 1

    def system(block):
        return jnp.where(block == 3, last_ref[...], diags_ref[block]) + shift

    def choose(block, flipped, ref, turned_ref):
        value = coups_ref[block]
        turned = value.T
        ref[...] = jnp.where(flipped, turned, value)
        turned_ref[...] = jnp.where(flipped, value, turned)

    first = jnp.where(place == 0, 1, jnp.where(place == 1, 0, jnp.where(place == 2, 3, 2)))
    second = jnp.where(lower, 3, 0)
    middle = jnp.where(lower, 2, 1)
    choose(1, jnp.logical_not(lower), c_ref, ct_ref)
    choose(jnp.where(lower, 2, 0), lower, v_ref, vt_ref)
    choose(jnp.where(lower, 0, 2), lax.rem(place, 2) == 0, w_ref, wt_ref)

    invert([system(first), system(second)], [x_ref, y_ref])
    x = split(x_ref[...])
    y = split(y_ref[...])
    wt_s = split(wt_ref[...])
    xw = split(mul(x, split(w_ref[...])))
    yv = split(mul(y, split(v_ref[...])))
    reduced_ref[...] = system(place) - mul(wt_s, xw)
    last_ref[...] = system(middle) - mul(split(vt_ref[...]), yv)

    @pl.when(jnp.logical_or(place == 0, place == 3))
    def _():
        xu = split(mul(x, split(c_ref[...])))
        ut_s = split(ct_ref[...])
        last_ref[...] = last_ref[...] - mul(ut_s, xu)
        c_ref[...] = mul(wt_s, xu)
        ct_ref[...] = mul(ut_s, xw)

    invert([last_ref[...]], [x_ref])
    cz = split(product(c_ref[...], x_ref[...]))
    reduced = reduced_ref[...] - mul(cz, split(ct_ref[...]))
    reduced_ref[...] = reduced
    invert([reduced], [base_ref])


def screen(samples, bare, scale):
    count = len(samples)
    result = []
    for lag in range(count):
        total = samples[0] * samples[lag]
        for m in range(1, count - lag):
            total = total + samples[m] * samples[m + lag]
        scaled = bare * (total * scale)
        result.append(bare * lax.rsqrt(1.0 + scaled * scaled))
    return result


PAIRS_FIRST = 2
PAIRS_SECOND = 7


def regroup_kernel(
    count, base_ref, rows_ref, slots_ref, bare_pos_ref, spread_ref, taken_ref,
    lhs, arrived, selfen, taken, send_a, recv_a, send_b, recv_b, send_c, recv_c,
):
    me = lax.axis_index("energy")
    width = base_ref.shape[0]
    half = width // 2
    chunk = rows_ref.shape[2]
    lines = taken.shape[1]
    pairs = count // 2

    barrier = pltpu.get_barrier_semaphore()

    def greet(step, carry):
        pl.semaphore_signal(
            barrier, inc=1, device_id={"energy": peer_of(me, count - step)}, device_id_type=MESH)
        return carry

    lax.fori_loop(1, count, greet, 0)
    arrived[me] = rows_of(base_ref, me)[...]

    upper = base_ref[:half, :half]
    lower = base_ref[half:, half:]
    r = lax.broadcasted_iota(jnp.int32, (half, half), 0)
    c = lax.broadcasted_iota(jnp.int32, (half, half), 1)
    table = jnp.concatenate([jnp.where(r <= c, upper, lower), base_ref[:half, half:]], axis=1)
    diagonal = jnp.sum(jnp.where(r == c, lower, 0.0), axis=0, keepdims=True)
    extra = jnp.concatenate([jnp.zeros((1, half), F32), diagonal], axis=1)
    first = lax.broadcasted_iota(jnp.int32, (8, width), 0) == 0
    table = jnp.concatenate([table, jnp.where(first, extra, 0.0)], axis=0)
    tall = table.shape[0]
    high = table.astype(BF16).astype(F32)
    lhs[...] = jnp.concatenate([high, table - high], axis=0).astype(BF16)
    row_index = lax.broadcasted_iota(jnp.int32, (width, chunk), 0).astype(F32).astype(BF16)
    line_index = lax.broadcasted_iota(jnp.int32, (8, chunk), 0)
    one, none = jnp.bfloat16(1), jnp.bfloat16(0)

    def take(part):
        hot = jnp.where(row_index == rows_ref[part].astype(F32).astype(BF16), one, none)
        both = dot(lhs[...], hot)
        slots = slots_ref[part]
        group = jnp.broadcast_to(lax.shift_right_logical(slots, 3), (8, chunk))
        found, found_rest = both[:8], both[tall:tall + 8]
        for at in range(1, tall // 8):
            here = group == at
            found = jnp.where(here, both[at * 8:at * 8 + 8], found)
            found_rest = jnp.where(here, both[tall + at * 8:tall + at * 8 + 8], found_rest)
        here = line_index == jnp.bitwise_and(slots, 7)
        line = jnp.sum(jnp.where(here, found + found_rest, 0.0), axis=0, keepdims=True)
        for piece in range(chunk // 128):
            taken[part, piece:piece + 1, :] = line[:, piece * 128:(piece + 1) * 128]
        taken[part, chunk // 128:, :] = jnp.zeros((lines - chunk // 128, 128), F32)

    source_a, target_a = lambda peer: rows_of(base_ref, peer), lambda slot: arrived.at[slot]
    source_b, target_b = lambda peer: selfen.at[peer], lambda slot: rows_of(spread_ref, slot)
    source_c, target_c = lambda peer: taken.at[peer], lambda slot: taken_ref.at[slot]

    def take_pair(pair, carry):
        take(peer_of(me, count - 1 - 2 * pair))
        take(peer_of(me, count - 2 - 2 * pair))
        return carry

    def send_pair(pair, carry):
        for offset in (count - 1 - 2 * pair, count - 2 - 2 * pair):
            block_copy(me, offset, source_c, target_c, me, send_c, recv_c).start()
        return carry

    def take_and_send(pair, carry):
        take_pair(pair, carry)
        return send_pair(pair, carry)

    lax.fori_loop(0, PAIRS_FIRST, take_pair, 0)
    pl.semaphore_wait(barrier, count - 1)
    send_blocks(count, me, source_a, target_a, send_a, recv_a)
    lax.fori_loop(0, PAIRS_FIRST, send_pair, 0)
    lax.fori_loop(PAIRS_FIRST, PAIRS_FIRST + PAIRS_SECOND, take_and_send, 0)
    await_blocks(count, me, source_a, target_a, send_a, recv_a)

    scale = polar_coef * width / count
    for side in range(width // 128):
        cols = slice(side * 128, (side + 1) * 128)
        samples = [arrived[e, :, cols] for e in range(count)]
        screened = screen(samples, bare_pos_ref[:, cols], scale)
        for e in range(count):
            total = samples[e] * screened[0]
            for n in range(1, e + 1):
                total = total + samples[e - n] * screened[n]
            selfen[e, :, cols] = total * (sigma_coef / count)
    send_blocks(count, me, source_b, target_b, send_b, recv_b)
    lax.fori_loop(PAIRS_FIRST + PAIRS_SECOND, pairs - 1, take_and_send, 0)
    take_pair(pairs - 1, 0)
    block_copy(me, 1, source_c, target_c, me, send_c, recv_c).start()
    taken_ref[me] = taken[me]
    spread_ref[pl.ds(pl.multiple_of(me * 8, 8), 8), :] = selfen[me]
    await_blocks(count, me, source_b, target_b, send_b, recv_b)
    await_blocks(count, me, source_c, target_c, send_c, recv_c)


def finish_kernel(reduced_ref, base_ref, spread_ref, taken_ref, bare_ref, green_ref, screened_ref, x_ref):
    count = taken_ref.shape[0]
    width = base_ref.shape[0]
    chunk = screened_ref.shape[2]
    spread = spread_ref[...]
    matrix = reduced_ref[...] - 0.5 * (spread + spread.T)
    x_ref[...] = base_ref[...]
    settle([matrix], [x_ref])
    green_ref[0, 0] = x_ref[...]
    scale = polar_coef * width / count
    for group in range(taken_ref.shape[1] // 8):
        lines = slice(group * 8, group * 8 + 8)
        samples = [taken_ref[e, lines, :] for e in range(count)]
        screened = screen(samples, bare_ref[lines, :], scale)
        for line in range(group * 8, min(group * 8 + 8, pl.cdiv(chunk, 128))):
            start = line * 128
            stop = min(start + 128, chunk)
            for n in range(count):
                at = line - group * 8
                screened_ref[n, :, start:stop] = screened[n][at:at + 1, :stop - start]


def on_device(count, spaces, ham_diag, ham_coup, energies, pattern, coulomb):
    width = ham_diag.shape[1]
    span = coulomb.shape[1]
    chunk = pl.cdiv(span, 128) * 128
    lines = pl.cdiv(chunk // 128, 8) * 8
    vmem = pl.BlockSpec(memory_space=pltpu.VMEM)
    smem = pl.BlockSpec(memory_space=pltpu.SMEM)
    square = jax.ShapeDtypeStruct((width, width), F32)
    diags, coups, rows, slots, bare_pos, bare_own = pl.pallas_call(
        functools.partial(collect_kernel, count, spaces),
        out_shape=(
            jax.ShapeDtypeStruct((spaces, width, width), F32),
            jax.ShapeDtypeStruct((spaces, width, width), F32),
            jax.ShapeDtypeStruct((count, 1, chunk), jnp.int32),
            jax.ShapeDtypeStruct((count, 1, chunk), jnp.int32),
            jax.ShapeDtypeStruct((8, width), F32),
            jax.ShapeDtypeStruct((lines, 128), F32),
        ),
        in_specs=[pl.BlockSpec(memory_space=pltpu.HBM)] * 4,
        out_specs=(vmem,) * 6,
        scratch_shapes=[
            VMEM((1, pattern.shape[1]), jnp.int32), VMEM((1, span), F32),
            VMEM((count, 1, chunk), jnp.int32), VMEM((1, chunk), F32),
            VMEM((2, 4, 4, 8, width), F32), VMEM((4, 4, 8, width), F32), VMEM((4, 4, 8, width), F32),
            VMEM((4, 4, 8, width), F32), VMEM((4, 8, width), F32), VMEM((4, 8, width), F32),
            DMA((4,)), DMA((2, 3)), DMA((2, 3)), DMA((2, 3)), DMA((2, 3)),
            DMA((2,)), DMA((4,)), DMA((4,)), DMA((4,)), DMA((4,)),
        ],
        compiler_params=pltpu.CompilerParams(collective_id=0, has_side_effects=True, vmem_limit_bytes=VMEM_LIMIT),
        name="collect",
    )(*(pltpu.with_memory_space_constraint(value, pltpu.HBM) for value in (ham_diag, ham_coup, pattern, coulomb)))

    reduced, base = pl.pallas_call(
        chain_kernel,
        out_shape=(square, square),
        in_specs=[smem, vmem, vmem],
        out_specs=(vmem, vmem),
        scratch_shapes=[VMEM((width, width), F32)] * 9,
        compiler_params=pltpu.CompilerParams(vmem_limit_bytes=VMEM_LIMIT),
        name="chain",
    )(energies, diags, coups)

    spread, taken = pl.pallas_call(
        functools.partial(regroup_kernel, count),
        out_shape=(square, jax.ShapeDtypeStruct((count, lines, 128), F32)),
        in_specs=[vmem] * 4,
        out_specs=(vmem, vmem),
        scratch_shapes=[
            VMEM((width + 16, width), BF16), VMEM((count, 8, width), F32),
            VMEM((count, 8, width), F32), VMEM((count, lines, 128), F32),
        ] + [DMA((count,))] * 6,
        compiler_params=pltpu.CompilerParams(collective_id=1, has_side_effects=True, vmem_limit_bytes=VMEM_LIMIT),
        name="regroup",
    )(base, rows, slots, bare_pos)

    return pl.pallas_call(
        finish_kernel,
        out_shape=(
            jax.ShapeDtypeStruct((1, 1, width, width), F32),
            jax.ShapeDtypeStruct((count, 1, span), F32),
        ),
        in_specs=[vmem] * 5,
        out_specs=(vmem, vmem),
        scratch_shapes=[VMEM((width, width), F32)],
        compiler_params=pltpu.CompilerParams(vmem_limit_bytes=VMEM_LIMIT),
        name="finish",
    )(reduced, base, spread, taken, bare_own)


def solution(mesh):
    count, spaces = mesh.shape["energy"], mesh.shape["space"]
    return jax.shard_map(
        functools.partial(on_device, count, spaces),
        mesh=mesh,
        in_specs=(
            P("space", None, None),
            P("space", None, None),
            P("energy"),
            P("space", None),
            P("space", "energy"),
        ),
        out_specs=(P("energy", "space", None, None), P(None, "space", "energy")),
        check_vma=False,
    )
```

```python
import functools

import jax
import jax.numpy as jnp
from jax import lax
from jax.experimental import pallas as pl
from jax.experimental.pallas import tpu as pltpu
from jax.sharding import PartitionSpec as P

F32, BF16 = jnp.float32, jnp.bfloat16
MESH = pl.DeviceIdType.MESH
VMEM = pltpu.VMEM
DMA = pltpu.SemaphoreType.DMA

polar_coef = 128.0
sigma_coef = 0.5

TOLERANCE = 1e-5
VMEM_LIMIT = 20 << 20


def split(value):
    high = value.astype(BF16)
    return high, (value - high.astype(F32)).astype(BF16)


def dot(a, b):
    return jnp.dot(a, b, preferred_element_type=F32)


def dot_nt(a, b):
    return lax.dot_general(a, b, (((1,), (1,)), ((), ())), preferred_element_type=F32)


def mul(a, b):
    return dot(a[0], b[0]) + (dot(a[0], b[1]) + dot(a[1], b[0]))


def product(a, b):
    return mul(split(a), split(b))


def identity(width):
    rows = lax.broadcasted_iota(jnp.int32, (width, width), 0)
    cols = lax.broadcasted_iota(jnp.int32, (width, width), 1)
    return jnp.where(rows == cols, 1.0, 0.0).astype(F32)


def series(matrix, alpha, doublings):
    power = identity(matrix.shape[0]) - matrix * alpha
    guess = alpha * (identity(matrix.shape[0]) + power)
    parts = split(power)
    power = mul(parts, parts)
    guess = guess + product(guess, power)
    for _ in range(doublings - 1):
        high = power.astype(BF16)
        power = dot(high, high)
        guess = guess + dot(guess.astype(BF16), power.astype(BF16))
    return guess


def total_of(value):
    return jnp.sum(jnp.sum(value, axis=0, keepdims=True), axis=1, keepdims=True)


def mean_scale(matrix):
    trace = total_of(jnp.where(identity(matrix.shape[0]) > 0.0, matrix, 0.0))
    return trace / total_of(matrix * matrix)


def safe_scale(matrix):
    return 1.9 / jnp.max(jnp.sum(jnp.abs(matrix), axis=0, keepdims=True), axis=1, keepdims=True)


def eliminate(matrix, out_ref):
    width = matrix.shape[0]
    out_ref[...] = matrix
    lanes = lax.broadcasted_iota(jnp.int32, (1, width), 1)

    def step(pivot, carry):
        whole = out_ref[...]
        row = out_ref[pl.ds(pivot, 1), :]
        here = lanes == pivot
        value = jnp.sum(jnp.where(here, row, 0.0), axis=1, keepdims=True)
        column = jnp.sum(jnp.where(here, whole, 0.0), axis=1, keepdims=True)
        scaled = jnp.where(here, 1.0, row) / value
        out_ref[...] = jnp.where(here, 0.0, whole) - column * scaled
        out_ref[pl.ds(pivot, 1), :] = scaled
        return carry

    lax.fori_loop(0, width, step, 0)


def newton(matrices, refs, limit):
    ident = identity(matrices[0].shape[0])
    parts = [split(matrix) for matrix in matrices]

    def unsettled(carry):
        steps, worst = carry
        return jnp.logical_and(worst > TOLERANCE, steps < limit)

    def step(carry):
        worst = jnp.float32(0.0)
        for own, ref in zip(parts, refs):
            guess = ref[...]
            guess_parts = split(guess)
            residual = ident - mul(own, guess_parts)
            ref[...] = guess + dot(guess_parts[0], residual.astype(BF16))
            worst = jnp.maximum(worst, jnp.sum(residual * residual))
        return carry[0] + 1, worst

    return lax.while_loop(unsettled, step, (jnp.int32(0), jnp.float32(1.0)))[1]


def settle(matrices, refs):
    worst = newton(matrices, refs, 8)

    @pl.when(jnp.logical_not(worst <= TOLERANCE))
    def _():
        for matrix, ref in zip(matrices, refs):
            ref[...] = series(matrix, safe_scale(matrix), 5)
        again = newton(matrices, refs, 48)

        @pl.when(jnp.logical_not(again <= TOLERANCE))
        def _():
            for matrix, ref in zip(matrices, refs):
                eliminate(matrix, ref)


def invert(matrices, refs):
    for matrix, ref in zip(matrices, refs):
        ref[...] = series(matrix, mean_scale(matrix), 3)
    settle(matrices, refs)


def peer_of(me, offset):
    core = lax.rem(me + offset, 2)
    y = lax.rem(me // 2 + offset // 2, 4)
    z = lax.rem(me // 8 + offset // 8, 4)
    return z * 8 + y * 2 + core


def block_copy(me, offset, source, target, slot, send_sems, recv_sems):
    peer = peer_of(me, offset)
    return pltpu.make_async_remote_copy(
        src_ref=source(peer), dst_ref=target(slot),
        send_sem=send_sems.at[offset], recv_sem=recv_sems.at[slot],
        device_id={"energy": peer}, device_id_type=MESH,
    )


def send_blocks(count, me, source, target, send_sems, recv_sems):
    def one(step, carry):
        block_copy(me, count - step, source, target, me, send_sems, recv_sems).start()
        return carry

    lax.fori_loop(1, count, one, 0)


def await_blocks(count, me, source, target, send_sems, recv_sems):
    def one(step, carry):
        offset = count - step
        copy = block_copy(me, offset, source, target, peer_of(me, offset), send_sems, recv_sems)
        copy.wait_send()
        copy.wait_recv()
        return carry

    lax.fori_loop(1, count, one, 0)


def rows_of(ref, peer):
    return ref.at[pl.ds(pl.multiple_of(peer * 8, 8), 8), :]


def collect_kernel(
    count, spaces, diag_ref, coup_ref, pattern_ref, bare_ref,
    diags_ref, coups_ref, rows_ref, slots_ref, bare_pos_ref, bare_own_ref,
    pattern, bare_in, own_pattern, own_bare, scattered, from_core, by_y, from_y, by_z, from_z,
    own_sem, far_send, far_recv, near_send, near_recv, core_sems, y_send, y_recv, z_send, z_recv,
):
    me = lax.axis_index("energy")
    place = lax.axis_index("space")
    width = diag_ref.shape[1]
    half = width // 2
    core = lax.rem(me, 2)
    other = me + 1 - 2 * core
    own_y = lax.rem(me // 2, 4)
    own_z = me // 8
    span = bare_ref.shape[1]
    chunk = own_bare.shape[1]
    sides = (lax.rem(place + 1, spaces), lax.rem(place + spaces - 1, spaces))
    across = lax.rem(place + 2, spaces)

    own_copies = [
        pltpu.make_async_copy(pattern_ref, pattern, own_sem.at[0]),
        pltpu.make_async_copy(bare_ref, bare_in, own_sem.at[1]),
        pltpu.make_async_copy(diag_ref.at[0], diags_ref.at[place], own_sem.at[2]),
        pltpu.make_async_copy(coup_ref.at[0], coups_ref.at[place], own_sem.at[3]),
    ]
    for copy in own_copies:
        copy.start()

    barrier = pltpu.get_barrier_semaphore()
    for side in sides:
        pl.semaphore_signal(barrier, inc=1, device_id={"space": side}, device_id_type=MESH)
    for step in (2, 1, 3):
        for stride in (2, 8):
            pl.semaphore_signal(
                barrier, inc=1, device_id={"energy": peer_of(me, step * stride)}, device_id_type=MESH)
    pl.semaphore_signal(barrier, inc=1, device_id={"energy": other}, device_id_type=MESH)

    own_copies[0].wait()
    own_copies[1].wait()
    tail = chunk - 128
    for part in range(count):
        size = chunk if part < count - 1 else span
        if size < chunk:
            own_pattern[part, :, tail:] = jnp.zeros((1, 128), jnp.int32)
            rows_ref[part, :, tail:] = jnp.zeros((1, 128), jnp.int32)
            slots_ref[part, :, tail:] = jnp.zeros((1, 128), jnp.int32)
        piece = pattern[:, part * span:part * span + size]
        own_pattern[part, :, :size] = piece
        row = lax.shift_right_logical(piece, 8)
        col = jnp.bitwise_and(piece, 255)
        high = jnp.maximum(row, col)
        low = jnp.minimum(row, col)
        lower = low >= 128
        pivot = high == low
        rows_ref[part, :, :size] = jnp.where(jnp.logical_and(lower, jnp.logical_not(pivot)), low - 128, high)
        slots_ref[part, :, :size] = jnp.where(lower, jnp.where(pivot, 128, high - 128), low)
    own_bare[:, tail:] = jnp.zeros((1, 128), F32)
    own_bare[:, :span] = bare_in[...]

    pl.semaphore_wait(barrier, 9)
    own_half = pl.ds(pl.multiple_of(core * half, half), half)
    other_half = pl.ds(pl.multiple_of((1 - core) * half, half), half)
    given = (diag_ref, coup_ref)
    stores = (diags_ref, coups_ref)

    def far(way, stage):
        kind = (way, 1 - way, way)[stage]
        block = place if stage < 2 else sides[1 - way]
        source = given[kind].at[0, own_half] if stage < 2 else stores[kind].at[block, own_half]
        return pltpu.make_async_remote_copy(
            src_ref=source, dst_ref=stores[kind].at[block, own_half],
            send_sem=far_send.at[way, stage], recv_sem=far_recv.at[way, stage],
            device_id={"space": sides[way]}, device_id_type=MESH)

    def near(way, stage, part):
        kind = (way, 1 - way, way)[stage]
        block = sides[1 - way] if stage < 2 else across
        piece = stores[kind].at[block, part]
        return pltpu.make_async_remote_copy(
            src_ref=piece, dst_ref=piece,
            send_sem=near_send.at[way, stage], recv_sem=near_recv.at[way, stage],
            device_id={"energy": other}, device_id_type=MESH)

    for stage in range(2):
        for way in range(2):
            far(way, stage).start()

    mine = own_pattern[me]
    bare = own_bare[...]
    index = lax.broadcasted_iota(jnp.int32, (width, chunk), 0)
    on_row = index == lax.shift_right_logical(mine, 8)
    on_col = jnp.where(index == jnp.bitwise_and(mine, 255), 1.0, 0.0).astype(BF16)
    rest = bare
    total = None
    for _ in range(3):
        part = rest.astype(BF16).astype(F32)
        rest = rest - part
        term = dot_nt(jnp.where(on_row, part, 0.0).astype(BF16), on_col)
        total = term if total is None else total + term
    for peer in range(count):
        scattered[peer % 2, peer // 2 % 4, peer // 8] = total[peer * 8:peer * 8 + 8, :]
    for line in range(chunk // 128):
        bare_own_ref[line:line + 1, :] = bare[:, line * 128:(line + 1) * 128]
    for line in range(chunk // 128, bare_own_ref.shape[0]):
        bare_own_ref[line:line + 1, :] = jnp.zeros((1, 128), F32)

    to_core = pltpu.make_async_remote_copy(
        src_ref=scattered.at[1 - core], dst_ref=from_core,
        send_sem=core_sems.at[0], recv_sem=core_sems.at[1],
        device_id={"energy": other}, device_id_type=MESH)

    def to_y(step):
        return pltpu.make_async_remote_copy(
            src_ref=by_y.at[lax.rem(own_y + step, 4)], dst_ref=from_y.at[step],
            send_sem=y_send.at[step], recv_sem=y_recv.at[step],
            device_id={"energy": peer_of(me, 2 * step)}, device_id_type=MESH)

    def to_z(step):
        return pltpu.make_async_remote_copy(
            src_ref=by_z.at[lax.rem(own_z + step, 4)], dst_ref=from_z.at[step],
            send_sem=z_send.at[step], recv_sem=z_recv.at[step],
            device_id={"energy": peer_of(me, 8 * step)}, device_id_type=MESH)

    to_core.start()
    for way in range(2):
        far(way, 0).wait_recv()
        far(way, 2).start()
        near(way, 0, own_half).start()
    to_core.wait()
    for y in range(4):
        for z in range(4):
            by_y[y, z] = scattered[core, y, z] + from_core[y, z]
    for step in (2, 1, 3):
        to_y(step).start()
    for step in (1, 3, 2):
        to_y(step).wait()
    for z in range(4):
        by_z[z] = (by_y[own_y, z] + from_y[1, z]) + (from_y[2, z] + from_y[3, z])
    for step in (2, 1, 3):
        to_z(step).start()
    for stage in (1, 2):
        for way in range(2):
            far(way, stage).wait_recv()
            near(way, stage, own_half).start()
    for step in (1, 3, 2):
        to_z(step).wait()
    bare_pos_ref[...] = (by_z[own_z] + from_z[1]) + (from_z[2] + from_z[3])
    for copy in own_copies[2:]:
        copy.wait()
    for stage in range(3):
        for way in range(2):
            far(way, stage).wait_send()
            near(way, stage, own_half).wait_send()
            near(way, stage, other_half).wait_recv()


def chain_kernel(
    shift_ref, diags_ref, coups_ref, reduced_ref, base_ref,
    v_ref, vt_ref, w_ref, wt_ref, c_ref, ct_ref, last_ref, x_ref, y_ref,
):
    place = lax.axis_index("space")
    width = base_ref.shape[0]
    shift = identity(width) * shift_ref[0]
    lead_parts = split(coups_ref[3])
    quarter = (
        dot_nt(lead_parts[0], lead_parts[0])
        + (dot_nt(lead_parts[0], lead_parts[1]) + dot_nt(lead_parts[1], lead_parts[0]))
    ) * 0.25
    last_ref[...] = diags_ref[3] - quarter
    lower = place <= 1

    def system(block):
        return jnp.where(block == 3, last_ref[...], diags_ref[block]) + shift

    def choose(block, flipped, ref, turned_ref):
        value = coups_ref[block]
        turned = value.T
        ref[...] = jnp.where(flipped, turned, value)
        turned_ref[...] = jnp.where(flipped, value, turned)

    first = jnp.where(place == 0, 1, jnp.where(place == 1, 0, jnp.where(place == 2, 3, 2)))
    second = jnp.where(lower, 3, 0)
    middle = jnp.where(lower, 2, 1)
    choose(1, jnp.logical_not(lower), c_ref, ct_ref)
    choose(jnp.where(lower, 2, 0), lower, v_ref, vt_ref)
    choose(jnp.where(lower, 0, 2), lax.rem(place, 2) == 0, w_ref, wt_ref)

    invert([system(first), system(second)], [x_ref, y_ref])
    x = split(x_ref[...])
    y = split(y_ref[...])
    wt_s = split(wt_ref[...])
    xw = split(mul(x, split(w_ref[...])))
    yv = split(mul(y, split(v_ref[...])))
    reduced_ref[...] = system(place) - mul(wt_s, xw)
    last_ref[...] = system(middle) - mul(split(vt_ref[...]), yv)

    @pl.when(jnp.logical_or(place == 0, place == 3))
    def _():
        xu = split(mul(x, split(c_ref[...])))
        ut_s = split(ct_ref[...])
        last_ref[...] = last_ref[...] - mul(ut_s, xu)
        c_ref[...] = mul(wt_s, xu)
        ct_ref[...] = mul(ut_s, xw)

    invert([last_ref[...]], [x_ref])
    cz = split(product(c_ref[...], x_ref[...]))
    reduced = reduced_ref[...] - mul(cz, split(ct_ref[...]))
    reduced_ref[...] = reduced
    invert([reduced], [base_ref])


def screen(samples, bare, scale):
    count = len(samples)
    result = []
    for lag in range(count):
        total = samples[0] * samples[lag]
        for m in range(1, count - lag):
            total = total + samples[m] * samples[m + lag]
        scaled = bare * (total * scale)
        result.append(bare * lax.rsqrt(1.0 + scaled * scaled))
    return result


PAIRS_FIRST = 2
PAIRS_SECOND = 9


def regroup_kernel(
    count, base_ref, rows_ref, slots_ref, bare_pos_ref, spread_ref, taken_ref,
    lhs, arrived, selfen, taken, send_a, recv_a, send_b, recv_b, send_c, recv_c,
):
    me = lax.axis_index("energy")
    width = base_ref.shape[0]
    half = width // 2
    chunk = rows_ref.shape[2]
    lines = taken.shape[1]
    pairs = count // 2
    for peer in range(count):
        taken_ref[peer, chunk // 128:, :] = jnp.zeros((lines - chunk // 128, 128), F32)

    barrier = pltpu.get_barrier_semaphore()

    def greet(step, carry):
        pl.semaphore_signal(
            barrier, inc=1, device_id={"energy": peer_of(me, count - step)}, device_id_type=MESH)
        return carry

    lax.fori_loop(1, count, greet, 0)
    arrived[me] = rows_of(base_ref, me)[...]

    upper = base_ref[:half, :half]
    lower = base_ref[half:, half:]
    r = lax.broadcasted_iota(jnp.int32, (half, half), 0)
    c = lax.broadcasted_iota(jnp.int32, (half, half), 1)
    table = jnp.concatenate([jnp.where(r <= c, upper, lower), base_ref[:half, half:]], axis=1)
    diagonal = jnp.sum(jnp.where(r == c, lower, 0.0), axis=0, keepdims=True)
    extra = jnp.concatenate([jnp.zeros((1, half), F32), diagonal], axis=1)
    first = lax.broadcasted_iota(jnp.int32, (8, width), 0) == 0
    table = jnp.concatenate([table, jnp.where(first, extra, 0.0)], axis=0)
    tall = table.shape[0]
    high = table.astype(BF16).astype(F32)
    lhs[...] = jnp.concatenate([high, table - high], axis=0).astype(BF16)
    row_index = lax.broadcasted_iota(jnp.int32, (width, chunk), 0).astype(F32).astype(BF16)
    line_index = lax.broadcasted_iota(jnp.int32, (8, chunk), 0)
    one, none = jnp.bfloat16(1), jnp.bfloat16(0)

    def take(part):
        hot = jnp.where(row_index == rows_ref[part].astype(F32).astype(BF16), one, none)
        both = dot(lhs[...], hot)
        slots = slots_ref[part]
        group = jnp.broadcast_to(lax.shift_right_logical(slots, 3), (8, chunk))
        found, found_rest = both[:8], both[tall:tall + 8]
        for at in range(1, tall // 8):
            here = group == at
            found = jnp.where(here, both[at * 8:at * 8 + 8], found)
            found_rest = jnp.where(here, both[tall + at * 8:tall + at * 8 + 8], found_rest)
        here = line_index == jnp.bitwise_and(slots, 7)
        line = jnp.sum(jnp.where(here, found + found_rest, 0.0), axis=0, keepdims=True)
        for piece in range(chunk // 128):
            taken[part, piece:piece + 1, :] = line[:, piece * 128:(piece + 1) * 128]

    source_a, target_a = lambda peer: rows_of(base_ref, peer), lambda slot: arrived.at[slot]
    source_b, target_b = lambda peer: selfen.at[peer], lambda slot: rows_of(spread_ref, slot)
    filled = chunk // 128
    source_c, target_c = lambda peer: taken.at[peer, :filled], lambda slot: taken_ref.at[slot, :filled]

    def take_pair(pair, carry):
        take(peer_of(me, count - 1 - 2 * pair))
        take(peer_of(me, count - 2 - 2 * pair))
        return carry

    def send_pair(pair, carry):
        for offset in (count - 1 - 2 * pair, count - 2 - 2 * pair):
            block_copy(me, offset, source_c, target_c, me, send_c, recv_c).start()
        return carry

    def take_and_send(pair, carry):
        take_pair(pair, carry)
        return send_pair(pair, carry)

    lax.fori_loop(0, PAIRS_FIRST, take_pair, 0)
    pl.semaphore_wait(barrier, count - 1)
    send_blocks(count, me, source_a, target_a, send_a, recv_a)
    lax.fori_loop(0, PAIRS_FIRST, send_pair, 0)
    lax.fori_loop(PAIRS_FIRST, PAIRS_FIRST + PAIRS_SECOND, take_and_send, 0)
    await_blocks(count, me, source_a, target_a, send_a, recv_a)

    scale = polar_coef * width / count
    for side in range(width // 128):
        cols = slice(side * 128, (side + 1) * 128)
        samples = [arrived[e, :, cols] for e in range(count)]
        screened = screen(samples, bare_pos_ref[:, cols], scale)
        for e in range(count):
            total = samples[e] * screened[0]
            for n in range(1, e + 1):
                total = total + samples[e - n] * screened[n]
            selfen[e, :, cols] = total * (sigma_coef / count)
    send_blocks(count, me, source_b, target_b, send_b, recv_b)
    lax.fori_loop(PAIRS_FIRST + PAIRS_SECOND, pairs - 1, take_and_send, 0)
    take_pair(pairs - 1, 0)
    block_copy(me, 1, source_c, target_c, me, send_c, recv_c).start()
    taken_ref[me, :filled] = taken[me, :filled]
    spread_ref[pl.ds(pl.multiple_of(me * 8, 8), 8), :] = selfen[me]
    await_blocks(count, me, source_b, target_b, send_b, recv_b)
    await_blocks(count, me, source_c, target_c, send_c, recv_c)


def finish_kernel(reduced_ref, base_ref, spread_ref, taken_ref, bare_ref, green_ref, screened_ref, x_ref):
    count = taken_ref.shape[0]
    width = base_ref.shape[0]
    chunk = screened_ref.shape[2]
    spread = spread_ref[...]
    matrix = reduced_ref[...] - 0.5 * (spread + spread.T)
    x_ref[...] = base_ref[...]
    settle([matrix], [x_ref])
    green_ref[0, 0] = x_ref[...]
    scale = polar_coef * width / count
    for group in range(taken_ref.shape[1] // 8):
        lines = slice(group * 8, group * 8 + 8)
        samples = [taken_ref[e, lines, :] for e in range(count)]
        screened = screen(samples, bare_ref[lines, :], scale)
        for line in range(group * 8, min(group * 8 + 8, pl.cdiv(chunk, 128))):
            start = line * 128
            stop = min(start + 128, chunk)
            for n in range(count):
                at = line - group * 8
                screened_ref[n, :, start:stop] = screened[n][at:at + 1, :stop - start]


def on_device(count, spaces, ham_diag, ham_coup, energies, pattern, coulomb):
    width = ham_diag.shape[1]
    span = coulomb.shape[1]
    chunk = pl.cdiv(span, 128) * 128
    lines = pl.cdiv(chunk // 128, 8) * 8
    vmem = pl.BlockSpec(memory_space=pltpu.VMEM)
    smem = pl.BlockSpec(memory_space=pltpu.SMEM)
    square = jax.ShapeDtypeStruct((width, width), F32)
    diags, coups, rows, slots, bare_pos, bare_own = pl.pallas_call(
        functools.partial(collect_kernel, count, spaces),
        out_shape=(
            jax.ShapeDtypeStruct((spaces, width, width), F32),
            jax.ShapeDtypeStruct((spaces, width, width), F32),
            jax.ShapeDtypeStruct((count, 1, chunk), jnp.int32),
            jax.ShapeDtypeStruct((count, 1, chunk), jnp.int32),
            jax.ShapeDtypeStruct((8, width), F32),
            jax.ShapeDtypeStruct((lines, 128), F32),
        ),
        in_specs=[pl.BlockSpec(memory_space=pltpu.HBM)] * 4,
        out_specs=(vmem,) * 6,
        scratch_shapes=[
            VMEM((1, pattern.shape[1]), jnp.int32), VMEM((1, span), F32),
            VMEM((count, 1, chunk), jnp.int32), VMEM((1, chunk), F32),
            VMEM((2, 4, 4, 8, width), F32), VMEM((4, 4, 8, width), F32), VMEM((4, 4, 8, width), F32),
            VMEM((4, 4, 8, width), F32), VMEM((4, 8, width), F32), VMEM((4, 8, width), F32),
            DMA((4,)), DMA((2, 3)), DMA((2, 3)), DMA((2, 3)), DMA((2, 3)),
            DMA((2,)), DMA((4,)), DMA((4,)), DMA((4,)), DMA((4,)),
        ],
        compiler_params=pltpu.CompilerParams(collective_id=0, has_side_effects=True, vmem_limit_bytes=VMEM_LIMIT),
        name="collect",
    )(*(pltpu.with_memory_space_constraint(value, pltpu.HBM) for value in (ham_diag, ham_coup, pattern, coulomb)))

    reduced, base = pl.pallas_call(
        chain_kernel,
        out_shape=(square, square),
        in_specs=[smem, vmem, vmem],
        out_specs=(vmem, vmem),
        scratch_shapes=[VMEM((width, width), F32)] * 9,
        compiler_params=pltpu.CompilerParams(vmem_limit_bytes=VMEM_LIMIT),
        name="chain",
    )(energies, diags, coups)

    spread, taken = pl.pallas_call(
        functools.partial(regroup_kernel, count),
        out_shape=(square, jax.ShapeDtypeStruct((count, lines, 128), F32)),
        in_specs=[vmem] * 4,
        out_specs=(vmem, vmem),
        scratch_shapes=[
            VMEM((width + 16, width), BF16), VMEM((count, 8, width), F32),
            VMEM((count, 8, width), F32), VMEM((count, lines, 128), F32),
        ] + [DMA((count,))] * 6,
        compiler_params=pltpu.CompilerParams(collective_id=1, has_side_effects=True, vmem_limit_bytes=VMEM_LIMIT),
        name="regroup",
    )(base, rows, slots, bare_pos)

    return pl.pallas_call(
        finish_kernel,
        out_shape=(
            jax.ShapeDtypeStruct((1, 1, width, width), F32),
            jax.ShapeDtypeStruct((count, 1, span), F32),
        ),
        in_specs=[vmem] * 5,
        out_specs=(vmem, vmem),
        scratch_shapes=[VMEM((width, width), F32)],
        compiler_params=pltpu.CompilerParams(vmem_limit_bytes=VMEM_LIMIT),
        name="finish",
    )(reduced, base, spread, taken, bare_own)


def solution(mesh):
    count, spaces = mesh.shape["energy"], mesh.shape["space"]
    return jax.shard_map(
        functools.partial(on_device, count, spaces),
        mesh=mesh,
        in_specs=(
            P("space", None, None),
            P("space", None, None),
            P("energy"),
            P("space", None),
            P("space", "energy"),
        ),
        out_specs=(P("energy", "space", None, None), P(None, "space", "energy")),
        check_vma=False,
    )
```

```python
import functools

import jax
import jax.numpy as jnp
from jax import lax
from jax.experimental import pallas as pl
from jax.experimental.pallas import tpu as pltpu
from jax.sharding import PartitionSpec as P

F32, BF16 = jnp.float32, jnp.bfloat16
MESH = pl.DeviceIdType.MESH
VMEM = pltpu.VMEM
DMA = pltpu.SemaphoreType.DMA

polar_coef = 128.0
sigma_coef = 0.5

TOLERANCE = 1e-5
VMEM_LIMIT = 20 << 20


def split(value):
    high = value.astype(BF16)
    return high, (value - high.astype(F32)).astype(BF16)


def dot(a, b):
    return jnp.dot(a, b, preferred_element_type=F32)


def dot_nt(a, b):
    return lax.dot_general(a, b, (((1,), (1,)), ((), ())), preferred_element_type=F32)


def mul(a, b):
    return dot(a[0], b[0]) + (dot(a[0], b[1]) + dot(a[1], b[0]))


def product(a, b):
    return mul(split(a), split(b))


def identity(width):
    rows = lax.broadcasted_iota(jnp.int32, (width, width), 0)
    cols = lax.broadcasted_iota(jnp.int32, (width, width), 1)
    return jnp.where(rows == cols, 1.0, 0.0).astype(F32)


def series(matrix, alpha, doublings):
    ident = identity(matrix.shape[0])
    parts = split(matrix)
    power = ident - matrix * (2.0 * alpha) + mul(parts, parts) * (alpha * alpha)
    guess = alpha * (2.0 * ident - matrix * alpha)
    guess = guess + product(guess, power)
    for _ in range(doublings - 1):
        high = power.astype(BF16)
        power = dot(high, high)
        guess = guess + dot(guess.astype(BF16), power.astype(BF16))
    return guess


def total_of(value):
    return jnp.sum(jnp.sum(value, axis=0, keepdims=True), axis=1, keepdims=True)


def mean_scale(matrix):
    trace = total_of(jnp.where(identity(matrix.shape[0]) > 0.0, matrix, 0.0))
    return trace / total_of(matrix * matrix)


def safe_scale(matrix):
    return 1.9 / jnp.max(jnp.sum(jnp.abs(matrix), axis=0, keepdims=True), axis=1, keepdims=True)


def eliminate(matrix, out_ref):
    width = matrix.shape[0]
    out_ref[...] = matrix
    lanes = lax.broadcasted_iota(jnp.int32, (1, width), 1)

    def step(pivot, carry):
        whole = out_ref[...]
        row = out_ref[pl.ds(pivot, 1), :]
        here = lanes == pivot
        value = jnp.sum(jnp.where(here, row, 0.0), axis=1, keepdims=True)
        column = jnp.sum(jnp.where(here, whole, 0.0), axis=1, keepdims=True)
        scaled = jnp.where(here, 1.0, row) / value
        out_ref[...] = jnp.where(here, 0.0, whole) - column * scaled
        out_ref[pl.ds(pivot, 1), :] = scaled
        return carry

    lax.fori_loop(0, width, step, 0)


def newton(matrices, refs, limit):
    ident = identity(matrices[0].shape[0])
    parts = [split(matrix) for matrix in matrices]

    def unsettled(carry):
        steps, worst = carry
        return jnp.logical_and(worst > TOLERANCE, steps < limit)

    def step(carry):
        worst = jnp.float32(0.0)
        for own, ref in zip(parts, refs):
            guess = ref[...]
            guess_parts = split(guess)
            residual = ident - mul(own, guess_parts)
            ref[...] = guess + dot(guess_parts[0], residual.astype(BF16))
            worst = jnp.maximum(worst, jnp.sum(residual * residual))
        return carry[0] + 1, worst

    return lax.while_loop(unsettled, step, (jnp.int32(0), jnp.float32(1.0)))[1]


def settle(matrices, refs):
    worst = newton(matrices, refs, 8)

    @pl.when(jnp.logical_not(worst <= TOLERANCE))
    def _():
        for matrix, ref in zip(matrices, refs):
            ref[...] = series(matrix, safe_scale(matrix), 5)
        again = newton(matrices, refs, 48)

        @pl.when(jnp.logical_not(again <= TOLERANCE))
        def _():
            for matrix, ref in zip(matrices, refs):
                eliminate(matrix, ref)


def invert(matrices, refs):
    for matrix, ref in zip(matrices, refs):
        ref[...] = series(matrix, mean_scale(matrix), 3)
    settle(matrices, refs)


def peer_of(me, offset):
    core = lax.rem(me + offset, 2)
    y = lax.rem(me // 2 + offset // 2, 4)
    z = lax.rem(me // 8 + offset // 8, 4)
    return z * 8 + y * 2 + core


def peers_of(count, me):
    cores = [lax.rem(me + step, 2) for step in range(2)]
    ys = [lax.rem(me // 2 + step, 4) * 2 for step in range(4)]
    zs = [lax.rem(me // 8 + step, 4) * 8 for step in range(4)]
    return [zs[offset // 8] + ys[offset // 2 % 4] + cores[offset % 2] for offset in range(count - 1, 0, -1)]


def to_peer(peer, source, target, sems):
    return pltpu.make_async_remote_copy(
        src_ref=source, dst_ref=target, send_sem=sems.at[0], recv_sem=sems.at[1],
        device_id={"energy": peer}, device_id_type=MESH,
    )


def rows_of(ref, peer):
    return ref.at[pl.ds(pl.multiple_of(peer * 8, 8), 8), :]


def collect_kernel(
    count, spaces, diag_ref, coup_ref, pattern_ref, bare_ref,
    diags_ref, coups_ref, rows_ref, slots_ref, bare_pos_ref, bare_own_ref,
    pattern, bare_in, own_pattern, own_bare, scattered, from_core, by_y, from_y, by_z, from_z,
    own_sem, far_send, far_recv, near_send, near_recv, core_sems, y_send, y_recv, z_send, z_recv,
):
    me = lax.axis_index("energy")
    place = lax.axis_index("space")
    width = diag_ref.shape[1]
    half = width // 2
    core = lax.rem(me, 2)
    other = me + 1 - 2 * core
    own_y = lax.rem(me // 2, 4)
    own_z = me // 8
    span = bare_ref.shape[1]
    chunk = own_bare.shape[1]
    sides = (lax.rem(place + 1, spaces), lax.rem(place + spaces - 1, spaces))
    across = lax.rem(place + 2, spaces)

    own_copies = [
        pltpu.make_async_copy(pattern_ref, pattern, own_sem.at[0]),
        pltpu.make_async_copy(bare_ref, bare_in, own_sem.at[1]),
        pltpu.make_async_copy(diag_ref.at[0], diags_ref.at[place], own_sem.at[2]),
        pltpu.make_async_copy(coup_ref.at[0], coups_ref.at[place], own_sem.at[3]),
    ]
    for copy in own_copies:
        copy.start()

    barrier = pltpu.get_barrier_semaphore()
    for side in sides:
        pl.semaphore_signal(barrier, inc=1, device_id={"space": side}, device_id_type=MESH)
    for step in (2, 1, 3):
        for stride in (2, 8):
            pl.semaphore_signal(
                barrier, inc=1, device_id={"energy": peer_of(me, step * stride)}, device_id_type=MESH)
    pl.semaphore_signal(barrier, inc=1, device_id={"energy": other}, device_id_type=MESH)

    own_copies[0].wait()
    own_copies[1].wait()
    tail = chunk - 128
    for part in range(count):
        size = chunk if part < count - 1 else span
        if size < chunk:
            own_pattern[part, :, tail:] = jnp.zeros((1, 128), jnp.int32)
            rows_ref[part, :, tail:] = jnp.zeros((1, 128), jnp.int32)
            slots_ref[part, :, tail:] = jnp.zeros((1, 128), jnp.int32)
        piece = pattern[:, part * span:part * span + size]
        own_pattern[part, :, :size] = piece
        row = lax.shift_right_logical(piece, 8)
        col = jnp.bitwise_and(piece, 255)
        high = jnp.maximum(row, col)
        low = jnp.minimum(row, col)
        lower = low >= 128
        pivot = high == low
        rows_ref[part, :, :size] = jnp.where(jnp.logical_and(lower, jnp.logical_not(pivot)), low - 128, high)
        slots_ref[part, :, :size] = jnp.where(lower, jnp.where(pivot, 128, high - 128), low)
    own_bare[:, tail:] = jnp.zeros((1, 128), F32)
    own_bare[:, :span] = bare_in[...]

    pl.semaphore_wait(barrier, 9)
    own_half = pl.ds(pl.multiple_of(core * half, half), half)
    other_half = pl.ds(pl.multiple_of((1 - core) * half, half), half)
    given = (diag_ref, coup_ref)
    stores = (diags_ref, coups_ref)

    def far(way, stage):
        kind = (way, 1 - way, way)[stage]
        block = place if stage < 2 else sides[1 - way]
        source = given[kind].at[0, own_half] if stage < 2 else stores[kind].at[block, own_half]
        return pltpu.make_async_remote_copy(
            src_ref=source, dst_ref=stores[kind].at[block, own_half],
            send_sem=far_send.at[way, stage], recv_sem=far_recv.at[way, stage],
            device_id={"space": sides[way]}, device_id_type=MESH)

    def near(way, stage, part):
        kind = (way, 1 - way, way)[stage]
        block = sides[1 - way] if stage < 2 else across
        piece = stores[kind].at[block, part]
        return pltpu.make_async_remote_copy(
            src_ref=piece, dst_ref=piece,
            send_sem=near_send.at[way, stage], recv_sem=near_recv.at[way, stage],
            device_id={"energy": other}, device_id_type=MESH)

    for stage in range(2):
        for way in range(2):
            far(way, stage).start()

    mine = own_pattern[me]
    bare = own_bare[...]
    index = lax.broadcasted_iota(jnp.int32, (width, chunk), 0)
    on_row = index == lax.shift_right_logical(mine, 8)
    on_col = jnp.where(index == jnp.bitwise_and(mine, 255), 1.0, 0.0).astype(BF16)
    rest = bare
    total = None
    for _ in range(3):
        part = rest.astype(BF16).astype(F32)
        rest = rest - part
        term = dot_nt(jnp.where(on_row, part, 0.0).astype(BF16), on_col)
        total = term if total is None else total + term
    for peer in range(count):
        scattered[peer % 2, peer // 2 % 4, peer // 8] = total[peer * 8:peer * 8 + 8, :]
    for line in range(chunk // 128):
        bare_own_ref[line:line + 1, :] = bare[:, line * 128:(line + 1) * 128]
    for line in range(chunk // 128, bare_own_ref.shape[0]):
        bare_own_ref[line:line + 1, :] = jnp.zeros((1, 128), F32)

    to_core = pltpu.make_async_remote_copy(
        src_ref=scattered.at[1 - core], dst_ref=from_core,
        send_sem=core_sems.at[0], recv_sem=core_sems.at[1],
        device_id={"energy": other}, device_id_type=MESH)

    def to_y(step):
        return pltpu.make_async_remote_copy(
            src_ref=by_y.at[lax.rem(own_y + step, 4)], dst_ref=from_y.at[step],
            send_sem=y_send.at[step], recv_sem=y_recv.at[step],
            device_id={"energy": peer_of(me, 2 * step)}, device_id_type=MESH)

    def to_z(step):
        return pltpu.make_async_remote_copy(
            src_ref=by_z.at[lax.rem(own_z + step, 4)], dst_ref=from_z.at[step],
            send_sem=z_send.at[step], recv_sem=z_recv.at[step],
            device_id={"energy": peer_of(me, 8 * step)}, device_id_type=MESH)

    to_core.start()
    for way in range(2):
        far(way, 0).wait_recv()
        far(way, 2).start()
        near(way, 0, own_half).start()
    to_core.wait()
    for y in range(4):
        for z in range(4):
            by_y[y, z] = scattered[core, y, z] + from_core[y, z]
    for step in (2, 1, 3):
        to_y(step).start()
    for step in (1, 3, 2):
        to_y(step).wait()
    for z in range(4):
        by_z[z] = (by_y[own_y, z] + from_y[1, z]) + (from_y[2, z] + from_y[3, z])
    for step in (2, 1, 3):
        to_z(step).start()
    for stage in (1, 2):
        for way in range(2):
            far(way, stage).wait_recv()
            near(way, stage, own_half).start()
    for step in (1, 3, 2):
        to_z(step).wait()
    bare_pos_ref[...] = (by_z[own_z] + from_z[1]) + (from_z[2] + from_z[3])
    for copy in own_copies[2:]:
        copy.wait()
    for stage in range(3):
        for way in range(2):
            far(way, stage).wait_send()
            near(way, stage, own_half).wait_send()
            near(way, stage, other_half).wait_recv()


def chain_kernel(
    shift_ref, diags_ref, coups_ref, reduced_ref, base_ref,
    v_ref, vt_ref, w_ref, wt_ref, c_ref, ct_ref, last_ref, x_ref, y_ref,
):
    place = lax.axis_index("space")
    width = base_ref.shape[0]
    shift = identity(width) * shift_ref[0]
    lead_parts = split(coups_ref[3])
    quarter = (
        dot_nt(lead_parts[0], lead_parts[0])
        + (dot_nt(lead_parts[0], lead_parts[1]) + dot_nt(lead_parts[1], lead_parts[0]))
    ) * 0.25
    last_ref[...] = diags_ref[3] - quarter
    lower = place <= 1

    def system(block):
        return jnp.where(block == 3, last_ref[...], diags_ref[block]) + shift

    def choose(block, flipped, ref, turned_ref):
        value = coups_ref[block]
        turned = value.T
        ref[...] = jnp.where(flipped, turned, value)
        turned_ref[...] = jnp.where(flipped, value, turned)

    first = jnp.where(place == 0, 1, jnp.where(place == 1, 0, jnp.where(place == 2, 3, 2)))
    second = jnp.where(lower, 3, 0)
    middle = jnp.where(lower, 2, 1)
    choose(1, jnp.logical_not(lower), c_ref, ct_ref)
    choose(jnp.where(lower, 2, 0), lower, v_ref, vt_ref)
    choose(jnp.where(lower, 0, 2), lax.rem(place, 2) == 0, w_ref, wt_ref)

    invert([system(first), system(second)], [x_ref, y_ref])
    x = split(x_ref[...])
    y = split(y_ref[...])
    wt_s = split(wt_ref[...])
    xw = split(mul(x, split(w_ref[...])))
    yv = split(mul(y, split(v_ref[...])))
    reduced_ref[...] = system(place) - mul(wt_s, xw)
    last_ref[...] = system(middle) - mul(split(vt_ref[...]), yv)

    @pl.when(jnp.logical_or(place == 0, place == 3))
    def _():
        xu = split(mul(x, split(c_ref[...])))
        ut_s = split(ct_ref[...])
        last_ref[...] = last_ref[...] - mul(ut_s, xu)
        c_ref[...] = mul(wt_s, xu)
        ct_ref[...] = mul(ut_s, xw)

    invert([last_ref[...]], [x_ref])
    cz = split(product(c_ref[...], x_ref[...]))
    reduced = reduced_ref[...] - mul(cz, split(ct_ref[...]))
    reduced_ref[...] = reduced
    invert([reduced], [base_ref])


def screen(samples, bare, scale):
    count = len(samples)
    result = []
    for lag in range(count):
        total = samples[0] * samples[lag]
        for m in range(1, count - lag):
            total = total + samples[m] * samples[m + lag]
        scaled = bare * (total * scale)
        result.append(bare * lax.rsqrt(1.0 + scaled * scaled))
    return result


PAIRS_FIRST = 2
PAIRS_SECOND = 9


def regroup_kernel(
    count, base_ref, rows_ref, slots_ref, bare_pos_ref, spread_ref, taken_ref,
    lhs, arrived, selfen, taken, sems_a, sems_b, sems_c,
):
    me = lax.axis_index("energy")
    width = base_ref.shape[0]
    half = width // 2
    chunk = rows_ref.shape[2]
    lines = taken.shape[1]
    pairs = count // 2
    for peer in range(count):
        taken_ref[peer, chunk // 128:, :] = jnp.zeros((lines - chunk // 128, 128), F32)

    barrier = pltpu.get_barrier_semaphore()

    others = peers_of(count, me)
    for peer in others:
        pl.semaphore_signal(barrier, inc=1, device_id={"energy": peer}, device_id_type=MESH)
    arrived[me] = rows_of(base_ref, me)[...]

    upper = base_ref[:half, :half]
    lower = base_ref[half:, half:]
    r = lax.broadcasted_iota(jnp.int32, (half, half), 0)
    c = lax.broadcasted_iota(jnp.int32, (half, half), 1)
    table = jnp.concatenate([jnp.where(r <= c, upper, lower), base_ref[:half, half:]], axis=1)
    diagonal = jnp.sum(jnp.where(r == c, lower, 0.0), axis=0, keepdims=True)
    extra = jnp.concatenate([jnp.zeros((1, half), F32), diagonal], axis=1)
    first = lax.broadcasted_iota(jnp.int32, (8, width), 0) == 0
    table = jnp.concatenate([table, jnp.where(first, extra, 0.0)], axis=0)
    tall = table.shape[0]
    high = table.astype(BF16).astype(F32)
    lhs[...] = jnp.concatenate([high, table - high], axis=0).astype(BF16)
    row_index = lax.broadcasted_iota(jnp.int32, (width, chunk), 0).astype(F32).astype(BF16)
    line_index = lax.broadcasted_iota(jnp.int32, (8, chunk), 0)
    one, none = jnp.bfloat16(1), jnp.bfloat16(0)

    def take(part):
        hot = jnp.where(row_index == rows_ref[part].astype(F32).astype(BF16), one, none)
        both = dot(lhs[...], hot)
        slots = slots_ref[part]
        group = jnp.broadcast_to(lax.shift_right_logical(slots, 3), (8, chunk))
        found, found_rest = both[:8], both[tall:tall + 8]
        for at in range(1, tall // 8):
            here = group == at
            found = jnp.where(here, both[at * 8:at * 8 + 8], found)
            found_rest = jnp.where(here, both[tall + at * 8:tall + at * 8 + 8], found_rest)
        here = line_index == jnp.bitwise_and(slots, 7)
        line = jnp.sum(jnp.where(here, found + found_rest, 0.0), axis=0, keepdims=True)
        for piece in range(chunk // 128):
            taken[part, piece:piece + 1, :] = line[:, piece * 128:(piece + 1) * 128]

    filled = chunk // 128

    def all_but_one(source, target, sems):
        return to_peer(others[0], source, target, sems)

    def take_pair(pair, carry):
        take(peer_of(me, count - 1 - 2 * pair))
        take(peer_of(me, count - 2 - 2 * pair))
        return carry

    def send_taken(peer):
        to_peer(peer, taken.at[peer, :filled], taken_ref.at[me, :filled], sems_c).start()

    def send_pair(pair, carry):
        for offset in (count - 1 - 2 * pair, count - 2 - 2 * pair):
            send_taken(peer_of(me, offset))
        return carry

    def take_and_send(pair, carry):
        take_pair(pair, carry)
        return send_pair(pair, carry)

    lax.fori_loop(0, PAIRS_FIRST, take_pair, 0)
    pl.semaphore_wait(barrier, count - 1)
    for peer in others:
        to_peer(peer, rows_of(base_ref, peer), arrived.at[me], sems_a).start()
    lax.fori_loop(0, PAIRS_FIRST, send_pair, 0)
    lax.fori_loop(PAIRS_FIRST, PAIRS_FIRST + PAIRS_SECOND, take_and_send, 0)
    rest = pl.ds(8, width - 8)
    first_exchange = all_but_one(base_ref.at[rest, :], arrived.at[pl.ds(1, count - 1)], sems_a)
    first_exchange.wait_send()
    first_exchange.wait_recv()

    scale = polar_coef * width / count
    for side in range(width // 128):
        cols = slice(side * 128, (side + 1) * 128)
        samples = [arrived[e, :, cols] for e in range(count)]
        screened = screen(samples, bare_pos_ref[:, cols], scale)
        for e in range(count):
            total = samples[e] * screened[0]
            for n in range(1, e + 1):
                total = total + samples[e - n] * screened[n]
            selfen[e, :, cols] = total * (sigma_coef / count)
    for peer in others:
        to_peer(peer, selfen.at[peer], rows_of(spread_ref, me), sems_b).start()
    lax.fori_loop(PAIRS_FIRST + PAIRS_SECOND, pairs - 1, take_and_send, 0)
    take_pair(pairs - 1, 0)
    send_taken(peer_of(me, 1))
    taken_ref[me, :filled] = taken[me, :filled]
    spread_ref[pl.ds(pl.multiple_of(me * 8, 8), 8), :] = selfen[me]
    for last_exchange in (
        all_but_one(selfen.at[pl.ds(1, count - 1)], spread_ref.at[rest, :], sems_b),
        all_but_one(taken.at[pl.ds(1, count - 1), :filled], taken_ref.at[pl.ds(1, count - 1), :filled], sems_c),
    ):
        last_exchange.wait_send()
        last_exchange.wait_recv()


def finish_kernel(reduced_ref, base_ref, spread_ref, taken_ref, bare_ref, green_ref, screened_ref, x_ref):
    count = taken_ref.shape[0]
    width = base_ref.shape[0]
    chunk = screened_ref.shape[2]
    spread = spread_ref[...]
    matrix = reduced_ref[...] - 0.5 * (spread + spread.T)
    x_ref[...] = base_ref[...]
    settle([matrix], [x_ref])
    green_ref[0, 0] = x_ref[...]
    scale = polar_coef * width / count
    for group in range(taken_ref.shape[1] // 8):
        lines = slice(group * 8, group * 8 + 8)
        samples = [taken_ref[e, lines, :] for e in range(count)]
        screened = screen(samples, bare_ref[lines, :], scale)
        for line in range(group * 8, min(group * 8 + 8, pl.cdiv(chunk, 128))):
            start = line * 128
            stop = min(start + 128, chunk)
            for n in range(count):
                at = line - group * 8
                screened_ref[n, :, start:stop] = screened[n][at:at + 1, :stop - start]


def on_device(count, spaces, ham_diag, ham_coup, energies, pattern, coulomb):
    width = ham_diag.shape[1]
    span = coulomb.shape[1]
    chunk = pl.cdiv(span, 128) * 128
    lines = pl.cdiv(chunk // 128, 8) * 8
    vmem = pl.BlockSpec(memory_space=pltpu.VMEM)
    smem = pl.BlockSpec(memory_space=pltpu.SMEM)
    square = jax.ShapeDtypeStruct((width, width), F32)
    diags, coups, rows, slots, bare_pos, bare_own = pl.pallas_call(
        functools.partial(collect_kernel, count, spaces),
        out_shape=(
            jax.ShapeDtypeStruct((spaces, width, width), F32),
            jax.ShapeDtypeStruct((spaces, width, width), F32),
            jax.ShapeDtypeStruct((count, 1, chunk), jnp.int32),
            jax.ShapeDtypeStruct((count, 1, chunk), jnp.int32),
            jax.ShapeDtypeStruct((8, width), F32),
            jax.ShapeDtypeStruct((lines, 128), F32),
        ),
        in_specs=[pl.BlockSpec(memory_space=pltpu.HBM)] * 4,
        out_specs=(vmem,) * 6,
        scratch_shapes=[
            VMEM((1, pattern.shape[1]), jnp.int32), VMEM((1, span), F32),
            VMEM((count, 1, chunk), jnp.int32), VMEM((1, chunk), F32),
            VMEM((2, 4, 4, 8, width), F32), VMEM((4, 4, 8, width), F32), VMEM((4, 4, 8, width), F32),
            VMEM((4, 4, 8, width), F32), VMEM((4, 8, width), F32), VMEM((4, 8, width), F32),
            DMA((4,)), DMA((2, 3)), DMA((2, 3)), DMA((2, 3)), DMA((2, 3)),
            DMA((2,)), DMA((4,)), DMA((4,)), DMA((4,)), DMA((4,)),
        ],
        compiler_params=pltpu.CompilerParams(collective_id=0, has_side_effects=True, vmem_limit_bytes=VMEM_LIMIT),
        name="collect",
    )(*(pltpu.with_memory_space_constraint(value, pltpu.HBM) for value in (ham_diag, ham_coup, pattern, coulomb)))

    reduced, base = pl.pallas_call(
        chain_kernel,
        out_shape=(square, square),
        in_specs=[smem, vmem, vmem],
        out_specs=(vmem, vmem),
        scratch_shapes=[VMEM((width, width), F32)] * 9,
        compiler_params=pltpu.CompilerParams(vmem_limit_bytes=VMEM_LIMIT),
        name="chain",
    )(energies, diags, coups)

    spread, taken = pl.pallas_call(
        functools.partial(regroup_kernel, count),
        out_shape=(square, jax.ShapeDtypeStruct((count, lines, 128), F32)),
        in_specs=[vmem] * 4,
        out_specs=(vmem, vmem),
        scratch_shapes=[
            VMEM((width + 16, width), BF16), VMEM((count, 8, width), F32),
            VMEM((count, 8, width), F32), VMEM((count, lines, 128), F32),
        ] + [DMA((2,))] * 3,
        compiler_params=pltpu.CompilerParams(collective_id=1, has_side_effects=True, vmem_limit_bytes=VMEM_LIMIT),
        name="regroup",
    )(base, rows, slots, bare_pos)

    return pl.pallas_call(
        finish_kernel,
        out_shape=(
            jax.ShapeDtypeStruct((1, 1, width, width), F32),
            jax.ShapeDtypeStruct((count, 1, span), F32),
        ),
        in_specs=[vmem] * 5,
        out_specs=(vmem, vmem),
        scratch_shapes=[VMEM((width, width), F32)],
        compiler_params=pltpu.CompilerParams(vmem_limit_bytes=VMEM_LIMIT),
        name="finish",
    )(reduced, base, spread, taken, bare_own)


def solution(mesh):
    count, spaces = mesh.shape["energy"], mesh.shape["space"]
    return jax.shard_map(
        functools.partial(on_device, count, spaces),
        mesh=mesh,
        in_specs=(
            P("space", None, None),
            P("space", None, None),
            P("energy"),
            P("space", None),
            P("space", "energy"),
        ),
        out_specs=(P("energy", "space", None, None), P(None, "space", "energy")),
        check_vma=False,
    )
```

```python
import functools

import jax
import jax.numpy as jnp
from jax import lax
from jax.experimental import pallas as pl
from jax.experimental.pallas import tpu as pltpu
from jax.sharding import PartitionSpec as P

F32, BF16 = jnp.float32, jnp.bfloat16
MESH = pl.DeviceIdType.MESH
VMEM = pltpu.VMEM
DMA = pltpu.SemaphoreType.DMA

polar_coef = 128.0
sigma_coef = 0.5

TOLERANCE = 2e-5
VMEM_LIMIT = 20 << 20


def split(value):
    high = value.astype(BF16)
    return high, (value - high.astype(F32)).astype(BF16)


def dot(a, b):
    return jnp.dot(a, b, preferred_element_type=F32)


def dot_nt(a, b):
    return lax.dot_general(a, b, (((1,), (1,)), ((), ())), preferred_element_type=F32)


def mul(a, b):
    return dot(a[0], b[0]) + (dot(a[0], b[1]) + dot(a[1], b[0]))


def product(a, b):
    return mul(split(a), split(b))


def identity(width):
    rows = lax.broadcasted_iota(jnp.int32, (width, width), 0)
    cols = lax.broadcasted_iota(jnp.int32, (width, width), 1)
    return jnp.where(rows == cols, 1.0, 0.0).astype(F32)


def series(matrices, scales, doublings):
    ident = identity(matrices[0].shape[0])
    parts = [split(matrix) for matrix in matrices]
    squares = [mul(own, own) for own in parts]
    powers = [
        ident - matrix * (2.0 * scale) + square * (scale * scale)
        for matrix, scale, square in zip(matrices, scales, squares)
    ]
    guesses = [scale * (2.0 * ident - matrix * scale) for matrix, scale in zip(matrices, scales)]
    guesses = [guess + product(guess, power) for guess, power in zip(guesses, powers)]
    for _ in range(doublings - 1):
        highs = [power.astype(BF16) for power in powers]
        powers = [dot(high, high) for high in highs]
        guesses = [
            guess + dot(guess.astype(BF16), power.astype(BF16)) for guess, power in zip(guesses, powers)
        ]
    return guesses


def total_of(value):
    return jnp.sum(jnp.sum(value, axis=0, keepdims=True), axis=1, keepdims=True)


def mean_scale(matrix):
    trace = total_of(jnp.where(identity(matrix.shape[0]) > 0.0, matrix, 0.0))
    return trace / total_of(matrix * matrix)


def safe_scale(matrix):
    return 1.9 / jnp.max(jnp.sum(jnp.abs(matrix), axis=0, keepdims=True), axis=1, keepdims=True)


def eliminate(matrix, out_ref):
    width = matrix.shape[0]
    out_ref[...] = matrix
    lanes = lax.broadcasted_iota(jnp.int32, (1, width), 1)

    def step(pivot, carry):
        whole = out_ref[...]
        row = out_ref[pl.ds(pivot, 1), :]
        here = lanes == pivot
        value = jnp.sum(jnp.where(here, row, 0.0), axis=1, keepdims=True)
        column = jnp.sum(jnp.where(here, whole, 0.0), axis=1, keepdims=True)
        scaled = jnp.where(here, 1.0, row) / value
        out_ref[...] = jnp.where(here, 0.0, whole) - column * scaled
        out_ref[pl.ds(pivot, 1), :] = scaled
        return carry

    lax.fori_loop(0, width, step, 0)


def newton_step(parts, guesses):
    ident = identity(guesses[0].shape[0])
    split_guesses = [split(guess) for guess in guesses]
    residuals = [ident - mul(own, guess) for own, guess in zip(parts, split_guesses)]
    better = [
        guess + dot(guess_parts[0], residual.astype(BF16))
        for guess, guess_parts, residual in zip(guesses, split_guesses, residuals)
    ]
    return better, [residual * residual for residual in residuals]


def newton(matrices, refs, limit, worst=1.0):
    parts = [split(matrix) for matrix in matrices]

    def unsettled(carry):
        steps, last = carry
        return jnp.logical_and(last > TOLERANCE, steps < limit)

    def step(carry):
        better, squares = newton_step(parts, [ref[...] for ref in refs])
        largest = jnp.float32(0.0)
        for ref, value, square in zip(refs, better, squares):
            ref[...] = value
            largest = jnp.maximum(largest, jnp.sum(square))
        return carry[0] + 1, largest

    return lax.while_loop(unsettled, step, (jnp.int32(0), jnp.asarray(worst, F32)))[1]


def settle(matrices, refs, worst=1.0):
    worst = newton(matrices, refs, 8, worst)

    @pl.when(jnp.logical_not(worst <= TOLERANCE))
    def _():
        for matrix, ref in zip(matrices, refs):
            ref[...] = series([matrix], [safe_scale(matrix)], 5)[0]
        again = newton(matrices, refs, 48)

        @pl.when(jnp.logical_not(again <= TOLERANCE))
        def _():
            for matrix, ref in zip(matrices, refs):
                eliminate(matrix, ref)


def quick(matrices):
    guesses = series(matrices, [mean_scale(matrix) for matrix in matrices], 3)
    return newton_step([split(matrix) for matrix in matrices], guesses)


def peer_of(me, offset):
    core = lax.rem(me + offset, 2)
    y = lax.rem(me // 2 + offset // 2, 4)
    z = lax.rem(me // 8 + offset // 8, 4)
    return z * 8 + y * 2 + core


def peers_of(count, me):
    cores = [lax.rem(me + step, 2) for step in range(2)]
    ys = [lax.rem(me // 2 + step, 4) * 2 for step in range(4)]
    zs = [lax.rem(me // 8 + step, 4) * 8 for step in range(4)]
    return [zs[offset // 8] + ys[offset // 2 % 4] + cores[offset % 2] for offset in range(count - 1, 0, -1)]


def to_peer(peer, source, target, sems):
    return pltpu.make_async_remote_copy(
        src_ref=source, dst_ref=target, send_sem=sems.at[0], recv_sem=sems.at[1],
        device_id={"energy": peer}, device_id_type=MESH,
    )


def rows_of(ref, peer):
    return ref.at[pl.ds(pl.multiple_of(peer * 8, 8), 8), :]


def collect_kernel(
    count, spaces, diag_ref, coup_ref, pattern_ref, bare_ref,
    diags_ref, coups_ref, rows_ref, slots_ref, bare_pos_ref, bare_own_ref,
    pattern, bare_in, own_pattern, own_bare, scattered, from_core, by_y, from_y, by_z, from_z,
    own_sem, far_send, far_recv, near_send, near_recv, core_sems, y_send, y_recv, z_send, z_recv,
):
    me = lax.axis_index("energy")
    place = lax.axis_index("space")
    width = diag_ref.shape[1]
    half = width // 2
    core = lax.rem(me, 2)
    other = me + 1 - 2 * core
    own_y = lax.rem(me // 2, 4)
    own_z = me // 8
    span = bare_ref.shape[1]
    chunk = own_bare.shape[1]
    sides = (lax.rem(place + 1, spaces), lax.rem(place + spaces - 1, spaces))
    across = lax.rem(place + 2, spaces)

    own_copies = [
        pltpu.make_async_copy(pattern_ref, pattern, own_sem.at[0]),
        pltpu.make_async_copy(bare_ref, bare_in, own_sem.at[1]),
        pltpu.make_async_copy(diag_ref.at[0], diags_ref.at[place], own_sem.at[2]),
        pltpu.make_async_copy(coup_ref.at[0], coups_ref.at[place], own_sem.at[3]),
    ]
    for copy in own_copies:
        copy.start()

    barrier = pltpu.get_barrier_semaphore()
    for side in sides:
        pl.semaphore_signal(barrier, inc=1, device_id={"space": side}, device_id_type=MESH)
    for step in (2, 1, 3):
        for stride in (2, 8):
            pl.semaphore_signal(
                barrier, inc=1, device_id={"energy": peer_of(me, step * stride)}, device_id_type=MESH)
    pl.semaphore_signal(barrier, inc=1, device_id={"energy": other}, device_id_type=MESH)

    own_copies[0].wait()
    own_copies[1].wait()
    tail = chunk - 128
    for part in range(count):
        size = chunk if part < count - 1 else span
        if size < chunk:
            own_pattern[part, :, tail:] = jnp.zeros((1, 128), jnp.int32)
            rows_ref[part, :, tail:] = jnp.zeros((1, 128), jnp.int32)
            slots_ref[part, :, tail:] = jnp.zeros((1, 128), jnp.int32)
        piece = pattern[:, part * span:part * span + size]
        own_pattern[part, :, :size] = piece
        row = lax.shift_right_logical(piece, 8)
        col = jnp.bitwise_and(piece, 255)
        high = jnp.maximum(row, col)
        low = jnp.minimum(row, col)
        lower = low >= 128
        pivot = high == low
        rows_ref[part, :, :size] = jnp.where(jnp.logical_and(lower, jnp.logical_not(pivot)), low - 128, high)
        slots_ref[part, :, :size] = jnp.where(lower, jnp.where(pivot, 128, high - 128), low)
    own_bare[:, tail:] = jnp.zeros((1, 128), F32)
    own_bare[:, :span] = bare_in[...]

    pl.semaphore_wait(barrier, 9)
    own_half = pl.ds(pl.multiple_of(core * half, half), half)
    other_half = pl.ds(pl.multiple_of((1 - core) * half, half), half)
    given = (diag_ref, coup_ref)
    stores = (diags_ref, coups_ref)

    def far(way, stage):
        kind = (way, 1 - way, way)[stage]
        block = place if stage < 2 else sides[1 - way]
        source = given[kind].at[0, own_half] if stage < 2 else stores[kind].at[block, own_half]
        return pltpu.make_async_remote_copy(
            src_ref=source, dst_ref=stores[kind].at[block, own_half],
            send_sem=far_send.at[way, stage], recv_sem=far_recv.at[way, stage],
            device_id={"space": sides[way]}, device_id_type=MESH)

    def near(way, stage, part):
        kind = (way, 1 - way, way)[stage]
        block = sides[1 - way] if stage < 2 else across
        piece = stores[kind].at[block, part]
        return pltpu.make_async_remote_copy(
            src_ref=piece, dst_ref=piece,
            send_sem=near_send.at[way, stage], recv_sem=near_recv.at[way, stage],
            device_id={"energy": other}, device_id_type=MESH)

    for stage in range(2):
        for way in range(2):
            far(way, stage).start()

    mine = own_pattern[me]
    bare = own_bare[...]
    index = lax.broadcasted_iota(jnp.int32, (width, chunk), 0)
    on_row = index == lax.shift_right_logical(mine, 8)
    on_col = jnp.where(index == jnp.bitwise_and(mine, 255), 1.0, 0.0).astype(BF16)
    rest = bare
    total = None
    for _ in range(3):
        part = rest.astype(BF16).astype(F32)
        rest = rest - part
        term = dot_nt(jnp.where(on_row, part, 0.0).astype(BF16), on_col)
        total = term if total is None else total + term
    for peer in range(count):
        scattered[peer % 2, peer // 2 % 4, peer // 8] = total[peer * 8:peer * 8 + 8, :]
    for line in range(chunk // 128):
        bare_own_ref[line:line + 1, :] = bare[:, line * 128:(line + 1) * 128]
    for line in range(chunk // 128, bare_own_ref.shape[0]):
        bare_own_ref[line:line + 1, :] = jnp.zeros((1, 128), F32)

    to_core = pltpu.make_async_remote_copy(
        src_ref=scattered.at[1 - core], dst_ref=from_core,
        send_sem=core_sems.at[0], recv_sem=core_sems.at[1],
        device_id={"energy": other}, device_id_type=MESH)

    def to_y(step):
        return pltpu.make_async_remote_copy(
            src_ref=by_y.at[lax.rem(own_y + step, 4)], dst_ref=from_y.at[step],
            send_sem=y_send.at[step], recv_sem=y_recv.at[step],
            device_id={"energy": peer_of(me, 2 * step)}, device_id_type=MESH)

    def to_z(step):
        return pltpu.make_async_remote_copy(
            src_ref=by_z.at[lax.rem(own_z + step, 4)], dst_ref=from_z.at[step],
            send_sem=z_send.at[step], recv_sem=z_recv.at[step],
            device_id={"energy": peer_of(me, 8 * step)}, device_id_type=MESH)

    to_core.start()
    for way in range(2):
        far(way, 0).wait_recv()
        far(way, 2).start()
        near(way, 0, own_half).start()
    to_core.wait()
    for y in range(4):
        for z in range(4):
            by_y[y, z] = scattered[core, y, z] + from_core[y, z]
    for step in (2, 1, 3):
        to_y(step).start()
    for step in (1, 3, 2):
        to_y(step).wait()
    for z in range(4):
        by_z[z] = (by_y[own_y, z] + from_y[1, z]) + (from_y[2, z] + from_y[3, z])
    for step in (2, 1, 3):
        to_z(step).start()
    for stage in (1, 2):
        for way in range(2):
            far(way, stage).wait_recv()
            near(way, stage, own_half).start()
    for step in (1, 3, 2):
        to_z(step).wait()
    bare_pos_ref[...] = (by_z[own_z] + from_z[1]) + (from_z[2] + from_z[3])
    for copy in own_copies[2:]:
        copy.wait()
    for stage in range(3):
        for way in range(2):
            far(way, stage).wait_send()
            near(way, stage, own_half).wait_send()
            near(way, stage, other_half).wait_recv()


def chain_kernel(
    shift_ref, diags_ref, coups_ref, reduced_ref, base_ref,
    v_ref, vt_ref, w_ref, wt_ref, c_ref, ct_ref, last_ref, x_ref, y_ref,
):
    place = lax.axis_index("space")
    width = base_ref.shape[0]
    lead_parts = split(coups_ref[3])
    quarter = (
        dot_nt(lead_parts[0], lead_parts[0])
        + (dot_nt(lead_parts[0], lead_parts[1]) + dot_nt(lead_parts[1], lead_parts[0]))
    ) * 0.25
    last_ref[...] = diags_ref[3] - quarter
    lower = place <= 1
    at_end = jnp.logical_or(place == 0, place == 3)

    def choose(block, flipped, ref, turned_ref):
        value = coups_ref[block]
        turned = value.T
        ref[...] = jnp.where(flipped, turned, value)
        turned_ref[...] = jnp.where(flipped, value, turned)

    first = jnp.where(place == 0, 1, jnp.where(place == 1, 0, jnp.where(place == 2, 3, 2)))
    second = jnp.where(lower, 3, 0)
    middle = jnp.where(lower, 2, 1)
    choose(1, jnp.logical_not(lower), c_ref, ct_ref)
    choose(jnp.where(lower, 2, 0), lower, v_ref, vt_ref)
    choose(jnp.where(lower, 0, 2), lax.rem(place, 2) == 0, w_ref, wt_ref)
    shift = identity(width) * shift_ref[0]

    def system(block):
        return jnp.where(block == 3, last_ref[...], diags_ref[block]) + shift

    def run(solve):
        x, y = solve([system(first), system(second)], [x_ref, y_ref])
        x, y = split(x), split(y)
        wt_s, ut_s = split(wt_ref[...]), split(ct_ref[...])
        xw = split(mul(x, split(w_ref[...])))
        yv = split(mul(y, split(v_ref[...])))
        xu = split(mul(x, split(c_ref[...])))
        rest = system(place) - mul(wt_s, xw)
        inner = system(middle) - mul(split(vt_ref[...]), yv) - jnp.where(at_end, mul(ut_s, xu), 0.0)
        c = jnp.where(at_end, mul(wt_s, xu), c_ref[...])
        ct = jnp.where(at_end, mul(ut_s, xw), ct_ref[...])
        (z,) = solve([inner], [x_ref])
        reduced = rest - mul(split(product(c, z)), split(ct))
        reduced_ref[...] = reduced
        (base,) = solve([reduced], [base_ref])
        return base

    squares = []

    def solve_quickly(matrices, refs):
        inverses, residuals = quick(matrices)
        squares.extend(residuals)
        return inverses

    base_ref[...] = run(solve_quickly)
    worst = total_of(squares[0])
    for square in squares[1:]:
        worst = jnp.maximum(worst, total_of(square))
    worst = jnp.where(worst <= TOLERANCE, worst, 2.0 * TOLERANCE)

    @pl.when(jnp.logical_not(jnp.max(worst) <= TOLERANCE))
    def _():
        def solve_surely(matrices, refs):
            for matrix, ref in zip(matrices, refs):
                ref[...] = series([matrix], [mean_scale(matrix)], 3)[0]
            settle(matrices, refs)
            return [ref[...] for ref in refs]

        base_ref[...] = run(solve_surely)


def screen(samples, bare, scale):
    count = len(samples)
    result = []
    for lag in range(count):
        total = samples[0] * samples[lag]
        for m in range(1, count - lag):
            total = total + samples[m] * samples[m + lag]
        scaled = bare * (total * scale)
        result.append(bare * lax.rsqrt(1.0 + scaled * scaled))
    return result


PAIRS_FIRST = 2
PAIRS_SECOND = 9


def regroup_kernel(
    count, base_ref, rows_ref, slots_ref, bare_pos_ref, spread_ref, taken_ref,
    lhs, arrived, selfen, taken, sems_a, sems_b, sems_c,
):
    me = lax.axis_index("energy")
    width = base_ref.shape[0]
    half = width // 2
    chunk = rows_ref.shape[2]
    lines = taken.shape[1]
    pairs = count // 2
    for peer in range(count):
        taken_ref[peer, chunk // 128:, :] = jnp.zeros((lines - chunk // 128, 128), F32)

    barrier = pltpu.get_barrier_semaphore()

    others = peers_of(count, me)
    for peer in others:
        pl.semaphore_signal(barrier, inc=1, device_id={"energy": peer}, device_id_type=MESH)
    arrived[me] = rows_of(base_ref, me)[...]

    upper = base_ref[:half, :half]
    lower = base_ref[half:, half:]
    r = lax.broadcasted_iota(jnp.int32, (half, half), 0)
    c = lax.broadcasted_iota(jnp.int32, (half, half), 1)
    table = jnp.concatenate([jnp.where(r <= c, upper, lower), base_ref[:half, half:]], axis=1)
    diagonal = jnp.sum(jnp.where(r == c, lower, 0.0), axis=0, keepdims=True)
    extra = jnp.concatenate([jnp.zeros((1, half), F32), diagonal], axis=1)
    first = lax.broadcasted_iota(jnp.int32, (8, width), 0) == 0
    table = jnp.concatenate([table, jnp.where(first, extra, 0.0)], axis=0)
    tall = table.shape[0]
    high = table.astype(BF16).astype(F32)
    lhs[...] = jnp.concatenate([high, table - high], axis=0).astype(BF16)
    row_index = lax.broadcasted_iota(jnp.int32, (width, chunk), 0).astype(F32).astype(BF16)
    line_index = lax.broadcasted_iota(jnp.int32, (8, chunk), 0)
    one, none = jnp.bfloat16(1), jnp.bfloat16(0)

    def take(part):
        hot = jnp.where(row_index == rows_ref[part].astype(F32).astype(BF16), one, none)
        both = dot(lhs[...], hot)
        slots = slots_ref[part]
        group = jnp.broadcast_to(lax.shift_right_logical(slots, 3), (8, chunk))
        found, found_rest = both[:8], both[tall:tall + 8]
        for at in range(1, tall // 8):
            here = group == at
            found = jnp.where(here, both[at * 8:at * 8 + 8], found)
            found_rest = jnp.where(here, both[tall + at * 8:tall + at * 8 + 8], found_rest)
        here = line_index == jnp.bitwise_and(slots, 7)
        line = jnp.sum(jnp.where(here, found + found_rest, 0.0), axis=0, keepdims=True)
        for piece in range(chunk // 128):
            taken[part, piece:piece + 1, :] = line[:, piece * 128:(piece + 1) * 128]

    filled = chunk // 128

    def all_but_one(source, target, sems):
        return to_peer(others[0], source, target, sems)

    def take_pair(pair, carry):
        take(peer_of(me, count - 1 - 2 * pair))
        take(peer_of(me, count - 2 - 2 * pair))
        return carry

    def send_taken(peer):
        to_peer(peer, taken.at[peer, :filled], taken_ref.at[me, :filled], sems_c).start()

    def send_pair(pair, carry):
        for offset in (count - 1 - 2 * pair, count - 2 - 2 * pair):
            send_taken(peer_of(me, offset))
        return carry

    def take_and_send(pair, carry):
        take_pair(pair, carry)
        return send_pair(pair, carry)

    lax.fori_loop(0, PAIRS_FIRST, take_pair, 0)
    pl.semaphore_wait(barrier, count - 1)
    for peer in others:
        to_peer(peer, rows_of(base_ref, peer), arrived.at[me], sems_a).start()
    lax.fori_loop(0, PAIRS_FIRST, send_pair, 0)
    lax.fori_loop(PAIRS_FIRST, PAIRS_FIRST + PAIRS_SECOND, take_and_send, 0)
    rest = pl.ds(8, width - 8)
    first_exchange = all_but_one(base_ref.at[rest, :], arrived.at[pl.ds(1, count - 1)], sems_a)
    first_exchange.wait_send()
    first_exchange.wait_recv()

    scale = polar_coef * width / count
    for side in range(width // 128):
        cols = slice(side * 128, (side + 1) * 128)
        samples = [arrived[e, :, cols] for e in range(count)]
        screened = screen(samples, bare_pos_ref[:, cols], scale)
        for e in range(count):
            total = samples[e] * screened[0]
            for n in range(1, e + 1):
                total = total + samples[e - n] * screened[n]
            selfen[e, :, cols] = total * (sigma_coef / count)
    for peer in others:
        to_peer(peer, selfen.at[peer], rows_of(spread_ref, me), sems_b).start()
    lax.fori_loop(PAIRS_FIRST + PAIRS_SECOND, pairs - 1, take_and_send, 0)
    take_pair(pairs - 1, 0)
    send_taken(peer_of(me, 1))
    taken_ref[me, :filled] = taken[me, :filled]
    spread_ref[pl.ds(pl.multiple_of(me * 8, 8), 8), :] = selfen[me]
    for last_exchange in (
        all_but_one(selfen.at[pl.ds(1, count - 1)], spread_ref.at[rest, :], sems_b),
        all_but_one(taken.at[pl.ds(1, count - 1), :filled], taken_ref.at[pl.ds(1, count - 1), :filled], sems_c),
    ):
        last_exchange.wait_send()
        last_exchange.wait_recv()


def finish_kernel(
    reduced_ref, base_ref, spread_ref, taken_ref, bare_ref, green_ref, screened_ref, x_ref, green_sem,
):
    count = taken_ref.shape[0]
    width = base_ref.shape[0]
    chunk = screened_ref.shape[2]
    spread = spread_ref[...]
    matrix = reduced_ref[...] - 0.5 * (spread + spread.T)
    (better,), (square,) = newton_step([split(matrix)], [base_ref[...]])
    x_ref[...] = better
    worst = jnp.sum(square)

    scale = polar_coef * width / count
    lines = taken_ref.shape[1]

    def write_screened(group):
        at = slice(group * 8, group * 8 + 8)
        samples = [taken_ref[e, at, :] for e in range(count)]
        screened = screen(samples, bare_ref[at, :], scale)
        for line in range(group * 8, min(group * 8 + 8, pl.cdiv(chunk, 128))):
            start = line * 128
            stop = min(start + 128, chunk)
            for n in range(count):
                row = line - group * 8
                screened_ref[n, :, start:stop] = screened[n][row:row + 1, :stop - start]

    write_screened(0)
    settle([matrix], [x_ref], worst)
    copy = pltpu.make_async_copy(x_ref, green_ref.at[0, 0], green_sem)
    copy.start()
    for group in range(1, lines // 8):
        write_screened(group)
    copy.wait()


def on_device(count, spaces, ham_diag, ham_coup, energies, pattern, coulomb):
    width = ham_diag.shape[1]
    span = coulomb.shape[1]
    chunk = pl.cdiv(span, 128) * 128
    lines = pl.cdiv(chunk // 128, 8) * 8
    vmem = pl.BlockSpec(memory_space=pltpu.VMEM)
    hbm = pl.BlockSpec(memory_space=pltpu.HBM)
    smem = pl.BlockSpec(memory_space=pltpu.SMEM)
    square = jax.ShapeDtypeStruct((width, width), F32)
    diags, coups, rows, slots, bare_pos, bare_own = pl.pallas_call(
        functools.partial(collect_kernel, count, spaces),
        out_shape=(
            jax.ShapeDtypeStruct((spaces, width, width), F32),
            jax.ShapeDtypeStruct((spaces, width, width), F32),
            jax.ShapeDtypeStruct((count, 1, chunk), jnp.int32),
            jax.ShapeDtypeStruct((count, 1, chunk), jnp.int32),
            jax.ShapeDtypeStruct((8, width), F32),
            jax.ShapeDtypeStruct((lines, 128), F32),
        ),
        in_specs=[hbm] * 4,
        out_specs=(vmem,) * 6,
        scratch_shapes=[
            VMEM((1, pattern.shape[1]), jnp.int32), VMEM((1, span), F32),
            VMEM((count, 1, chunk), jnp.int32), VMEM((1, chunk), F32),
            VMEM((2, 4, 4, 8, width), F32), VMEM((4, 4, 8, width), F32), VMEM((4, 4, 8, width), F32),
            VMEM((4, 4, 8, width), F32), VMEM((4, 8, width), F32), VMEM((4, 8, width), F32),
            DMA((4,)), DMA((2, 3)), DMA((2, 3)), DMA((2, 3)), DMA((2, 3)),
            DMA((2,)), DMA((4,)), DMA((4,)), DMA((4,)), DMA((4,)),
        ],
        compiler_params=pltpu.CompilerParams(collective_id=0, has_side_effects=True, vmem_limit_bytes=VMEM_LIMIT),
        name="collect",
    )(*(pltpu.with_memory_space_constraint(value, pltpu.HBM) for value in (ham_diag, ham_coup, pattern, coulomb)))

    reduced, base = pl.pallas_call(
        chain_kernel,
        out_shape=(square, square),
        in_specs=[smem, vmem, vmem],
        out_specs=(vmem, vmem),
        scratch_shapes=[VMEM((width, width), F32)] * 9,
        compiler_params=pltpu.CompilerParams(vmem_limit_bytes=VMEM_LIMIT),
        name="chain",
    )(energies, diags, coups)

    spread, taken = pl.pallas_call(
        functools.partial(regroup_kernel, count),
        out_shape=(square, jax.ShapeDtypeStruct((count, lines, 128), F32)),
        in_specs=[vmem] * 4,
        out_specs=(vmem, vmem),
        scratch_shapes=[
            VMEM((width + 16, width), BF16), VMEM((count, 8, width), F32),
            VMEM((count, 8, width), F32), VMEM((count, lines, 128), F32),
        ] + [DMA((2,))] * 3,
        compiler_params=pltpu.CompilerParams(collective_id=1, has_side_effects=True, vmem_limit_bytes=VMEM_LIMIT),
        name="regroup",
    )(base, rows, slots, bare_pos)

    return pl.pallas_call(
        finish_kernel,
        out_shape=(
            jax.ShapeDtypeStruct((1, 1, width, width), F32),
            jax.ShapeDtypeStruct((count, 1, span), F32),
        ),
        in_specs=[vmem] * 5,
        out_specs=(hbm, vmem),
        scratch_shapes=[VMEM((width, width), F32), DMA],
        compiler_params=pltpu.CompilerParams(vmem_limit_bytes=VMEM_LIMIT),
        name="finish",
    )(reduced, base, spread, taken, bare_own)


def solution(mesh):
    count, spaces = mesh.shape["energy"], mesh.shape["space"]
    return jax.shard_map(
        functools.partial(on_device, count, spaces),
        mesh=mesh,
        in_specs=(
            P("space", None, None),
            P("space", None, None),
            P("energy"),
            P("space", None),
            P("space", "energy"),
        ),
        out_specs=(P("energy", "space", None, None), P(None, "space", "energy")),
        check_vma=False,
    )
```

```python
import functools

import jax
import jax.numpy as jnp
from jax import lax
from jax.experimental import pallas as pl
from jax.experimental.pallas import tpu as pltpu
from jax.sharding import PartitionSpec as P

F32, BF16 = jnp.float32, jnp.bfloat16
MESH = pl.DeviceIdType.MESH
VMEM = pltpu.VMEM
DMA = pltpu.SemaphoreType.DMA

polar_coef = 128.0
sigma_coef = 0.5

TOLERANCE = 2e-5
VMEM_LIMIT = 20 << 20


def split(value):
    high = value.astype(BF16)
    return high, (value - high.astype(F32)).astype(BF16)


def dot(a, b):
    return jnp.dot(a, b, preferred_element_type=F32)


def dot_nt(a, b):
    return lax.dot_general(a, b, (((1,), (1,)), ((), ())), preferred_element_type=F32)


def mul(a, b):
    return dot(a[0], b[0]) + (dot(a[0], b[1]) + dot(a[1], b[0]))


def product(a, b):
    return mul(split(a), split(b))


def identity(width):
    rows = lax.broadcasted_iota(jnp.int32, (width, width), 0)
    cols = lax.broadcasted_iota(jnp.int32, (width, width), 1)
    return jnp.where(rows == cols, 1.0, 0.0).astype(F32)


def series(matrices, scales, doublings):
    ident = identity(matrices[0].shape[0])
    parts = [split(matrix) for matrix in matrices]
    squares = [mul(own, own) for own in parts]
    powers = [
        ident - matrix * (2.0 * scale) + square * (scale * scale)
        for matrix, scale, square in zip(matrices, scales, squares)
    ]
    guesses = [scale * (2.0 * ident - matrix * scale) for matrix, scale in zip(matrices, scales)]
    guesses = [guess + product(guess, power) for guess, power in zip(guesses, powers)]
    for _ in range(doublings - 1):
        highs = [power.astype(BF16) for power in powers]
        powers = [dot(high, high) for high in highs]
        guesses = [
            guess + dot(guess.astype(BF16), power.astype(BF16)) for guess, power in zip(guesses, powers)
        ]
    return guesses


def total_of(value):
    return jnp.sum(jnp.sum(value, axis=0, keepdims=True), axis=1, keepdims=True)


def mean_scale(matrix):
    trace = total_of(jnp.where(identity(matrix.shape[0]) > 0.0, matrix, 0.0))
    return trace / total_of(matrix * matrix)


def safe_scale(matrix):
    return 1.9 / jnp.max(jnp.sum(jnp.abs(matrix), axis=0, keepdims=True), axis=1, keepdims=True)


def eliminate(matrix, out_ref):
    width = matrix.shape[0]
    out_ref[...] = matrix
    lanes = lax.broadcasted_iota(jnp.int32, (1, width), 1)

    def step(pivot, carry):
        whole = out_ref[...]
        row = out_ref[pl.ds(pivot, 1), :]
        here = lanes == pivot
        value = jnp.sum(jnp.where(here, row, 0.0), axis=1, keepdims=True)
        column = jnp.sum(jnp.where(here, whole, 0.0), axis=1, keepdims=True)
        scaled = jnp.where(here, 1.0, row) / value
        out_ref[...] = jnp.where(here, 0.0, whole) - column * scaled
        out_ref[pl.ds(pivot, 1), :] = scaled
        return carry

    lax.fori_loop(0, width, step, 0)


def newton_step(parts, guesses):
    ident = identity(guesses[0].shape[0])
    split_guesses = [split(guess) for guess in guesses]
    residuals = [ident - mul(own, guess) for own, guess in zip(parts, split_guesses)]
    better = [
        guess + dot(guess_parts[0], residual.astype(BF16))
        for guess, guess_parts, residual in zip(guesses, split_guesses, residuals)
    ]
    return better, [residual * residual for residual in residuals]


def newton(matrices, refs, limit, worst=1.0):
    parts = [split(matrix) for matrix in matrices]

    def unsettled(carry):
        steps, last = carry
        return jnp.logical_and(last > TOLERANCE, steps < limit)

    def step(carry):
        better, squares = newton_step(parts, [ref[...] for ref in refs])
        largest = jnp.float32(0.0)
        for ref, value, square in zip(refs, better, squares):
            ref[...] = value
            largest = jnp.maximum(largest, jnp.sum(square))
        return carry[0] + 1, largest

    return lax.while_loop(unsettled, step, (jnp.int32(0), jnp.asarray(worst, F32)))[1]


def settle(matrices, refs, worst=1.0):
    worst = newton(matrices, refs, 8, worst)

    @pl.when(jnp.logical_not(worst <= TOLERANCE))
    def _():
        for matrix, ref in zip(matrices, refs):
            ref[...] = series([matrix], [safe_scale(matrix)], 5)[0]
        again = newton(matrices, refs, 48)

        @pl.when(jnp.logical_not(again <= TOLERANCE))
        def _():
            for matrix, ref in zip(matrices, refs):
                eliminate(matrix, ref)


def quick(matrices):
    guesses = series(matrices, [mean_scale(matrix) for matrix in matrices], 3)
    return newton_step([split(matrix) for matrix in matrices], guesses)


def peer_of(me, offset):
    core = lax.rem(me + offset, 2)
    y = lax.rem(me // 2 + offset // 2, 4)
    z = lax.rem(me // 8 + offset // 8, 4)
    return z * 8 + y * 2 + core


def peers_of(count, me):
    cores = [lax.rem(me + step, 2) for step in range(2)]
    ys = [lax.rem(me // 2 + step, 4) * 2 for step in range(4)]
    zs = [lax.rem(me // 8 + step, 4) * 8 for step in range(4)]
    return [zs[offset // 8] + ys[offset // 2 % 4] + cores[offset % 2] for offset in range(count - 1, 0, -1)]


def to_peer(peer, source, target, sems):
    return pltpu.make_async_remote_copy(
        src_ref=source, dst_ref=target, send_sem=sems.at[0], recv_sem=sems.at[1],
        device_id={"energy": peer}, device_id_type=MESH,
    )


def rows_of(ref, peer):
    return ref.at[pl.ds(pl.multiple_of(peer * 8, 8), 8), :]


def collect_kernel(
    count, spaces, diag_ref, coup_ref, pattern_ref, bare_ref,
    diags_ref, coups_ref, rows_ref, slots_ref, bare_pos_ref, bare_own_ref,
    pattern, bare_in, own_pattern, own_bare, scattered, from_core, by_y, from_y, by_z, from_z,
    own_sem, far_send, far_recv, near_send, near_recv, more_sems, core_sems, y_send, y_recv, z_send, z_recv,
):
    me = lax.axis_index("energy")
    place = lax.axis_index("space")
    width = diag_ref.shape[1]
    half = width // 2
    core = lax.rem(me, 2)
    other = me + 1 - 2 * core
    own_y = lax.rem(me // 2, 4)
    own_z = me // 8
    span = bare_ref.shape[1]
    chunk = own_bare.shape[1]
    sides = (lax.rem(place + 1, spaces), lax.rem(place + spaces - 1, spaces))
    across = lax.rem(place + 2, spaces)

    own_copies = [
        pltpu.make_async_copy(pattern_ref, pattern, own_sem.at[0]),
        pltpu.make_async_copy(bare_ref, bare_in, own_sem.at[1]),
        pltpu.make_async_copy(diag_ref.at[0], diags_ref.at[place], own_sem.at[2]),
        pltpu.make_async_copy(coup_ref.at[0], coups_ref.at[place], own_sem.at[3]),
    ]
    for copy in own_copies:
        copy.start()

    barrier = pltpu.get_barrier_semaphore()
    for side in sides:
        pl.semaphore_signal(barrier, inc=1, device_id={"space": side}, device_id_type=MESH)
    for step in (2, 1, 3):
        for stride in (2, 8):
            pl.semaphore_signal(
                barrier, inc=1, device_id={"energy": peer_of(me, step * stride)}, device_id_type=MESH)
    pl.semaphore_signal(barrier, inc=1, device_id={"energy": other}, device_id_type=MESH)

    own_copies[0].wait()
    own_copies[1].wait()
    tail = chunk - 128
    for part in range(count):
        size = chunk if part < count - 1 else span
        if size < chunk:
            own_pattern[part, :, tail:] = jnp.zeros((1, 128), jnp.int32)
            rows_ref[part, :, tail:] = jnp.zeros((1, 128), jnp.int32)
            slots_ref[part, :, tail:] = jnp.zeros((1, 128), jnp.int32)
        piece = pattern[:, part * span:part * span + size]
        own_pattern[part, :, :size] = piece
        row = lax.shift_right_logical(piece, 8)
        col = jnp.bitwise_and(piece, 255)
        high = jnp.maximum(row, col)
        low = jnp.minimum(row, col)
        lower = low >= 128
        pivot = high == low
        rows_ref[part, :, :size] = jnp.where(jnp.logical_and(lower, jnp.logical_not(pivot)), low - 128, high)
        slots_ref[part, :, :size] = jnp.where(lower, jnp.where(pivot, 128, high - 128), low)
    own_bare[:, tail:] = jnp.zeros((1, 128), F32)
    own_bare[:, :span] = bare_in[...]

    pl.semaphore_wait(barrier, 9)
    own_half = pl.ds(pl.multiple_of(core * half, half), half)
    other_half = pl.ds(pl.multiple_of((1 - core) * half, half), half)
    given = (diag_ref, coup_ref)
    stores = (diags_ref, coups_ref)

    own_quarter = pl.ds(pl.multiple_of(half + core * (half // 2), half // 2), half // 2)
    other_quarter = pl.ds(pl.multiple_of(half + (1 - core) * (half // 2), half // 2), half // 2)

    class Pieces:
        def __init__(self, kind, source, store, part, quarter, sems, device):
            views = ((part,),) if kind else ((part, part), (quarter, pl.ds(0, half)))
            self.copies = [
                pltpu.make_async_remote_copy(
                    src_ref=source.at[view], dst_ref=store.at[view], send_sem=sems[0][at], recv_sem=sems[1][at],
                    device_id=device, device_id_type=MESH)
                for at, view in enumerate(views)
            ]

        def start(self):
            for copy in self.copies:
                copy.start()

        def wait_send(self):
            for copy in self.copies:
                copy.wait_send()

        def wait_recv(self):
            for copy in self.copies:
                copy.wait_recv()

    def far(way, stage):
        kind = (way, 1 - way, way)[stage]
        block = place if stage < 2 else sides[1 - way]
        store = stores[kind].at[block]
        source = given[kind].at[0] if stage < 2 else store
        sems = (
            (far_send.at[way, stage], more_sems.at[way, stage, 0]),
            (far_recv.at[way, stage], more_sems.at[way, stage, 1]),
        )
        return Pieces(kind, source, store, own_half, own_quarter, sems, {"space": sides[way]})

    def near(way, stage, own):
        kind = (way, 1 - way, way)[stage]
        block = sides[1 - way] if stage < 2 else across
        store = stores[kind].at[block]
        sems = (
            (near_send.at[way, stage], more_sems.at[way, stage, 2]),
            (near_recv.at[way, stage], more_sems.at[way, stage, 3]),
        )
        part, quarter = (own_half, own_quarter) if own else (other_half, other_quarter)
        return Pieces(kind, store, store, part, quarter, sems, {"energy": other})

    for stage in range(2):
        for way in range(2):
            far(way, stage).start()

    mine = own_pattern[me]
    bare = own_bare[...]
    index = lax.broadcasted_iota(jnp.int32, (width, chunk), 0)
    on_row = index == lax.shift_right_logical(mine, 8)
    on_col = jnp.where(index == jnp.bitwise_and(mine, 255), 1.0, 0.0).astype(BF16)
    rest = bare
    total = None
    for _ in range(3):
        part = rest.astype(BF16).astype(F32)
        rest = rest - part
        term = dot_nt(jnp.where(on_row, part, 0.0).astype(BF16), on_col)
        total = term if total is None else total + term
    for peer in range(count):
        scattered[peer % 2, peer // 2 % 4, peer // 8] = total[peer * 8:peer * 8 + 8, :]
    for line in range(chunk // 128):
        bare_own_ref[line:line + 1, :] = bare[:, line * 128:(line + 1) * 128]
    for line in range(chunk // 128, bare_own_ref.shape[0]):
        bare_own_ref[line:line + 1, :] = jnp.zeros((1, 128), F32)

    to_core = pltpu.make_async_remote_copy(
        src_ref=scattered.at[1 - core], dst_ref=from_core,
        send_sem=core_sems.at[0], recv_sem=core_sems.at[1],
        device_id={"energy": other}, device_id_type=MESH)

    def to_y(step):
        return pltpu.make_async_remote_copy(
            src_ref=by_y.at[lax.rem(own_y + step, 4)], dst_ref=from_y.at[step],
            send_sem=y_send.at[step], recv_sem=y_recv.at[step],
            device_id={"energy": peer_of(me, 2 * step)}, device_id_type=MESH)

    def to_z(step):
        return pltpu.make_async_remote_copy(
            src_ref=by_z.at[lax.rem(own_z + step, 4)], dst_ref=from_z.at[step],
            send_sem=z_send.at[step], recv_sem=z_recv.at[step],
            device_id={"energy": peer_of(me, 8 * step)}, device_id_type=MESH)

    to_core.start()
    for way in range(2):
        far(way, 0).wait_recv()
        far(way, 2).start()
        near(way, 0, True).start()
    to_core.wait()
    for y in range(4):
        for z in range(4):
            by_y[y, z] = scattered[core, y, z] + from_core[y, z]
    for step in (2, 1, 3):
        to_y(step).start()
    for step in (1, 3, 2):
        to_y(step).wait()
    for z in range(4):
        by_z[z] = (by_y[own_y, z] + from_y[1, z]) + (from_y[2, z] + from_y[3, z])
    for step in (2, 1, 3):
        to_z(step).start()
    for stage in (1, 2):
        for way in range(2):
            far(way, stage).wait_recv()
            near(way, stage, True).start()
    for step in (1, 3, 2):
        to_z(step).wait()
    bare_pos_ref[...] = (by_z[own_z] + from_z[1]) + (from_z[2] + from_z[3])
    for copy in own_copies[2:]:
        copy.wait()
    for stage in range(3):
        for way in range(2):
            far(way, stage).wait_send()
            near(way, stage, True).wait_send()
            near(way, stage, False).wait_recv()


def chain_kernel(
    shift_ref, diags_ref, coups_ref, reduced_ref, base_ref,
    v_ref, vt_ref, w_ref, wt_ref, c_ref, ct_ref, last_ref, x_ref, y_ref,
):
    place = lax.axis_index("space")
    width = base_ref.shape[0]
    lead_parts = split(coups_ref[3])
    quarter = (
        dot_nt(lead_parts[0], lead_parts[0])
        + (dot_nt(lead_parts[0], lead_parts[1]) + dot_nt(lead_parts[1], lead_parts[0]))
    ) * 0.25

    def whole(block):
        half = width // 2
        left = diags_ref[block, :, :half]
        right = diags_ref[block, half:, half:]
        return jnp.concatenate([left, jnp.concatenate([left[half:].T, right], axis=0)], axis=1)

    last_ref[...] = whole(3) - quarter
    lower = place <= 1
    at_end = jnp.logical_or(place == 0, place == 3)

    def choose(block, flipped, ref, turned_ref):
        value = coups_ref[block]
        turned = value.T
        ref[...] = jnp.where(flipped, turned, value)
        turned_ref[...] = jnp.where(flipped, value, turned)

    first = jnp.where(place == 0, 1, jnp.where(place == 1, 0, jnp.where(place == 2, 3, 2)))
    second = jnp.where(lower, 3, 0)
    middle = jnp.where(lower, 2, 1)
    choose(1, jnp.logical_not(lower), c_ref, ct_ref)
    choose(jnp.where(lower, 2, 0), lower, v_ref, vt_ref)
    choose(jnp.where(lower, 0, 2), lax.rem(place, 2) == 0, w_ref, wt_ref)
    shift = identity(width) * shift_ref[0]

    def system(block):
        return jnp.where(block == 3, last_ref[...], whole(block)) + shift

    def run(solve):
        x, y = solve([system(first), system(second)], [x_ref, y_ref])
        x, y = split(x), split(y)
        wt_s, ut_s = split(wt_ref[...]), split(ct_ref[...])
        xw = split(mul(x, split(w_ref[...])))
        yv = split(mul(y, split(v_ref[...])))
        xu = split(mul(x, split(c_ref[...])))
        rest = system(place) - mul(wt_s, xw)
        inner = system(middle) - mul(split(vt_ref[...]), yv) - jnp.where(at_end, mul(ut_s, xu), 0.0)
        c = jnp.where(at_end, mul(wt_s, xu), c_ref[...])
        ct = jnp.where(at_end, mul(ut_s, xw), ct_ref[...])
        (z,) = solve([inner], [x_ref])
        reduced = rest - mul(split(product(c, z)), split(ct))
        reduced_ref[...] = reduced
        (base,) = solve([reduced], [base_ref])
        return base

    squares = []

    def solve_quickly(matrices, refs):
        inverses, residuals = quick(matrices)
        squares.extend(residuals)
        return inverses

    base_ref[...] = run(solve_quickly)
    worst = total_of(squares[0])
    for square in squares[1:]:
        worst = jnp.maximum(worst, total_of(square))
    worst = jnp.where(worst <= TOLERANCE, worst, 2.0 * TOLERANCE)

    @pl.when(jnp.logical_not(jnp.max(worst) <= TOLERANCE))
    def _():
        def solve_surely(matrices, refs):
            for matrix, ref in zip(matrices, refs):
                ref[...] = series([matrix], [mean_scale(matrix)], 3)[0]
            settle(matrices, refs)
            return [ref[...] for ref in refs]

        base_ref[...] = run(solve_surely)


def screen(samples, bare, scale):
    count = len(samples)
    result = []
    for lag in range(count):
        total = samples[0] * samples[lag]
        for m in range(1, count - lag):
            total = total + samples[m] * samples[m + lag]
        scaled = bare * (total * scale)
        result.append(bare * lax.rsqrt(1.0 + scaled * scaled))
    return result


PAIRS_FIRST = 2
PAIRS_SECOND = 9


def regroup_kernel(
    count, base_ref, rows_ref, slots_ref, bare_pos_ref, spread_ref, taken_ref,
    lhs, arrived, selfen, taken, sems_a, sems_b, sems_c,
):
    me = lax.axis_index("energy")
    width = base_ref.shape[0]
    half = width // 2
    chunk = rows_ref.shape[2]
    lines = taken.shape[1]
    pairs = count // 2
    for peer in range(count):
        taken_ref[peer, chunk // 128:, :] = jnp.zeros((lines - chunk // 128, 128), F32)

    barrier = pltpu.get_barrier_semaphore()

    others = peers_of(count, me)
    for peer in others:
        pl.semaphore_signal(barrier, inc=1, device_id={"energy": peer}, device_id_type=MESH)
    arrived[me] = rows_of(base_ref, me)[...]

    upper = base_ref[:half, :half]
    lower = base_ref[half:, half:]
    r = lax.broadcasted_iota(jnp.int32, (half, half), 0)
    c = lax.broadcasted_iota(jnp.int32, (half, half), 1)
    table = jnp.concatenate([jnp.where(r <= c, upper, lower), base_ref[:half, half:]], axis=1)
    diagonal = jnp.sum(jnp.where(r == c, lower, 0.0), axis=0, keepdims=True)
    extra = jnp.concatenate([jnp.zeros((1, half), F32), diagonal], axis=1)
    first = lax.broadcasted_iota(jnp.int32, (8, width), 0) == 0
    table = jnp.concatenate([table, jnp.where(first, extra, 0.0)], axis=0)
    tall = table.shape[0]
    high = table.astype(BF16).astype(F32)
    lhs[...] = jnp.concatenate([high, table - high], axis=0).astype(BF16)
    row_index = lax.broadcasted_iota(jnp.int32, (width, chunk), 0).astype(F32).astype(BF16)
    line_index = lax.broadcasted_iota(jnp.int32, (8, chunk), 0)
    one, none = jnp.bfloat16(1), jnp.bfloat16(0)

    def take(part):
        hot = jnp.where(row_index == rows_ref[part].astype(F32).astype(BF16), one, none)
        both = dot(lhs[...], hot)
        slots = slots_ref[part]
        group = jnp.broadcast_to(lax.shift_right_logical(slots, 3), (8, chunk))
        found, found_rest = both[:8], both[tall:tall + 8]
        for at in range(1, tall // 8):
            here = group == at
            found = jnp.where(here, both[at * 8:at * 8 + 8], found)
            found_rest = jnp.where(here, both[tall + at * 8:tall + at * 8 + 8], found_rest)
        here = line_index == jnp.bitwise_and(slots, 7)
        line = jnp.sum(jnp.where(here, found + found_rest, 0.0), axis=0, keepdims=True)
        for piece in range(chunk // 128):
            taken[part, piece:piece + 1, :] = line[:, piece * 128:(piece + 1) * 128]

    filled = chunk // 128

    def all_but_one(source, target, sems):
        return to_peer(others[0], source, target, sems)

    def take_pair(pair, carry):
        take(peer_of(me, count - 1 - 2 * pair))
        take(peer_of(me, count - 2 - 2 * pair))
        return carry

    def send_taken(peer):
        to_peer(peer, taken.at[peer, :filled], taken_ref.at[me, :filled], sems_c).start()

    def send_pair(pair, carry):
        for offset in (count - 1 - 2 * pair, count - 2 - 2 * pair):
            send_taken(peer_of(me, offset))
        return carry

    def take_and_send(pair, carry):
        take_pair(pair, carry)
        return send_pair(pair, carry)

    lax.fori_loop(0, PAIRS_FIRST, take_pair, 0)
    pl.semaphore_wait(barrier, count - 1)
    for peer in others:
        to_peer(peer, rows_of(base_ref, peer), arrived.at[me], sems_a).start()
    lax.fori_loop(0, PAIRS_FIRST, send_pair, 0)
    lax.fori_loop(PAIRS_FIRST, PAIRS_FIRST + PAIRS_SECOND, take_and_send, 0)
    rest = pl.ds(8, width - 8)
    first_exchange = all_but_one(base_ref.at[rest, :], arrived.at[pl.ds(1, count - 1)], sems_a)
    first_exchange.wait_send()
    first_exchange.wait_recv()

    scale = polar_coef * width / count
    for side in range(width // 128):
        cols = slice(side * 128, (side + 1) * 128)
        samples = [arrived[e, :, cols] for e in range(count)]
        screened = screen(samples, bare_pos_ref[:, cols], scale)
        for e in range(count):
            total = samples[e] * screened[0]
            for n in range(1, e + 1):
                total = total + samples[e - n] * screened[n]
            selfen[e, :, cols] = total * (sigma_coef / count)
    for peer in others:
        to_peer(peer, selfen.at[peer], rows_of(spread_ref, me), sems_b).start()
    lax.fori_loop(PAIRS_FIRST + PAIRS_SECOND, pairs - 1, take_and_send, 0)
    take_pair(pairs - 1, 0)
    send_taken(peer_of(me, 1))
    taken_ref[me, :filled] = taken[me, :filled]
    spread_ref[pl.ds(pl.multiple_of(me * 8, 8), 8), :] = selfen[me]
    for last_exchange in (
        all_but_one(selfen.at[pl.ds(1, count - 1)], spread_ref.at[rest, :], sems_b),
        all_but_one(taken.at[pl.ds(1, count - 1), :filled], taken_ref.at[pl.ds(1, count - 1), :filled], sems_c),
    ):
        last_exchange.wait_send()
        last_exchange.wait_recv()


def finish_kernel(reduced_ref, base_ref, spread_ref, taken_ref, bare_ref, green_ref, screened_ref, x_ref):
    count = taken_ref.shape[0]
    width = base_ref.shape[0]
    chunk = screened_ref.shape[2]
    spread = spread_ref[...]
    matrix = reduced_ref[...] - 0.5 * (spread + spread.T)
    parts = split(matrix)
    base = base_ref[...]
    base_parts = split(base)
    residual = identity(width) - mul(parts, base_parts)
    near = residual.astype(BF16)
    guess = base + dot(base_parts[0], (residual + dot(near, near)).astype(BF16))
    (better,), (square,) = newton_step([parts], [guess])
    x_ref[...] = better

    scale = polar_coef * width / count
    for group in range(taken_ref.shape[1] // 8):
        at = slice(group * 8, group * 8 + 8)
        samples = [taken_ref[e, at, :] for e in range(count)]
        screened = screen(samples, bare_ref[at, :], scale)
        for line in range(group * 8, min(group * 8 + 8, pl.cdiv(chunk, 128))):
            start = line * 128
            stop = min(start + 128, chunk)
            for n in range(count):
                row = line - group * 8
                screened_ref[n, :, start:stop] = screened[n][row:row + 1, :stop - start]

    settle([matrix], [x_ref], jnp.sum(square))
    green_ref[0, 0] = x_ref[...]


def on_device(count, spaces, ham_diag, ham_coup, energies, pattern, coulomb):
    width = ham_diag.shape[1]
    span = coulomb.shape[1]
    chunk = pl.cdiv(span, 128) * 128
    lines = pl.cdiv(chunk // 128, 8) * 8
    vmem = pl.BlockSpec(memory_space=pltpu.VMEM)
    hbm = pl.BlockSpec(memory_space=pltpu.HBM)
    smem = pl.BlockSpec(memory_space=pltpu.SMEM)
    square = jax.ShapeDtypeStruct((width, width), F32)
    diags, coups, rows, slots, bare_pos, bare_own = pl.pallas_call(
        functools.partial(collect_kernel, count, spaces),
        out_shape=(
            jax.ShapeDtypeStruct((spaces, width, width), F32),
            jax.ShapeDtypeStruct((spaces, width, width), F32),
            jax.ShapeDtypeStruct((count, 1, chunk), jnp.int32),
            jax.ShapeDtypeStruct((count, 1, chunk), jnp.int32),
            jax.ShapeDtypeStruct((8, width), F32),
            jax.ShapeDtypeStruct((lines, 128), F32),
        ),
        in_specs=[hbm] * 4,
        out_specs=(vmem,) * 6,
        scratch_shapes=[
            VMEM((1, pattern.shape[1]), jnp.int32), VMEM((1, span), F32),
            VMEM((count, 1, chunk), jnp.int32), VMEM((1, chunk), F32),
            VMEM((2, 4, 4, 8, width), F32), VMEM((4, 4, 8, width), F32), VMEM((4, 4, 8, width), F32),
            VMEM((4, 4, 8, width), F32), VMEM((4, 8, width), F32), VMEM((4, 8, width), F32),
            DMA((4,)), DMA((2, 3)), DMA((2, 3)), DMA((2, 3)), DMA((2, 3)), DMA((2, 3, 4)),
            DMA((2,)), DMA((4,)), DMA((4,)), DMA((4,)), DMA((4,)),
        ],
        compiler_params=pltpu.CompilerParams(collective_id=0, has_side_effects=True, vmem_limit_bytes=VMEM_LIMIT),
        name="collect",
    )(*(pltpu.with_memory_space_constraint(value, pltpu.HBM) for value in (
        ham_diag, ham_coup, pattern, coulomb)))

    reduced, base = pl.pallas_call(
        chain_kernel,
        out_shape=(square, square),
        in_specs=[smem, vmem, vmem],
        out_specs=(vmem, vmem),
        scratch_shapes=[VMEM((width, width), F32)] * 9,
        compiler_params=pltpu.CompilerParams(vmem_limit_bytes=VMEM_LIMIT),
        name="chain",
    )(energies, diags, coups)

    spread, taken = pl.pallas_call(
        functools.partial(regroup_kernel, count),
        out_shape=(square, jax.ShapeDtypeStruct((count, lines, 128), F32)),
        in_specs=[vmem] * 4,
        out_specs=(vmem, vmem),
        scratch_shapes=[
            VMEM((width + 16, width), BF16), VMEM((count, 8, width), F32),
            VMEM((count, 8, width), F32), VMEM((count, lines, 128), F32),
        ] + [DMA((2,))] * 3,
        compiler_params=pltpu.CompilerParams(collective_id=1, has_side_effects=True, vmem_limit_bytes=VMEM_LIMIT),
        name="regroup",
    )(base, rows, slots, bare_pos)

    return pl.pallas_call(
        finish_kernel,
        out_shape=(
            jax.ShapeDtypeStruct((1, 1, width, width), F32),
            jax.ShapeDtypeStruct((count, 1, span), F32),
        ),
        in_specs=[vmem] * 5,
        out_specs=(vmem, vmem),
        scratch_shapes=[VMEM((width, width), F32)],
        compiler_params=pltpu.CompilerParams(vmem_limit_bytes=VMEM_LIMIT),
        name="finish",
    )(reduced, base, spread, taken, bare_own)


def solution(mesh):
    count, spaces = mesh.shape["energy"], mesh.shape["space"]
    return jax.shard_map(
        functools.partial(on_device, count, spaces),
        mesh=mesh,
        in_specs=(
            P("space", None, None),
            P("space", None, None),
            P("energy"),
            P("space", None),
            P("space", "energy"),
        ),
        out_specs=(P("energy", "space", None, None), P(None, "space", "energy")),
        check_vma=False,
    )
```

```python
import functools

import jax
import jax.numpy as jnp
from jax import lax
from jax.experimental import pallas as pl
from jax.experimental.pallas import tpu as pltpu
from jax.sharding import PartitionSpec as P

F32, BF16 = jnp.float32, jnp.bfloat16
MESH = pl.DeviceIdType.MESH
VMEM = pltpu.VMEM
DMA = pltpu.SemaphoreType.DMA

polar_coef = 128.0
sigma_coef = 0.5

TOLERANCE = 2e-5
VMEM_LIMIT = 20 << 20


def split(value):
    high = value.astype(BF16)
    return high, (value - high.astype(F32)).astype(BF16)


def dot(a, b):
    return jnp.dot(a, b, preferred_element_type=F32)


def dot_nt(a, b):
    return lax.dot_general(a, b, (((1,), (1,)), ((), ())), preferred_element_type=F32)


def mul(a, b):
    return dot(a[0], b[0]) + (dot(a[0], b[1]) + dot(a[1], b[0]))


def product(a, b):
    return mul(split(a), split(b))


def identity(width):
    rows = lax.broadcasted_iota(jnp.int32, (width, width), 0)
    cols = lax.broadcasted_iota(jnp.int32, (width, width), 1)
    return jnp.where(rows == cols, 1.0, 0.0).astype(F32)


def series(matrices, scales, doublings):
    ident = identity(matrices[0].shape[0])
    parts = [split(matrix) for matrix in matrices]
    squares = [mul(own, own) for own in parts]
    powers = [
        ident - matrix * (2.0 * scale) + square * (scale * scale)
        for matrix, scale, square in zip(matrices, scales, squares)
    ]
    guesses = [scale * (2.0 * ident - matrix * scale) for matrix, scale in zip(matrices, scales)]
    guesses = [guess + product(guess, power) for guess, power in zip(guesses, powers)]
    for _ in range(doublings - 1):
        highs = [power.astype(BF16) for power in powers]
        powers = [dot(high, high) for high in highs]
        guesses = [
            guess + dot(guess.astype(BF16), power.astype(BF16)) for guess, power in zip(guesses, powers)
        ]
    return guesses


def total_of(value):
    return jnp.sum(jnp.sum(value, axis=0, keepdims=True), axis=1, keepdims=True)


def mean_scale(matrix):
    trace = total_of(jnp.where(identity(matrix.shape[0]) > 0.0, matrix, 0.0))
    return trace / total_of(matrix * matrix)


def safe_scale(matrix):
    return 1.9 / jnp.max(jnp.sum(jnp.abs(matrix), axis=0, keepdims=True), axis=1, keepdims=True)


def eliminate(matrix, out_ref):
    width = matrix.shape[0]
    out_ref[...] = matrix
    lanes = lax.broadcasted_iota(jnp.int32, (1, width), 1)

    def step(pivot, carry):
        whole = out_ref[...]
        row = out_ref[pl.ds(pivot, 1), :]
        here = lanes == pivot
        value = jnp.sum(jnp.where(here, row, 0.0), axis=1, keepdims=True)
        column = jnp.sum(jnp.where(here, whole, 0.0), axis=1, keepdims=True)
        scaled = jnp.where(here, 1.0, row) / value
        out_ref[...] = jnp.where(here, 0.0, whole) - column * scaled
        out_ref[pl.ds(pivot, 1), :] = scaled
        return carry

    lax.fori_loop(0, width, step, 0)


def newton_step(parts, guesses):
    ident = identity(guesses[0].shape[0])
    split_guesses = [split(guess) for guess in guesses]
    residuals = [ident - mul(own, guess) for own, guess in zip(parts, split_guesses)]
    better = [
        guess + dot(guess_parts[0], residual.astype(BF16))
        for guess, guess_parts, residual in zip(guesses, split_guesses, residuals)
    ]
    return better, [residual * residual for residual in residuals]


def newton(matrices, refs, limit, worst=1.0):
    parts = [split(matrix) for matrix in matrices]

    def unsettled(carry):
        steps, last = carry
        return jnp.logical_and(last > TOLERANCE, steps < limit)

    def step(carry):
        better, squares = newton_step(parts, [ref[...] for ref in refs])
        largest = jnp.float32(0.0)
        for ref, value, square in zip(refs, better, squares):
            ref[...] = value
            largest = jnp.maximum(largest, jnp.sum(square))
        return carry[0] + 1, largest

    return lax.while_loop(unsettled, step, (jnp.int32(0), jnp.asarray(worst, F32)))[1]


def settle(matrices, refs, worst=1.0):
    worst = newton(matrices, refs, 8, worst)

    @pl.when(jnp.logical_not(worst <= TOLERANCE))
    def _():
        for matrix, ref in zip(matrices, refs):
            ref[...] = series([matrix], [safe_scale(matrix)], 5)[0]
        again = newton(matrices, refs, 48)

        @pl.when(jnp.logical_not(again <= TOLERANCE))
        def _():
            for matrix, ref in zip(matrices, refs):
                eliminate(matrix, ref)


def quick(matrices):
    guesses = series(matrices, [mean_scale(matrix) for matrix in matrices], 3)
    return newton_step([split(matrix) for matrix in matrices], guesses)


def peer_of(me, offset):
    core = lax.rem(me + offset, 2)
    y = lax.rem(me // 2 + offset // 2, 4)
    z = lax.rem(me // 8 + offset // 8, 4)
    return z * 8 + y * 2 + core


def peers_of(count, me):
    cores = [lax.rem(me + step, 2) for step in range(2)]
    ys = [lax.rem(me // 2 + step, 4) * 2 for step in range(4)]
    zs = [lax.rem(me // 8 + step, 4) * 8 for step in range(4)]
    return [zs[offset // 8] + ys[offset // 2 % 4] + cores[offset % 2] for offset in range(count - 1, 0, -1)]


def to_peer(peer, source, target, sems):
    return pltpu.make_async_remote_copy(
        src_ref=source, dst_ref=target, send_sem=sems.at[0], recv_sem=sems.at[1],
        device_id={"energy": peer}, device_id_type=MESH,
    )


def rows_of(ref, peer):
    return ref.at[pl.ds(pl.multiple_of(peer * 8, 8), 8), :]


def collect_kernel(
    count, spaces, diag_ref, coup_ref, pattern_ref, bare_ref,
    diags_ref, coups_ref, rows_ref, slots_ref, bare_pos_ref, bare_own_ref,
    pattern, bare_in, own_pattern, own_bare, scattered, from_core, by_y, from_y, by_z, from_z,
    own_sem, far_send, far_recv, near_send, near_recv, more_sems, core_sems, y_send, y_recv, z_send, z_recv,
):
    me = lax.axis_index("energy")
    place = lax.axis_index("space")
    width = diag_ref.shape[1]
    half = width // 2
    core = lax.rem(me, 2)
    other = me + 1 - 2 * core
    own_y = lax.rem(me // 2, 4)
    own_z = me // 8
    span = bare_ref.shape[1]
    chunk = own_bare.shape[1]
    sides = (lax.rem(place + 1, spaces), lax.rem(place + spaces - 1, spaces))
    across = lax.rem(place + 2, spaces)

    own_copies = [
        pltpu.make_async_copy(pattern_ref, pattern, own_sem.at[0]),
        pltpu.make_async_copy(bare_ref, bare_in, own_sem.at[1]),
        pltpu.make_async_copy(diag_ref.at[0], diags_ref.at[place], own_sem.at[2]),
        pltpu.make_async_copy(coup_ref.at[0], coups_ref.at[place], own_sem.at[3]),
    ]
    for copy in own_copies:
        copy.start()

    barrier = pltpu.get_barrier_semaphore()
    for side in sides:
        pl.semaphore_signal(barrier, inc=1, device_id={"space": side}, device_id_type=MESH)
    for step in (2, 1, 3):
        for stride in (2, 8):
            pl.semaphore_signal(
                barrier, inc=1, device_id={"energy": peer_of(me, step * stride)}, device_id_type=MESH)
    pl.semaphore_signal(barrier, inc=1, device_id={"energy": other}, device_id_type=MESH)

    pl.semaphore_wait(barrier, 9)
    own_half = pl.ds(pl.multiple_of(core * half, half), half)
    other_half = pl.ds(pl.multiple_of((1 - core) * half, half), half)
    given = (diag_ref, coup_ref)
    stores = (diags_ref, coups_ref)

    own_quarter = pl.ds(pl.multiple_of(half + core * (half // 2), half // 2), half // 2)
    other_quarter = pl.ds(pl.multiple_of(half + (1 - core) * (half // 2), half // 2), half // 2)

    class Pieces:
        def __init__(self, kind, source, store, part, quarter, sems, device):
            views = ((part,),) if kind else ((part, part), (quarter, pl.ds(0, half)))
            self.copies = [
                pltpu.make_async_remote_copy(
                    src_ref=source.at[view], dst_ref=store.at[view], send_sem=sems[0][at], recv_sem=sems[1][at],
                    device_id=device, device_id_type=MESH)
                for at, view in enumerate(views)
            ]

        def start(self):
            for copy in self.copies:
                copy.start()

        def wait_send(self):
            for copy in self.copies:
                copy.wait_send()

        def wait_recv(self):
            for copy in self.copies:
                copy.wait_recv()

    def far(way, stage):
        kind = (way, 1 - way, way)[stage]
        block = place if stage < 2 else sides[1 - way]
        store = stores[kind].at[block]
        source = given[kind].at[0] if stage < 2 else store
        sems = (
            (far_send.at[way, stage], more_sems.at[way, stage, 0]),
            (far_recv.at[way, stage], more_sems.at[way, stage, 1]),
        )
        return Pieces(kind, source, store, own_half, own_quarter, sems, {"space": sides[way]})

    def near(way, stage, own):
        kind = (way, 1 - way, way)[stage]
        block = sides[1 - way] if stage < 2 else across
        store = stores[kind].at[block]
        sems = (
            (near_send.at[way, stage], more_sems.at[way, stage, 2]),
            (near_recv.at[way, stage], more_sems.at[way, stage, 3]),
        )
        part, quarter = (own_half, own_quarter) if own else (other_half, other_quarter)
        return Pieces(kind, store, store, part, quarter, sems, {"energy": other})

    for stage in range(2):
        for way in range(2):
            far(way, stage).start()

    own_copies[0].wait()
    own_copies[1].wait()
    tail = chunk - 128
    for part in range(count):
        size = chunk if part < count - 1 else span
        if size < chunk:
            own_pattern[part, :, tail:] = jnp.zeros((1, 128), jnp.int32)
            rows_ref[part, :, tail:] = jnp.zeros((1, 128), jnp.int32)
            slots_ref[part, :, tail:] = jnp.zeros((1, 128), jnp.int32)
        piece = pattern[:, part * span:part * span + size]
        own_pattern[part, :, :size] = piece
        row = lax.shift_right_logical(piece, 8)
        col = jnp.bitwise_and(piece, 255)
        high = jnp.maximum(row, col)
        low = jnp.minimum(row, col)
        lower = low >= 128
        pivot = high == low
        rows_ref[part, :, :size] = jnp.where(jnp.logical_and(lower, jnp.logical_not(pivot)), low - 128, high)
        slots_ref[part, :, :size] = jnp.where(lower, jnp.where(pivot, 128, high - 128), low)
    own_bare[:, tail:] = jnp.zeros((1, 128), F32)
    own_bare[:, :span] = bare_in[...]

    mine = own_pattern[me]
    bare = own_bare[...]
    index = lax.broadcasted_iota(jnp.int32, (width, chunk), 0)
    on_row = index == lax.shift_right_logical(mine, 8)
    on_col = jnp.where(index == jnp.bitwise_and(mine, 255), 1.0, 0.0).astype(BF16)
    rest = bare
    total = None
    for _ in range(3):
        part = rest.astype(BF16).astype(F32)
        rest = rest - part
        term = dot_nt(jnp.where(on_row, part, 0.0).astype(BF16), on_col)
        total = term if total is None else total + term
    for peer in range(count):
        scattered[peer % 2, peer // 2 % 4, peer // 8] = total[peer * 8:peer * 8 + 8, :]
    for line in range(chunk // 128):
        bare_own_ref[line:line + 1, :] = bare[:, line * 128:(line + 1) * 128]
    for line in range(chunk // 128, bare_own_ref.shape[0]):
        bare_own_ref[line:line + 1, :] = jnp.zeros((1, 128), F32)

    to_core = pltpu.make_async_remote_copy(
        src_ref=scattered.at[1 - core], dst_ref=from_core,
        send_sem=core_sems.at[0], recv_sem=core_sems.at[1],
        device_id={"energy": other}, device_id_type=MESH)

    def to_y(step):
        return pltpu.make_async_remote_copy(
            src_ref=by_y.at[lax.rem(own_y + step, 4)], dst_ref=from_y.at[step],
            send_sem=y_send.at[step], recv_sem=y_recv.at[step],
            device_id={"energy": peer_of(me, 2 * step)}, device_id_type=MESH)

    def to_z(step):
        return pltpu.make_async_remote_copy(
            src_ref=by_z.at[lax.rem(own_z + step, 4)], dst_ref=from_z.at[step],
            send_sem=z_send.at[step], recv_sem=z_recv.at[step],
            device_id={"energy": peer_of(me, 8 * step)}, device_id_type=MESH)

    to_core.start()
    for way in range(2):
        far(way, 0).wait_recv()
        far(way, 2).start()
        near(way, 0, True).start()
    to_core.wait()
    for y in range(4):
        for z in range(4):
            by_y[y, z] = scattered[core, y, z] + from_core[y, z]
    for step in (2, 1, 3):
        to_y(step).start()
    for step in (1, 3, 2):
        to_y(step).wait()
    for z in range(4):
        by_z[z] = (by_y[own_y, z] + from_y[1, z]) + (from_y[2, z] + from_y[3, z])
    for step in (2, 1, 3):
        to_z(step).start()
    for stage in (1, 2):
        for way in range(2):
            far(way, stage).wait_recv()
            near(way, stage, True).start()
    for step in (1, 3, 2):
        to_z(step).wait()
    bare_pos_ref[...] = (by_z[own_z] + from_z[1]) + (from_z[2] + from_z[3])
    for copy in own_copies[2:]:
        copy.wait()
    for stage in range(3):
        for way in range(2):
            far(way, stage).wait_send()
            near(way, stage, True).wait_send()
            near(way, stage, False).wait_recv()


def chain_kernel(
    shift_ref, diags_ref, coups_ref, reduced_ref, base_ref,
    v_ref, vt_ref, w_ref, wt_ref, c_ref, ct_ref, last_ref, x_ref, y_ref,
):
    place = lax.axis_index("space")
    width = base_ref.shape[0]
    lead_parts = split(coups_ref[3])
    quarter = (
        dot_nt(lead_parts[0], lead_parts[0])
        + (dot_nt(lead_parts[0], lead_parts[1]) + dot_nt(lead_parts[1], lead_parts[0]))
    ) * 0.25

    def whole(block):
        half = width // 2
        left = diags_ref[block, :, :half]
        right = diags_ref[block, half:, half:]
        return jnp.concatenate([left, jnp.concatenate([left[half:].T, right], axis=0)], axis=1)

    last_ref[...] = whole(3) - quarter
    lower = place <= 1
    at_end = jnp.logical_or(place == 0, place == 3)

    def choose(block, flipped, ref, turned_ref):
        value = coups_ref[block]
        turned = value.T
        ref[...] = jnp.where(flipped, turned, value)
        turned_ref[...] = jnp.where(flipped, value, turned)

    first = jnp.where(place == 0, 1, jnp.where(place == 1, 0, jnp.where(place == 2, 3, 2)))
    second = jnp.where(lower, 3, 0)
    middle = jnp.where(lower, 2, 1)
    choose(1, jnp.logical_not(lower), c_ref, ct_ref)
    choose(jnp.where(lower, 2, 0), lower, v_ref, vt_ref)
    choose(jnp.where(lower, 0, 2), lax.rem(place, 2) == 0, w_ref, wt_ref)
    shift = identity(width) * shift_ref[0]

    def system(block):
        return jnp.where(block == 3, last_ref[...], whole(block)) + shift

    def run(solve):
        x, y = solve([system(first), system(second)], [x_ref, y_ref])
        x, y = split(x), split(y)
        wt_s, ut_s = split(wt_ref[...]), split(ct_ref[...])
        xw = split(mul(x, split(w_ref[...])))
        yv = split(mul(y, split(v_ref[...])))
        xu = split(mul(x, split(c_ref[...])))
        rest = system(place) - mul(wt_s, xw)
        inner = system(middle) - mul(split(vt_ref[...]), yv) - jnp.where(at_end, mul(ut_s, xu), 0.0)
        c = jnp.where(at_end, mul(wt_s, xu), c_ref[...])
        ct = jnp.where(at_end, mul(ut_s, xw), ct_ref[...])
        (z,) = solve([inner], [x_ref])
        reduced = rest - mul(split(product(c, z)), split(ct))
        reduced_ref[...] = reduced
        (base,) = solve([reduced], [base_ref])
        return base

    squares = []

    def solve_quickly(matrices, refs):
        inverses, residuals = quick(matrices)
        squares.extend(residuals)
        return inverses

    base_ref[...] = run(solve_quickly)
    worst = total_of(squares[0])
    for square in squares[1:]:
        worst = jnp.maximum(worst, total_of(square))
    worst = jnp.where(worst <= TOLERANCE, worst, 2.0 * TOLERANCE)

    @pl.when(jnp.logical_not(jnp.max(worst) <= TOLERANCE))
    def _():
        def solve_surely(matrices, refs):
            for matrix, ref in zip(matrices, refs):
                ref[...] = series([matrix], [mean_scale(matrix)], 3)[0]
            settle(matrices, refs)
            return [ref[...] for ref in refs]

        base_ref[...] = run(solve_surely)


def screen(samples, bare, scale):
    count = len(samples)
    result = []
    for lag in range(count):
        total = samples[0] * samples[lag]
        for m in range(1, count - lag):
            total = total + samples[m] * samples[m + lag]
        scaled = bare * (total * scale)
        result.append(bare * lax.rsqrt(1.0 + scaled * scaled))
    return result


PAIRS_FIRST = 2
PAIRS_SECOND = 9


def regroup_kernel(
    count, base_ref, rows_ref, slots_ref, bare_pos_ref, spread_ref, taken_ref,
    lhs, arrived, selfen, taken, sems_a, sems_b, sems_c,
):
    me = lax.axis_index("energy")
    width = base_ref.shape[0]
    half = width // 2
    chunk = rows_ref.shape[2]
    lines = taken.shape[1]
    pairs = count // 2
    for peer in range(count):
        taken_ref[peer, chunk // 128:, :] = jnp.zeros((lines - chunk // 128, 128), F32)

    barrier = pltpu.get_barrier_semaphore()

    others = peers_of(count, me)
    for peer in others:
        pl.semaphore_signal(barrier, inc=1, device_id={"energy": peer}, device_id_type=MESH)
    arrived[me] = rows_of(base_ref, me)[...]

    upper = base_ref[:half, :half]
    lower = base_ref[half:, half:]
    r = lax.broadcasted_iota(jnp.int32, (half, half), 0)
    c = lax.broadcasted_iota(jnp.int32, (half, half), 1)
    table = jnp.concatenate([jnp.where(r <= c, upper, lower), base_ref[:half, half:]], axis=1)
    diagonal = jnp.sum(jnp.where(r == c, lower, 0.0), axis=0, keepdims=True)
    extra = jnp.concatenate([jnp.zeros((1, half), F32), diagonal], axis=1)
    first = lax.broadcasted_iota(jnp.int32, (8, width), 0) == 0
    table = jnp.concatenate([table, jnp.where(first, extra, 0.0)], axis=0)
    tall = table.shape[0]
    high = table.astype(BF16).astype(F32)
    lhs[...] = jnp.concatenate([high, table - high], axis=0).astype(BF16)
    row_index = lax.broadcasted_iota(jnp.int32, (width, chunk), 0).astype(F32).astype(BF16)
    line_index = lax.broadcasted_iota(jnp.int32, (8, chunk), 0)
    one, none = jnp.bfloat16(1), jnp.bfloat16(0)

    def take(part):
        hot = jnp.where(row_index == rows_ref[part].astype(F32).astype(BF16), one, none)
        both = dot(lhs[...], hot)
        slots = slots_ref[part]
        group = jnp.broadcast_to(lax.shift_right_logical(slots, 3), (8, chunk))
        found, found_rest = both[:8], both[tall:tall + 8]
        for at in range(1, tall // 8):
            here = group == at
            found = jnp.where(here, both[at * 8:at * 8 + 8], found)
            found_rest = jnp.where(here, both[tall + at * 8:tall + at * 8 + 8], found_rest)
        here = line_index == jnp.bitwise_and(slots, 7)
        line = jnp.sum(jnp.where(here, found + found_rest, 0.0), axis=0, keepdims=True)
        for piece in range(chunk // 128):
            taken[part, piece:piece + 1, :] = line[:, piece * 128:(piece + 1) * 128]

    filled = chunk // 128

    def all_but_one(source, target, sems):
        return to_peer(others[0], source, target, sems)

    def take_pair(pair, carry):
        take(peer_of(me, count - 1 - 2 * pair))
        take(peer_of(me, count - 2 - 2 * pair))
        return carry

    def send_taken(peer):
        to_peer(peer, taken.at[peer, :filled], taken_ref.at[me, :filled], sems_c).start()

    def send_pair(pair, carry):
        for offset in (count - 1 - 2 * pair, count - 2 - 2 * pair):
            send_taken(peer_of(me, offset))
        return carry

    def take_and_send(pair, carry):
        take_pair(pair, carry)
        return send_pair(pair, carry)

    lax.fori_loop(0, PAIRS_FIRST, take_pair, 0)
    pl.semaphore_wait(barrier, count - 1)
    for peer in others:
        to_peer(peer, rows_of(base_ref, peer), arrived.at[me], sems_a).start()
    lax.fori_loop(0, PAIRS_FIRST, send_pair, 0)
    lax.fori_loop(PAIRS_FIRST, PAIRS_FIRST + PAIRS_SECOND, take_and_send, 0)
    rest = pl.ds(8, width - 8)
    first_exchange = all_but_one(base_ref.at[rest, :], arrived.at[pl.ds(1, count - 1)], sems_a)
    first_exchange.wait_send()
    first_exchange.wait_recv()

    scale = polar_coef * width / count
    for side in range(width // 128):
        cols = slice(side * 128, (side + 1) * 128)
        samples = [arrived[e, :, cols] for e in range(count)]
        screened = screen(samples, bare_pos_ref[:, cols], scale)
        for e in range(count):
            total = samples[e] * screened[0]
            for n in range(1, e + 1):
                total = total + samples[e - n] * screened[n]
            selfen[e, :, cols] = total * (sigma_coef / count)
    for peer in others:
        to_peer(peer, selfen.at[peer], rows_of(spread_ref, me), sems_b).start()
    lax.fori_loop(PAIRS_FIRST + PAIRS_SECOND, pairs - 1, take_and_send, 0)
    take_pair(pairs - 1, 0)
    send_taken(peer_of(me, 1))
    taken_ref[me, :filled] = taken[me, :filled]
    spread_ref[pl.ds(pl.multiple_of(me * 8, 8), 8), :] = selfen[me]
    for last_exchange in (
        all_but_one(selfen.at[pl.ds(1, count - 1)], spread_ref.at[rest, :], sems_b),
        all_but_one(taken.at[pl.ds(1, count - 1), :filled], taken_ref.at[pl.ds(1, count - 1), :filled], sems_c),
    ):
        last_exchange.wait_send()
        last_exchange.wait_recv()


def finish_kernel(reduced_ref, base_ref, spread_ref, taken_ref, bare_ref, green_ref, screened_ref, x_ref):
    count = taken_ref.shape[0]
    width = base_ref.shape[0]
    chunk = screened_ref.shape[2]
    spread = spread_ref[...]
    matrix = reduced_ref[...] - 0.5 * (spread + spread.T)
    parts = split(matrix)
    base = base_ref[...]
    base_parts = split(base)
    residual = identity(width) - mul(parts, base_parts)
    near = residual.astype(BF16)
    guess = base + dot(base_parts[0], (residual + dot(near, near)).astype(BF16))
    (better,), (square,) = newton_step([parts], [guess])
    x_ref[...] = better

    scale = polar_coef * width / count
    for group in range(taken_ref.shape[1] // 8):
        at = slice(group * 8, group * 8 + 8)
        samples = [taken_ref[e, at, :] for e in range(count)]
        screened = screen(samples, bare_ref[at, :], scale)
        for line in range(group * 8, min(group * 8 + 8, pl.cdiv(chunk, 128))):
            start = line * 128
            stop = min(start + 128, chunk)
            for n in range(count):
                row = line - group * 8
                screened_ref[n, :, start:stop] = screened[n][row:row + 1, :stop - start]

    settle([matrix], [x_ref], jnp.sum(square))
    green_ref[0, 0] = x_ref[...]


def on_device(count, spaces, ham_diag, ham_coup, energies, pattern, coulomb):
    width = ham_diag.shape[1]
    span = coulomb.shape[1]
    chunk = pl.cdiv(span, 128) * 128
    lines = pl.cdiv(chunk // 128, 8) * 8
    vmem = pl.BlockSpec(memory_space=pltpu.VMEM)
    hbm = pl.BlockSpec(memory_space=pltpu.HBM)
    smem = pl.BlockSpec(memory_space=pltpu.SMEM)
    square = jax.ShapeDtypeStruct((width, width), F32)
    diags, coups, rows, slots, bare_pos, bare_own = pl.pallas_call(
        functools.partial(collect_kernel, count, spaces),
        out_shape=(
            jax.ShapeDtypeStruct((spaces, width, width), F32),
            jax.ShapeDtypeStruct((spaces, width, width), F32),
            jax.ShapeDtypeStruct((count, 1, chunk), jnp.int32),
            jax.ShapeDtypeStruct((count, 1, chunk), jnp.int32),
            jax.ShapeDtypeStruct((8, width), F32),
            jax.ShapeDtypeStruct((lines, 128), F32),
        ),
        in_specs=[hbm] * 4,
        out_specs=(vmem,) * 6,
        scratch_shapes=[
            VMEM((1, pattern.shape[1]), jnp.int32), VMEM((1, span), F32),
            VMEM((count, 1, chunk), jnp.int32), VMEM((1, chunk), F32),
            VMEM((2, 4, 4, 8, width), F32), VMEM((4, 4, 8, width), F32), VMEM((4, 4, 8, width), F32),
            VMEM((4, 4, 8, width), F32), VMEM((4, 8, width), F32), VMEM((4, 8, width), F32),
            DMA((4,)), DMA((2, 3)), DMA((2, 3)), DMA((2, 3)), DMA((2, 3)), DMA((2, 3, 4)),
            DMA((2,)), DMA((4,)), DMA((4,)), DMA((4,)), DMA((4,)),
        ],
        compiler_params=pltpu.CompilerParams(collective_id=0, has_side_effects=True, vmem_limit_bytes=VMEM_LIMIT),
        name="collect",
    )(*(pltpu.with_memory_space_constraint(value, pltpu.HBM) for value in (
        ham_diag, ham_coup, pattern, coulomb)))

    reduced, base = pl.pallas_call(
        chain_kernel,
        out_shape=(square, square),
        in_specs=[smem, vmem, vmem],
        out_specs=(vmem, vmem),
        scratch_shapes=[VMEM((width, width), F32)] * 9,
        compiler_params=pltpu.CompilerParams(vmem_limit_bytes=VMEM_LIMIT),
        name="chain",
    )(energies, diags, coups)

    spread, taken = pl.pallas_call(
        functools.partial(regroup_kernel, count),
        out_shape=(square, jax.ShapeDtypeStruct((count, lines, 128), F32)),
        in_specs=[vmem] * 4,
        out_specs=(vmem, vmem),
        scratch_shapes=[
            VMEM((width + 16, width), BF16), VMEM((count, 8, width), F32),
            VMEM((count, 8, width), F32), VMEM((count, lines, 128), F32),
        ] + [DMA((2,))] * 3,
        compiler_params=pltpu.CompilerParams(collective_id=1, has_side_effects=True, vmem_limit_bytes=VMEM_LIMIT),
        name="regroup",
    )(base, rows, slots, bare_pos)

    return pl.pallas_call(
        finish_kernel,
        out_shape=(
            jax.ShapeDtypeStruct((1, 1, width, width), F32),
            jax.ShapeDtypeStruct((count, 1, span), F32),
        ),
        in_specs=[vmem] * 5,
        out_specs=(vmem, vmem),
        scratch_shapes=[VMEM((width, width), F32)],
        compiler_params=pltpu.CompilerParams(vmem_limit_bytes=VMEM_LIMIT),
        name="finish",
    )(reduced, base, spread, taken, bare_own)


def solution(mesh):
    count, spaces = mesh.shape["energy"], mesh.shape["space"]
    return jax.shard_map(
        functools.partial(on_device, count, spaces),
        mesh=mesh,
        in_specs=(
            P("space", None, None),
            P("space", None, None),
            P("energy"),
            P("space", None),
            P("space", "energy"),
        ),
        out_specs=(P("energy", "space", None, None), P(None, "space", "energy")),
        check_vma=False,
    )
```

```python
import functools

import jax
import jax.numpy as jnp
from jax import lax
from jax.experimental import pallas as pl
from jax.experimental.pallas import tpu as pltpu
from jax.sharding import PartitionSpec as P

F32, BF16 = jnp.float32, jnp.bfloat16
MESH = pl.DeviceIdType.MESH
VMEM = pltpu.VMEM
DMA = pltpu.SemaphoreType.DMA

polar_coef = 128.0
sigma_coef = 0.5

TOLERANCE = 2e-5
VMEM_LIMIT = 20 << 20


def split(value):
    high = value.astype(BF16)
    return high, (value - high.astype(F32)).astype(BF16)


def dot(a, b):
    return jnp.dot(a, b, preferred_element_type=F32)


def dot_nt(a, b):
    return lax.dot_general(a, b, (((1,), (1,)), ((), ())), preferred_element_type=F32)


def mul(a, b):
    return dot(a[0], b[0]) + (dot(a[0], b[1]) + dot(a[1], b[0]))


def product(a, b):
    return mul(split(a), split(b))


def identity(width):
    rows = lax.broadcasted_iota(jnp.int32, (width, width), 0)
    cols = lax.broadcasted_iota(jnp.int32, (width, width), 1)
    return jnp.where(rows == cols, 1.0, 0.0).astype(F32)


def series(matrices, scales, doublings):
    ident = identity(matrices[0].shape[0])
    parts = [split(matrix) for matrix in matrices]
    squares = [mul(own, own) for own in parts]
    powers = [
        ident - matrix * (2.0 * scale) + square * (scale * scale)
        for matrix, scale, square in zip(matrices, scales, squares)
    ]
    guesses = [scale * (2.0 * ident - matrix * scale) for matrix, scale in zip(matrices, scales)]
    guesses = [guess + product(guess, power) for guess, power in zip(guesses, powers)]
    for _ in range(doublings - 1):
        highs = [power.astype(BF16) for power in powers]
        powers = [dot(high, high) for high in highs]
        guesses = [
            guess + dot(guess.astype(BF16), power.astype(BF16)) for guess, power in zip(guesses, powers)
        ]
    return guesses


def total_of(value):
    return jnp.sum(jnp.sum(value, axis=0, keepdims=True), axis=1, keepdims=True)


def mean_scale(matrix):
    trace = total_of(jnp.where(identity(matrix.shape[0]) > 0.0, matrix, 0.0))
    return trace / total_of(matrix * matrix)


def safe_scale(matrix):
    return 1.9 / jnp.max(jnp.sum(jnp.abs(matrix), axis=0, keepdims=True), axis=1, keepdims=True)


def eliminate(matrix, out_ref):
    width = matrix.shape[0]
    out_ref[...] = matrix
    lanes = lax.broadcasted_iota(jnp.int32, (1, width), 1)

    def step(pivot, carry):
        whole = out_ref[...]
        row = out_ref[pl.ds(pivot, 1), :]
        here = lanes == pivot
        value = jnp.sum(jnp.where(here, row, 0.0), axis=1, keepdims=True)
        column = jnp.sum(jnp.where(here, whole, 0.0), axis=1, keepdims=True)
        scaled = jnp.where(here, 1.0, row) / value
        out_ref[...] = jnp.where(here, 0.0, whole) - column * scaled
        out_ref[pl.ds(pivot, 1), :] = scaled
        return carry

    lax.fori_loop(0, width, step, 0)


def newton_step(parts, guesses):
    ident = identity(guesses[0].shape[0])
    split_guesses = [split(guess) for guess in guesses]
    residuals = [ident - mul(own, guess) for own, guess in zip(parts, split_guesses)]
    better = [
        guess + dot(guess_parts[0], residual.astype(BF16))
        for guess, guess_parts, residual in zip(guesses, split_guesses, residuals)
    ]
    return better, [residual * residual for residual in residuals]


def newton(matrices, refs, limit, worst=1.0):
    parts = [split(matrix) for matrix in matrices]

    def unsettled(carry):
        steps, last = carry
        return jnp.logical_and(last > TOLERANCE, steps < limit)

    def step(carry):
        better, squares = newton_step(parts, [ref[...] for ref in refs])
        largest = jnp.float32(0.0)
        for ref, value, square in zip(refs, better, squares):
            ref[...] = value
            largest = jnp.maximum(largest, jnp.sum(square))
        return carry[0] + 1, largest

    return lax.while_loop(unsettled, step, (jnp.int32(0), jnp.asarray(worst, F32)))[1]


def settle(matrices, refs, worst=1.0):
    worst = newton(matrices, refs, 8, worst)

    @pl.when(jnp.logical_not(worst <= TOLERANCE))
    def _():
        for matrix, ref in zip(matrices, refs):
            ref[...] = series([matrix], [safe_scale(matrix)], 5)[0]
        again = newton(matrices, refs, 48)

        @pl.when(jnp.logical_not(again <= TOLERANCE))
        def _():
            for matrix, ref in zip(matrices, refs):
                eliminate(matrix, ref)


def quick(matrices):
    guesses = series(matrices, [mean_scale(matrix) for matrix in matrices], 3)
    return newton_step([split(matrix) for matrix in matrices], guesses)


def peer_of(me, offset):
    core = lax.rem(me + offset, 2)
    y = lax.rem(me // 2 + offset // 2, 4)
    z = lax.rem(me // 8 + offset // 8, 4)
    return z * 8 + y * 2 + core


def peers_of(count, me):
    cores = [lax.rem(me + step, 2) for step in range(2)]
    ys = [lax.rem(me // 2 + step, 4) * 2 for step in range(4)]
    zs = [lax.rem(me // 8 + step, 4) * 8 for step in range(4)]
    return [zs[offset // 8] + ys[offset // 2 % 4] + cores[offset % 2] for offset in range(count - 1, 0, -1)]


def to_peer(peer, source, target, sems):
    return pltpu.make_async_remote_copy(
        src_ref=source, dst_ref=target, send_sem=sems.at[0], recv_sem=sems.at[1],
        device_id={"energy": peer}, device_id_type=MESH,
    )


def rows_of(ref, peer):
    return ref.at[pl.ds(pl.multiple_of(peer * 8, 8), 8), :]


def collect_kernel(
    count, spaces, diag_ref, coup_ref, pattern_ref, bare_ref,
    diags_ref, coups_ref, rows_ref, slots_ref, bare_pos_ref, bare_own_ref,
    pattern, bare_in, own_pattern, own_bare, scattered, from_core, by_y, from_y, by_z, from_z,
    own_sem, far_send, far_recv, near_send, near_recv, more_sems, core_sems, y_send, y_recv, z_send, z_recv,
):
    me = lax.axis_index("energy")
    place = lax.axis_index("space")
    width = diag_ref.shape[1]
    half = width // 2
    core = lax.rem(me, 2)
    other = me + 1 - 2 * core
    own_y = lax.rem(me // 2, 4)
    own_z = me // 8
    span = bare_ref.shape[1]
    chunk = own_bare.shape[1]
    sides = (lax.rem(place + 1, spaces), lax.rem(place + spaces - 1, spaces))
    across = lax.rem(place + 2, spaces)

    own_copies = [
        pltpu.make_async_copy(pattern_ref, pattern, own_sem.at[0]),
        pltpu.make_async_copy(bare_ref, bare_in, own_sem.at[1]),
        pltpu.make_async_copy(diag_ref.at[0], diags_ref.at[place], own_sem.at[2]),
        pltpu.make_async_copy(coup_ref.at[0], coups_ref.at[place], own_sem.at[3]),
    ]
    for copy in own_copies:
        copy.start()

    barrier = pltpu.get_barrier_semaphore()
    for side in sides:
        pl.semaphore_signal(barrier, inc=1, device_id={"space": side}, device_id_type=MESH)
    for step in (2, 1, 3):
        for stride in (2, 8):
            pl.semaphore_signal(
                barrier, inc=1, device_id={"energy": peer_of(me, step * stride)}, device_id_type=MESH)
    pl.semaphore_signal(barrier, inc=1, device_id={"energy": other}, device_id_type=MESH)

    own_copies[0].wait()
    own_copies[1].wait()
    tail = chunk - 128
    for part in range(count):
        size = chunk if part < count - 1 else span
        if size < chunk:
            own_pattern[part, :, tail:] = jnp.zeros((1, 128), jnp.int32)
            rows_ref[part, :, tail:] = jnp.zeros((1, 128), jnp.int32)
            slots_ref[part, :, tail:] = jnp.zeros((1, 128), jnp.int32)
        piece = pattern[:, part * span:part * span + size]
        own_pattern[part, :, :size] = piece
        row = lax.shift_right_logical(piece, 8)
        col = jnp.bitwise_and(piece, 255)
        high = jnp.maximum(row, col)
        low = jnp.minimum(row, col)
        lower = low >= 128
        pivot = high == low
        rows_ref[part, :, :size] = jnp.where(jnp.logical_and(lower, jnp.logical_not(pivot)), low - 128, high)
        slots_ref[part, :, :size] = jnp.where(lower, jnp.where(pivot, 128, high - 128), low)
    own_bare[:, tail:] = jnp.zeros((1, 128), F32)
    own_bare[:, :span] = bare_in[...]

    pl.semaphore_wait(barrier, 9)
    own_half = pl.ds(pl.multiple_of(core * half, half), half)
    other_half = pl.ds(pl.multiple_of((1 - core) * half, half), half)
    given = (diag_ref, coup_ref)
    stores = (diags_ref, coups_ref)

    own_quarter = pl.ds(pl.multiple_of(half + core * (half // 2), half // 2), half // 2)
    other_quarter = pl.ds(pl.multiple_of(half + (1 - core) * (half // 2), half // 2), half // 2)

    class Pieces:
        def __init__(self, kind, source, store, part, quarter, sems, device):
            views = ((part,),) if kind else ((part, part), (quarter, pl.ds(0, half)))
            self.copies = [
                pltpu.make_async_remote_copy(
                    src_ref=source.at[view], dst_ref=store.at[view], send_sem=sems[0][at], recv_sem=sems[1][at],
                    device_id=device, device_id_type=MESH)
                for at, view in enumerate(views)
            ]

        def start(self):
            for copy in self.copies:
                copy.start()

        def wait_send(self):
            for copy in self.copies:
                copy.wait_send()

        def wait_recv(self):
            for copy in self.copies:
                copy.wait_recv()

    def far(way, stage):
        kind = (way, 1 - way, way)[stage]
        block = place if stage < 2 else sides[1 - way]
        store = stores[kind].at[block]
        source = given[kind].at[0] if stage < 2 else store
        sems = (
            (far_send.at[way, stage], more_sems.at[way, stage, 0]),
            (far_recv.at[way, stage], more_sems.at[way, stage, 1]),
        )
        return Pieces(kind, source, store, own_half, own_quarter, sems, {"space": sides[way]})

    def near(way, stage, own):
        kind = (way, 1 - way, way)[stage]
        block = sides[1 - way] if stage < 2 else across
        store = stores[kind].at[block]
        sems = (
            (near_send.at[way, stage], more_sems.at[way, stage, 2]),
            (near_recv.at[way, stage], more_sems.at[way, stage, 3]),
        )
        part, quarter = (own_half, own_quarter) if own else (other_half, other_quarter)
        return Pieces(kind, store, store, part, quarter, sems, {"energy": other})

    for stage in range(2):
        for way in range(2):
            far(way, stage).start()

    mine = own_pattern[me]
    bare = own_bare[...]
    index = lax.broadcasted_iota(jnp.int32, (width, chunk), 0)
    on_row = index == lax.shift_right_logical(mine, 8)
    on_col = jnp.where(index == jnp.bitwise_and(mine, 255), 1.0, 0.0).astype(BF16)
    rest = bare
    total = None
    for _ in range(3):
        part = rest.astype(BF16).astype(F32)
        rest = rest - part
        term = dot_nt(jnp.where(on_row, part, 0.0).astype(BF16), on_col)
        total = term if total is None else total + term
    for peer in range(count):
        scattered[peer % 2, peer // 2 % 4, peer // 8] = total[peer * 8:peer * 8 + 8, :]
    for line in range(chunk // 128):
        bare_own_ref[line:line + 1, :] = bare[:, line * 128:(line + 1) * 128]
    for line in range(chunk // 128, bare_own_ref.shape[0]):
        bare_own_ref[line:line + 1, :] = jnp.zeros((1, 128), F32)

    to_core = pltpu.make_async_remote_copy(
        src_ref=scattered.at[1 - core], dst_ref=from_core,
        send_sem=core_sems.at[0], recv_sem=core_sems.at[1],
        device_id={"energy": other}, device_id_type=MESH)

    def to_y(step):
        return pltpu.make_async_remote_copy(
            src_ref=by_y.at[lax.rem(own_y + step, 4)], dst_ref=from_y.at[step],
            send_sem=y_send.at[step], recv_sem=y_recv.at[step],
            device_id={"energy": peer_of(me, 2 * step)}, device_id_type=MESH)

    def to_z(step):
        return pltpu.make_async_remote_copy(
            src_ref=by_z.at[lax.rem(own_z + step, 4)], dst_ref=from_z.at[step],
            send_sem=z_send.at[step], recv_sem=z_recv.at[step],
            device_id={"energy": peer_of(me, 8 * step)}, device_id_type=MESH)

    to_core.start()
    for way in range(2):
        far(way, 0).wait_recv()
        far(way, 2).start()
        near(way, 0, True).start()
    to_core.wait()
    for y in range(4):
        for z in range(4):
            by_y[y, z] = scattered[core, y, z] + from_core[y, z]
    for step in (2, 1, 3):
        to_y(step).start()
    for step in (1, 3, 2):
        to_y(step).wait()
    for z in range(4):
        by_z[z] = (by_y[own_y, z] + from_y[1, z]) + (from_y[2, z] + from_y[3, z])
    for step in (2, 1, 3):
        to_z(step).start()
    for stage in (1, 2):
        for way in range(2):
            far(way, stage).wait_recv()
            near(way, stage, True).start()
    for step in (1, 3, 2):
        to_z(step).wait()
    bare_pos_ref[...] = (by_z[own_z] + from_z[1]) + (from_z[2] + from_z[3])
    for copy in own_copies[2:]:
        copy.wait()
    for stage in range(3):
        for way in range(2):
            far(way, stage).wait_send()
            near(way, stage, True).wait_send()
            near(way, stage, False).wait_recv()


def chain_kernel(
    shift_ref, diags_ref, coups_ref, reduced_ref, base_ref,
    v_ref, vt_ref, w_ref, wt_ref, c_ref, ct_ref, last_ref, x_ref, y_ref,
):
    place = lax.axis_index("space")
    width = base_ref.shape[0]
    lead_parts = split(coups_ref[3])
    quarter = (
        dot_nt(lead_parts[0], lead_parts[0])
        + (dot_nt(lead_parts[0], lead_parts[1]) + dot_nt(lead_parts[1], lead_parts[0]))
    ) * 0.25

    def whole(block):
        half = width // 2
        left = diags_ref[block, :, :half]
        right = diags_ref[block, half:, half:]
        return jnp.concatenate([left, jnp.concatenate([left[half:].T, right], axis=0)], axis=1)

    last_ref[...] = whole(3) - quarter
    lower = place <= 1
    at_end = jnp.logical_or(place == 0, place == 3)

    def choose(block, flipped, ref, turned_ref):
        value = coups_ref[block]
        turned = value.T
        ref[...] = jnp.where(flipped, turned, value)
        turned_ref[...] = jnp.where(flipped, value, turned)

    first = jnp.where(place == 0, 1, jnp.where(place == 1, 0, jnp.where(place == 2, 3, 2)))
    second = jnp.where(lower, 3, 0)
    middle = jnp.where(lower, 2, 1)
    choose(1, jnp.logical_not(lower), c_ref, ct_ref)
    choose(jnp.where(lower, 2, 0), lower, v_ref, vt_ref)
    choose(jnp.where(lower, 0, 2), lax.rem(place, 2) == 0, w_ref, wt_ref)
    shift = identity(width) * shift_ref[0]

    def system(block):
        return jnp.where(block == 3, last_ref[...], whole(block)) + shift

    def run(solve):
        x, y = solve([system(first), system(second)], [x_ref, y_ref])
        x, y = split(x), split(y)
        wt_s, ut_s = split(wt_ref[...]), split(ct_ref[...])
        xw = split(mul(x, split(w_ref[...])))
        yv = split(mul(y, split(v_ref[...])))
        xu = split(mul(x, split(c_ref[...])))
        rest = system(place) - mul(wt_s, xw)
        inner = system(middle) - mul(split(vt_ref[...]), yv) - jnp.where(at_end, mul(ut_s, xu), 0.0)
        c = jnp.where(at_end, mul(wt_s, xu), c_ref[...])
        ct = jnp.where(at_end, mul(ut_s, xw), ct_ref[...])
        (z,) = solve([inner], [x_ref])
        reduced = rest - mul(split(product(c, z)), split(ct))
        reduced_ref[...] = reduced
        (base,) = solve([reduced], [base_ref])
        return base

    squares = []

    def solve_quickly(matrices, refs):
        inverses, residuals = quick(matrices)
        squares.extend(residuals)
        return inverses

    base_ref[...] = run(solve_quickly)
    worst = total_of(squares[0])
    for square in squares[1:]:
        worst = jnp.maximum(worst, total_of(square))
    worst = jnp.where(worst <= TOLERANCE, worst, 2.0 * TOLERANCE)

    @pl.when(jnp.logical_not(jnp.max(worst) <= TOLERANCE))
    def _():
        def solve_surely(matrices, refs):
            for matrix, ref in zip(matrices, refs):
                ref[...] = series([matrix], [mean_scale(matrix)], 3)[0]
            settle(matrices, refs)
            return [ref[...] for ref in refs]

        base_ref[...] = run(solve_surely)


def screen(samples, bare, scale):
    count = len(samples)
    result = []
    for lag in range(count):
        total = samples[0] * samples[lag]
        for m in range(1, count - lag):
            total = total + samples[m] * samples[m + lag]
        scaled = bare * (total * scale)
        result.append(bare * lax.rsqrt(1.0 + scaled * scaled))
    return result


PAIRS_FIRST = 2
PAIRS_SECOND = 9


def regroup_kernel(
    count, base_ref, rows_ref, slots_ref, bare_pos_ref, spread_ref, taken_ref,
    lhs, arrived, selfen, taken, sems_a, sems_b, sems_c,
):
    me = lax.axis_index("energy")
    width = base_ref.shape[0]
    half = width // 2
    chunk = rows_ref.shape[2]
    lines = taken.shape[1]
    pairs = count // 2
    for peer in range(count):
        taken_ref[peer, chunk // 128:, :] = jnp.zeros((lines - chunk // 128, 128), F32)

    barrier = pltpu.get_barrier_semaphore()

    others = peers_of(count, me)
    for peer in others:
        pl.semaphore_signal(barrier, inc=1, device_id={"energy": peer}, device_id_type=MESH)
    arrived[me] = rows_of(base_ref, me)[...]

    upper = base_ref[:half, :half]
    lower = base_ref[half:, half:]
    r = lax.broadcasted_iota(jnp.int32, (half, half), 0)
    c = lax.broadcasted_iota(jnp.int32, (half, half), 1)
    table = jnp.concatenate([jnp.where(r <= c, upper, lower), base_ref[:half, half:]], axis=1)
    diagonal = jnp.sum(jnp.where(r == c, lower, 0.0), axis=0, keepdims=True)
    extra = jnp.concatenate([jnp.zeros((1, half), F32), diagonal], axis=1)
    first = lax.broadcasted_iota(jnp.int32, (8, width), 0) == 0
    table = jnp.concatenate([table, jnp.where(first, extra, 0.0)], axis=0)
    tall = table.shape[0]
    high = table.astype(BF16).astype(F32)
    lhs[...] = jnp.concatenate([high, table - high], axis=0).astype(BF16)
    row_index = lax.broadcasted_iota(jnp.int32, (width, chunk), 0).astype(F32).astype(BF16)
    line_index = lax.broadcasted_iota(jnp.int32, (8, chunk), 0)
    one, none = jnp.bfloat16(1), jnp.bfloat16(0)

    def take(part):
        hot = jnp.where(row_index == rows_ref[part].astype(F32).astype(BF16), one, none)
        both = dot(lhs[...], hot)
        slots = slots_ref[part]
        group = jnp.broadcast_to(lax.shift_right_logical(slots, 3), (8, chunk))
        found, found_rest = both[:8], both[tall:tall + 8]
        for at in range(1, tall // 8):
            here = group == at
            found = jnp.where(here, both[at * 8:at * 8 + 8], found)
            found_rest = jnp.where(here, both[tall + at * 8:tall + at * 8 + 8], found_rest)
        here = line_index == jnp.bitwise_and(slots, 7)
        line = jnp.sum(jnp.where(here, found + found_rest, 0.0), axis=0, keepdims=True)
        for piece in range(chunk // 128):
            taken[part, piece:piece + 1, :] = line[:, piece * 128:(piece + 1) * 128]

    filled = chunk // 128

    def all_but_one(source, target, sems):
        return to_peer(others[0], source, target, sems)

    def take_pair(pair, carry):
        take(peer_of(me, count - 1 - 2 * pair))
        take(peer_of(me, count - 2 - 2 * pair))
        return carry

    def send_taken(peer):
        to_peer(peer, taken.at[peer, :filled], taken_ref.at[me, :filled], sems_c).start()

    def send_pair(pair, carry):
        for offset in (count - 1 - 2 * pair, count - 2 - 2 * pair):
            send_taken(peer_of(me, offset))
        return carry

    def take_and_send(pair, carry):
        take_pair(pair, carry)
        return send_pair(pair, carry)

    lax.fori_loop(0, PAIRS_FIRST, take_pair, 0)
    pl.semaphore_wait(barrier, count - 1)
    for peer in others:
        to_peer(peer, rows_of(base_ref, peer), arrived.at[me], sems_a).start()
    lax.fori_loop(0, PAIRS_FIRST, send_pair, 0)
    lax.fori_loop(PAIRS_FIRST, PAIRS_FIRST + PAIRS_SECOND, take_and_send, 0)
    rest = pl.ds(8, width - 8)
    first_exchange = all_but_one(base_ref.at[rest, :], arrived.at[pl.ds(1, count - 1)], sems_a)
    first_exchange.wait_send()
    first_exchange.wait_recv()

    scale = polar_coef * width / count
    for side in range(width // 128):
        cols = slice(side * 128, (side + 1) * 128)
        samples = [arrived[e, :, cols] for e in range(count)]
        screened = screen(samples, bare_pos_ref[:, cols], scale)
        for e in range(count):
            total = samples[e] * screened[0]
            for n in range(1, e + 1):
                total = total + samples[e - n] * screened[n]
            selfen[e, :, cols] = total * (sigma_coef / count)
        for peer in others:
            to_peer(
                peer, selfen.at[peer, :, cols],
                spread_ref.at[pl.ds(pl.multiple_of(me * 8, 8), 8), cols], sems_b).start()
    lax.fori_loop(PAIRS_FIRST + PAIRS_SECOND, pairs - 1, take_and_send, 0)
    take_pair(pairs - 1, 0)
    send_taken(peer_of(me, 1))
    taken_ref[me, :filled] = taken[me, :filled]
    spread_ref[pl.ds(pl.multiple_of(me * 8, 8), 8), :] = selfen[me]
    for last_exchange in (
        all_but_one(selfen.at[pl.ds(1, count - 1)], spread_ref.at[rest, :], sems_b),
        all_but_one(taken.at[pl.ds(1, count - 1), :filled], taken_ref.at[pl.ds(1, count - 1), :filled], sems_c),
    ):
        last_exchange.wait_send()
        last_exchange.wait_recv()


def finish_kernel(reduced_ref, base_ref, spread_ref, taken_ref, bare_ref, green_ref, screened_ref, x_ref):
    count = taken_ref.shape[0]
    width = base_ref.shape[0]
    chunk = screened_ref.shape[2]
    spread = spread_ref[...]
    matrix = reduced_ref[...] - 0.5 * (spread + spread.T)
    parts = split(matrix)
    base = base_ref[...]
    base_parts = split(base)
    residual = identity(width) - mul(parts, base_parts)
    near = residual.astype(BF16)
    guess = base + dot(base_parts[0], (residual + dot(near, near)).astype(BF16))
    (better,), (square,) = newton_step([parts], [guess])
    x_ref[...] = better

    scale = polar_coef * width / count
    for group in range(taken_ref.shape[1] // 8):
        at = slice(group * 8, group * 8 + 8)
        samples = [taken_ref[e, at, :] for e in range(count)]
        screened = screen(samples, bare_ref[at, :], scale)
        for line in range(group * 8, min(group * 8 + 8, pl.cdiv(chunk, 128))):
            start = line * 128
            stop = min(start + 128, chunk)
            for n in range(count):
                row = line - group * 8
                screened_ref[n, :, start:stop] = screened[n][row:row + 1, :stop - start]

    settle([matrix], [x_ref], jnp.sum(square))
    green_ref[0, 0] = x_ref[...]


def on_device(count, spaces, ham_diag, ham_coup, energies, pattern, coulomb):
    width = ham_diag.shape[1]
    span = coulomb.shape[1]
    chunk = pl.cdiv(span, 128) * 128
    lines = pl.cdiv(chunk // 128, 8) * 8
    vmem = pl.BlockSpec(memory_space=pltpu.VMEM)
    hbm = pl.BlockSpec(memory_space=pltpu.HBM)
    smem = pl.BlockSpec(memory_space=pltpu.SMEM)
    square = jax.ShapeDtypeStruct((width, width), F32)
    diags, coups, rows, slots, bare_pos, bare_own = pl.pallas_call(
        functools.partial(collect_kernel, count, spaces),
        out_shape=(
            jax.ShapeDtypeStruct((spaces, width, width), F32),
            jax.ShapeDtypeStruct((spaces, width, width), F32),
            jax.ShapeDtypeStruct((count, 1, chunk), jnp.int32),
            jax.ShapeDtypeStruct((count, 1, chunk), jnp.int32),
            jax.ShapeDtypeStruct((8, width), F32),
            jax.ShapeDtypeStruct((lines, 128), F32),
        ),
        in_specs=[hbm] * 4,
        out_specs=(vmem,) * 6,
        scratch_shapes=[
            VMEM((1, pattern.shape[1]), jnp.int32), VMEM((1, span), F32),
            VMEM((count, 1, chunk), jnp.int32), VMEM((1, chunk), F32),
            VMEM((2, 4, 4, 8, width), F32), VMEM((4, 4, 8, width), F32), VMEM((4, 4, 8, width), F32),
            VMEM((4, 4, 8, width), F32), VMEM((4, 8, width), F32), VMEM((4, 8, width), F32),
            DMA((4,)), DMA((2, 3)), DMA((2, 3)), DMA((2, 3)), DMA((2, 3)), DMA((2, 3, 4)),
            DMA((2,)), DMA((4,)), DMA((4,)), DMA((4,)), DMA((4,)),
        ],
        compiler_params=pltpu.CompilerParams(collective_id=0, has_side_effects=True, vmem_limit_bytes=VMEM_LIMIT),
        name="collect",
    )(*(pltpu.with_memory_space_constraint(value, pltpu.HBM) for value in (
        ham_diag, ham_coup, pattern, coulomb)))

    reduced, base = pl.pallas_call(
        chain_kernel,
        out_shape=(square, square),
        in_specs=[smem, vmem, vmem],
        out_specs=(vmem, vmem),
        scratch_shapes=[VMEM((width, width), F32)] * 9,
        compiler_params=pltpu.CompilerParams(vmem_limit_bytes=VMEM_LIMIT),
        name="chain",
    )(energies, diags, coups)

    spread, taken = pl.pallas_call(
        functools.partial(regroup_kernel, count),
        out_shape=(square, jax.ShapeDtypeStruct((count, lines, 128), F32)),
        in_specs=[vmem] * 4,
        out_specs=(vmem, vmem),
        scratch_shapes=[
            VMEM((width + 16, width), BF16), VMEM((count, 8, width), F32),
            VMEM((count, 8, width), F32), VMEM((count, lines, 128), F32),
        ] + [DMA((2,))] * 3,
        compiler_params=pltpu.CompilerParams(collective_id=1, has_side_effects=True, vmem_limit_bytes=VMEM_LIMIT),
        name="regroup",
    )(base, rows, slots, bare_pos)

    return pl.pallas_call(
        finish_kernel,
        out_shape=(
            jax.ShapeDtypeStruct((1, 1, width, width), F32),
            jax.ShapeDtypeStruct((count, 1, span), F32),
        ),
        in_specs=[vmem] * 5,
        out_specs=(vmem, vmem),
        scratch_shapes=[VMEM((width, width), F32)],
        compiler_params=pltpu.CompilerParams(vmem_limit_bytes=VMEM_LIMIT),
        name="finish",
    )(reduced, base, spread, taken, bare_own)


def solution(mesh):
    count, spaces = mesh.shape["energy"], mesh.shape["space"]
    return jax.shard_map(
        functools.partial(on_device, count, spaces),
        mesh=mesh,
        in_specs=(
            P("space", None, None),
            P("space", None, None),
            P("energy"),
            P("space", None),
            P("space", "energy"),
        ),
        out_specs=(P("energy", "space", None, None), P(None, "space", "energy")),
        check_vma=False,
    )
```
